128 devices in a mesh: row: 16 (over x, z_lo, core), col: 8 (over y, z_hi).
Axes of the slice: x: 4, y: 4, z: 4 (z_hi: 2, z_lo: 2; z = z_hi * 2 + z_lo), core: 2. Of those that a mesh axis runs over, the one named last changes fastest.
Arguments:
- hidden: bfloat16 [8192, 2048], P('col', 'row'), may hold values from -6 to 6
- lengths: int32 [64], replicated, may hold values from 16 to 128, as said below
- square_matrix_shards: float32 [7, 2048, 2048], P(None, ('row', 'col')), may hold values from -0.125 to 0.125
- channel_mix_shards: float32 [2, 2048, 8192], P(None, ('row', 'col')), may hold values from -0.09375 to 0.09375
- lowrank_down: bfloat16 [2, 2048, 96], replicated, may hold values from -0.125 to 0.125
- lowrank_up: bfloat16 [2, 96, 2048], replicated, may hold values from -0.625 to 0.625
- token_shift_weights: float32 [9, 2048], replicated, may hold values from 0 to 1
- attention_coefficients: float32 [6, 2048], replicated, may hold values from -8 to 2, as said below
- norm_parameters: float32 [6, 2048], P(None, 'row'), may hold values from 0.25 to 1.75
Outputs:
- out_hidden: bfloat16 [8192, 2048], P('col', 'row')
- next_rkv: bfloat16 [3, 8192, 2048], P(None, 'row', 'col')
- final_state: float32 [64, 32, 4096], P('row', 'col')
The draws below stay inside these ranges and needn't reach their ends.
Inputs may be any that keep to these rules, and one draw needn't show every extreme that they name: `lengths`: every prompt length lies between 16 and 128; in every draw at least one prompt has length 128, most are under 41. `attention_coefficients`: row 0 lies in -8 to -1, row 1 in -2 to 2, row 2 in 0.5 to 1.5, row 3 in -1 to 1, row 4 in 0.5 to 1.5, row 5 in -0.5 to 0.5.
All inputs are finite; a program needn't handle non-finite values.
Results may differ from the reference program's by a relative error of at most 0.034.
Values may be sent and summed in bfloat16 or wider, within the bound.
A program may use at most 128 MiB of HBM per device.

```python
import jax
import jax.numpy as jnp
from jax import lax

MODEL_WIDTH = 2048
FF = 8192
ATTENTION_DIM = 64
LOWRANK_WIDTH = 96
LMAX = 128
PROMPTS = 64
TOKENS = 8192
N_ROW = 16


def draw_lengths(key, part):
    first_key, second_key, third_key = jax.random.split(jax.random.fold_in(key, 11), 3)
    short = jnp.minimum(jax.random.randint(first_key, (PROMPTS,), 16, 41), LMAX)
    longer = jax.random.randint(second_key, (PROMPTS,), 0, 4) == 0
    picked = jax.random.randint(third_key, (), 0, PROMPTS)
    forced = jnp.arange(PROMPTS) == picked
    return jnp.where(longer | forced, LMAX, short).astype(jnp.int32)


def draw_attention_coefficients(key, part):
    unit = jax.random.uniform(jax.random.fold_in(key, 23), (6, MODEL_WIDTH), jnp.float32)
    lower = jnp.array([-8.0, -2.0, 0.5, -1.0, 0.5, -0.5], jnp.float32)
    upper = jnp.array([-1.0, 2.0, 1.5, 1.0, 1.5, 0.5], jnp.float32)
    return lower[:, None] + (upper - lower)[:, None] * unit


def level_of(stream_key, dims, cuts, smallest, high):
    level = 1.0
    for dim, blocks in cuts:
        steps = jax.random.uniform(jax.random.fold_in(jax.random.fold_in(stream_key, 6), dim), (blocks,), jnp.float32, smallest / len(cuts), high / len(cuts))
        level = level * jnp.repeat(jnp.exp(steps), dims[dim] // blocks).reshape((-1,) + (1,) * (len(dims) - 1 - dim))
    return level


def scatter_about(rng, shape, deviation, bound, shards=(), kind=jnp.bfloat16):
    factor_of = level_of(rng, shape, shards, -0.22, 0.18) if shards else 1.0
    values = jax.random.normal(rng, shape, jnp.float32) * deviation * factor_of
    return jnp.minimum(jnp.maximum(values, -bound), bound).astype(kind)


def setup_inputs(seed: int = 0) -> dict:
    key_of = jax.random.split(jax.random.key(seed), 10)
    hidden = scatter_about(key_of[0], (TOKENS, MODEL_WIDTH), 1.0, 6.0, ((0, 8), (1, 16)))
    lengths = draw_lengths(jax.random.fold_in(key_of[9], 71), 0)
    square_matrix_shards = scatter_about(key_of[2], (7, MODEL_WIDTH, MODEL_WIDTH), MODEL_WIDTH ** -0.5, 0.125, ((1, 128),), jnp.float32)
    channel_mix_shards = scatter_about(key_of[3], (2, MODEL_WIDTH, FF), (2 * MODEL_WIDTH) ** -0.5, 0.09375, ((1, 128),), jnp.float32)
    lowrank_down = scatter_about(key_of[4], (2, MODEL_WIDTH, LOWRANK_WIDTH), MODEL_WIDTH ** -0.5, 0.125)
    lowrank_up = scatter_about(key_of[5], (2, LOWRANK_WIDTH, MODEL_WIDTH), LOWRANK_WIDTH ** -0.5, 0.625)
    token_shift_weights = jnp.clip(jax.random.uniform(key_of[6], (9, MODEL_WIDTH), jnp.float32, 0.0, 1.0), 0.0, 1.0)
    attention_coefficients = draw_attention_coefficients(jax.random.fold_in(key_of[9], 71), 0)
    norm_parameters = jnp.clip(1.0 + 0.15 * jax.random.normal(key_of[8], (6, MODEL_WIDTH), jnp.float32), 0.25, 1.75)
    return dict(hidden=hidden, lengths=lengths, square_matrix_shards=square_matrix_shards, channel_mix_shards=channel_mix_shards, lowrank_down=lowrank_down, lowrank_up=lowrank_up, token_shift_weights=token_shift_weights, attention_coefficients=attention_coefficients, norm_parameters=norm_parameters)


def shifted(source):
    grid = source.reshape(-1, LMAX, source.shape[-1])
    before = jnp.concatenate([jnp.zeros_like(grid[:, :1]), grid[:, :-1]], axis=1)
    return before.reshape(source.shape)

def mixed(source, weight):
    wide = source.astype(jnp.float32)
    return (wide + (shifted(wide) - wide) * weight).astype(jnp.bfloat16)

def normed(source, gain, bias):
    width = source.shape[-1]
    center = lax.optimization_barrier(jnp.sum(source, axis=-1, keepdims=True)) / width
    second = lax.optimization_barrier(jnp.sum(source * source, axis=-1, keepdims=True)) / width
    scaled = (source - center) * lax.rsqrt(second - center * center + 1e-05)
    return (scaled * gain + bias).astype(jnp.bfloat16)

def block_product_sum(source, weight):
    width = source.shape[1] // N_ROW
    total = jnp.zeros((source.shape[0], weight.shape[1]), jnp.float32)
    for block_index in range(N_ROW):
        lower = block_index * width
        partial_sum = jnp.dot(source[:, lower:lower + width], weight[lower:lower + width], preferred_element_type=jnp.float32)
        total = total + lax.optimization_barrier(partial_sum.astype(jnp.bfloat16)).astype(jnp.float32)
    return total

def run_scan(acceptance_gate_entries, key_vecs, value_vecs, decay_logarithm, remove_dir, write_dir):
    highest = lax.Precision.HIGHEST

    def advance(state, inputs):
        rec_now, key_now, val_now, decay_now, remove_now, write_now = inputs
        pulled = jnp.einsum('phvk,phk->phv', state, remove_now, precision=highest)
        state = state * jnp.exp(decay_now)[:, :, None, :] + pulled[..., None] * write_now[:, :, None, :] + val_now[..., None] * key_now[:, :, None, :]
        output = jnp.einsum('phvk,phk->phv', state, rec_now, precision=highest)
        return (state, output)
    inputs = tuple((jnp.moveaxis(item, 1, 0) for item in (acceptance_gate_entries, key_vecs, value_vecs, decay_logarithm, remove_dir, write_dir)))
    prompts, attention_entries = (acceptance_gate_entries.shape[0], acceptance_gate_entries.shape[2])
    start = jnp.zeros((prompts, attention_entries, ATTENTION_DIM, ATTENTION_DIM), jnp.float32)
    final, result_entries = lax.scan(advance, start, inputs)
    return (final, jnp.moveaxis(result_entries, 0, 1))

def reference(hidden, lengths, square_matrix_shards, channel_mix_shards, lowrank_down, lowrank_up, token_shift_weights, attention_coefficients, norm_parameters):
    square = square_matrix_shards.astype(jnp.bfloat16)
    mlp_weights = channel_mix_shards.astype(jnp.bfloat16)
    resid = hidden.astype(jnp.float32)
    first = normed(resid, norm_parameters[0], norm_parameters[1])
    shift_blends = [mixed(first, token_shift_weights[column_step]) for column_step in range(5)]
    acceptance_gate_entries = block_product_sum(shift_blends[0], square[0])
    key_vecs = block_product_sum(shift_blends[1], square[1])
    value_vecs = block_product_sum(shift_blends[2], square[2])
    decay_lowrank = block_product_sum(shift_blends[3], lowrank_down[0])
    rate_lowrank = block_product_sum(shift_blends[4], lowrank_down[1])
    decay_input = jnp.tanh(decay_lowrank).astype(jnp.bfloat16)
    decay_logarithm = -0.606531 * jax.nn.sigmoid(attention_coefficients[0] + jnp.dot(decay_input, lowrank_up[0], preferred_element_type=jnp.float32))
    incontext_rate = jax.nn.sigmoid(attention_coefficients[1] + jnp.dot(rate_lowrank.astype(jnp.bfloat16), lowrank_up[1], preferred_element_type=jnp.float32))
    prompts = lengths.shape[0]
    attention_entries = MODEL_WIDTH // ATTENTION_DIM

    def split_heads(source):
        return source.reshape(prompts, LMAX, attention_entries, ATTENTION_DIM)
    acceptance_gate_entries = split_heads(acceptance_gate_entries)
    key_vecs = split_heads(key_vecs)
    value_vecs = split_heads(value_vecs)
    decay_logarithm = split_heads(decay_logarithm)
    incontext_rate = split_heads(incontext_rate)
    kappa = key_vecs * attention_coefficients[2].reshape(attention_entries, ATTENTION_DIM)
    kappa_hat = kappa * lax.rsqrt(lax.optimization_barrier(jnp.sum(kappa * kappa, axis=-1, keepdims=True)) + 1e-05)
    present_entries = (jnp.arange(LMAX)[None, :] < lengths[:, None]).astype(jnp.float32)[:, :, None, None]
    remove_dir = -kappa_hat * present_entries
    write_dir = kappa_hat * incontext_rate * present_entries
    present_address_vector = key_vecs * present_entries
    present_payload_vector = value_vecs * present_entries
    final, result_entries = run_scan(acceptance_gate_entries, present_address_vector, present_payload_vector, decay_logarithm * present_entries, remove_dir, write_dir)
    extra_reward_factor = lax.optimization_barrier(jnp.sum(acceptance_gate_entries * present_address_vector * attention_coefficients[3].reshape(attention_entries, ATTENTION_DIM), axis=-1, keepdims=True)) * present_payload_vector
    attention_results = (result_entries + extra_reward_factor) * present_entries
    center = lax.optimization_barrier(jnp.mean(attention_results, axis=-1, keepdims=True))
    spread = lax.optimization_barrier(jnp.mean(jnp.square(attention_results - center), axis=-1, keepdims=True))
    grouped = ((attention_results - center) * lax.rsqrt(spread + 0.00064)).reshape(prompts * LMAX, MODEL_WIDTH)
    att = (grouped * attention_coefficients[4] + attention_coefficients[5]).astype(jnp.bfloat16)
    contract = (((1,), (1,)), ((), ()))
    attn_out = lax.dot_general(att, square[3], contract, preferred_element_type=jnp.float32)
    mid = (resid + attn_out).astype(jnp.bfloat16)
    mid_wide = mid.astype(jnp.float32)
    channel_in = mixed(normed(mid_wide, norm_parameters[2], norm_parameters[3]), token_shift_weights[5])
    pre_act = jnp.dot(channel_in, mlp_weights[0], preferred_element_type=jnp.float32)
    act = jnp.square(jax.nn.relu(pre_act)).astype(jnp.bfloat16)
    channel_out = lax.dot_general(act, mlp_weights[1], contract, preferred_element_type=jnp.float32)
    out_hidden = (mid_wide + channel_out).astype(jnp.bfloat16)
    third = normed(out_hidden.astype(jnp.float32), norm_parameters[4], norm_parameters[5])
    next_rkv = jnp.stack([block_product_sum(mixed(third, token_shift_weights[6 + column_step]), square[4 + column_step]).astype(jnp.bfloat16) for column_step in range(3)])
    final_state = final.reshape(prompts, attention_entries, ATTENTION_DIM * ATTENTION_DIM)
    return (out_hidden, next_rkv, final_state)
```

```python
import jax
import jax.numpy as jnp
from jax import lax
from jax.experimental import pallas as pl
from jax.experimental.pallas import tpu as pltpu
from jax.sharding import PartitionSpec as P

WIDTH = 2048
HEAD = 64
LMAX = 128
F32 = jnp.float32
BF16 = jnp.bfloat16
MESH = pl.DeviceIdType.MESH
ANY = pl.BlockSpec(memory_space=pl.ANY)
VMEM = pl.BlockSpec(memory_space=pltpu.VMEM)
N_ROW = 16
N_COL = 8
N_CHIP = 8
MINE = 512
FEAT = 128
SLICE = 256


def greet(devices):
    barrier = pltpu.get_barrier_semaphore()
    for device in devices:
        pl.semaphore_signal(barrier, inc=1, device_id=device, device_id_type=MESH)
    pl.semaphore_wait(barrier, len(devices))


def send(source, target, send_sem, recv_sem, device):
    copy = pltpu.make_async_remote_copy(
        src_ref=source,
        dst_ref=target,
        send_sem=send_sem,
        recv_sem=recv_sem,
        device_id=device,
        device_id_type=MESH,
    )
    copy.start()
    return copy


def keep(source, target, sem):
    copy = pltpu.make_async_copy(source, target, sem)
    copy.start()
    return copy


def exchange(kernel, outs, n_remote, n_local, collective_id, *operands):
    return pl.pallas_call(
        kernel,
        out_shape=[jax.ShapeDtypeStruct(*out) for out in outs],
        in_specs=[ANY] * len(operands),
        out_specs=[ANY] * len(outs),
        scratch_shapes=[
            pltpu.SemaphoreType.DMA((n_remote,)),
            pltpu.SemaphoreType.DMA((n_remote,)),
            pltpu.SemaphoreType.DMA((n_local,)),
        ],
        compiler_params=pltpu.CompilerParams(collective_id=collective_id, has_side_effects=True),
        cost_estimate=pl.CostEstimate(flops=0, bytes_accessed=48 * 2**20, transcendentals=0),
    )(*operands)


def start_kernel(
    hid, wa, wm, wn, par, hx, wt, wmr, wnr, parg, send_sem, recv_sem, local_sem
):
    r = lax.axis_index("row")
    c = lax.axis_index("col")
    h = lax.rem(r, 2)
    sibling = r + 1 - 2 * h
    rows = [lax.rem(r + d, N_ROW) for d in range(1, N_ROW)]
    cols = [lax.rem(c + d, N_COL) for d in range(1, N_COL)]
    greet([(p, c) for p in rows] + [(r, p) for p in cols])
    slot = iter(range(200))

    def go(source, target, device):
        at = next(slot)
        return send(source, target, send_sem.at[at], recv_sem.at[at], device)

    local = [
        keep(wa.at[r], wt.at[h, r, c], local_sem.at[0]),
        keep(hid.at[pl.ds(h * MINE, MINE)], hx.at[r], local_sem.at[1]),
        keep(wm.at[r], wmr.at[r], local_sem.at[2]),
        keep(wn.at[c], wnr.at[c], local_sem.at[3]),
        keep(par, parg.at[r], local_sem.at[4]),
    ]
    first = [go(wa.at[p], wt.at[lax.rem(p, 2), r, c], (p, c)) for p in rows]
    rest = [
        go(hid.at[pl.ds(lax.rem(p, 2) * MINE, MINE)], hx.at[r], (p, c)) for p in rows
    ]
    rest += [go(par, parg.at[r], (p, c)) for p in rows]
    for copy in first:
        copy.wait_recv()
    local[0].wait()
    spread = [go(wt.at[h, :, c], wt.at[h, :, c], (r, p)) for p in cols]
    rest += [go(wt.at[h, :, c], wt.at[h, :, c], (sibling, c))]
    rest += [go(wm.at[p], wmr.at[r], (p, c)) for p in rows]
    rest += [go(wn.at[p], wnr.at[c], (r, p)) for p in cols]
    for d in range(1, N_COL):
        spread[d - 1].wait_recv()
        origin = lax.rem(c - d + N_COL, N_COL)
        rest += [go(wt.at[h, :, origin], wt.at[h, :, origin], (sibling, c))]
    for copy in rest:
        copy.wait_recv()
    for copy in first + spread + rest:
        copy.wait_send()
    for copy in local[1:]:
        copy.wait()


def att_kernel(att, w3, attg, w3x, send_sem, recv_sem, local_sem):
    r = lax.axis_index("row")
    c = lax.axis_index("col")
    h = lax.rem(r, 2)
    q = lax.div(r, 2)
    sibling = r + 1 - 2 * h
    rows = [lax.rem(r + 2 * d, N_ROW) for d in range(1, N_CHIP)]
    greet([(p, c) for p in rows] + [(sibling, c)])
    local = [keep(att, attg.at[q], local_sem.at[0]), keep(w3, w3x.at[h], local_sem.at[1])]
    copies = [
        send(att, attg.at[q], send_sem.at[i], recv_sem.at[i], (p, c))
        for i, p in enumerate(rows)
    ]
    copies += [send(w3, w3x.at[h], send_sem.at[7], recv_sem.at[7], (sibling, c))]
    for copy in local + copies:
        copy.wait()


def mid_kernel(mid, wmg, midg, mlpw, send_sem, recv_sem, local_sem):
    r = lax.axis_index("row")
    c = lax.axis_index("col")
    h = lax.rem(r, 2)
    q = lax.div(r, 2)
    sibling = r + 1 - 2 * h
    rows = [lax.rem(r + 2 * d, N_ROW) for d in range(1, N_CHIP)]
    greet([(p, c) for p in rows] + [(sibling, c)])
    copies = [
        send(mid, midg.at[q], send_sem.at[i], recv_sem.at[i], (p, c))
        for i, p in enumerate(rows)
    ]
    local = [keep(mid, midg.at[q], local_sem.at[8])]
    for k in range(N_COL):
        copies += [
            send(
                wmg.at[k], mlpw.at[h, :, k], send_sem.at[7 + k], recv_sem.at[7 + k], (sibling, c)
            )
        ]
        local += [keep(wmg.at[k], mlpw.at[h, :, k], local_sem.at[k])]
    for copy in local + copies:
        copy.wait()


def sum_kernel(part, got, send_sem, recv_sem, local_sem):
    r = lax.axis_index("row")
    c = lax.axis_index("col")
    rows = [lax.rem(r + d, N_ROW) for d in range(1, N_ROW)]
    greet([(p, c) for p in rows])
    local = keep(part.at[r], got.at[r], local_sem.at[0])
    copies = [
        send(part.at[p], got.at[r], send_sem.at[i], recv_sem.at[i], (p, c))
        for i, p in enumerate(rows)
    ]
    local.wait()
    for copy in copies:
        copy.wait()


def next_kernel(out, got, send_sem, recv_sem, local_sem):
    r = lax.axis_index("row")
    c = lax.axis_index("col")
    h = lax.rem(r, 2)
    q = lax.div(r, 2)
    barrier = pltpu.get_barrier_semaphore()

    @pl.when(q != c)
    def _():
        pl.semaphore_signal(barrier, inc=1, device_id=(r, q), device_id_type=MESH)

    for d in range(1, N_ROW):
        pl.semaphore_signal(
            barrier, inc=1, device_id=(lax.rem(r + d, N_ROW), q), device_id_type=MESH
        )
    pl.semaphore_wait(barrier, N_ROW - (q == c).astype(jnp.int32))

    def move(i, e):
        half = lax.rem(h + i, 2)
        return pltpu.make_async_remote_copy(
            src_ref=out.at[pl.ds(half * MINE, MINE)],
            dst_ref=got.at[r],
            send_sem=send_sem.at[i * N_COL + e],
            recv_sem=recv_sem.at[r],
            device_id=(2 * c + half, lax.rem(c + e, N_COL)),
            device_id_type=MESH,
        )

    @pl.when(q == c)
    def _():
        keep(out.at[pl.ds(h * MINE, MINE)], got.at[r], recv_sem.at[r])

    @pl.when(q != c)
    def _():
        move(0, 0).start()

    for e in range(N_COL):
        for i in range(2):
            if i + e > 0:
                move(i, e).start()
    for s in range(N_ROW):
        pltpu.make_async_copy(got.at[s], got.at[s], recv_sem.at[s]).wait()

    @pl.when(q != c)
    def _():
        move(0, 0).wait_send()

    for e in range(N_COL):
        for i in range(2):
            if i + e > 0:
                move(i, e).wait_send()


def compute(kernel, outs, operands, scratch=(), grid=None, in_specs=None, out_specs=None, flops=0):
    return pl.pallas_call(
        kernel,
        grid=grid if grid is not None else (),
        out_shape=[jax.ShapeDtypeStruct(*out) for out in outs],
        in_specs=in_specs if in_specs is not None else [VMEM] * len(operands),
        out_specs=out_specs if out_specs is not None else [VMEM] * len(outs),
        scratch_shapes=list(scratch),
        compiler_params=pltpu.CompilerParams(vmem_limit_bytes=56 * 2**20),
        cost_estimate=pl.CostEstimate(flops=flops, bytes_accessed=16 * 2**20, transcendentals=0),
    )(*operands)


def dot(a, b, dims=((1,), (0,))):
    return lax.dot_general(a, b, (dims, ((), ())), preferred_element_type=F32)


def split(x):
    high = x.astype(BF16)
    return high, (x - high.astype(F32)).astype(BF16)


def dot3(a, b, dims=((1,), (0,))):
    a_high, a_low = a
    b_high, b_low = b
    return dot(a_high, b_high, dims) + (dot(a_high, b_low, dims) + dot(a_low, b_high, dims))


def norm(source, gain, bias):
    center = jnp.sum(source, axis=-1, keepdims=True) / WIDTH
    second = jnp.sum(source * source, axis=-1, keepdims=True) / WIDTH
    scaled = (source - center) * lax.rsqrt(second - center * center + 1e-05)
    return (scaled * gain + bias).astype(BF16).astype(F32)


def step_back(z):
    position = lax.rem(lax.broadcasted_iota(jnp.int32, z.shape, 0), LMAX)
    return jnp.where(position == 0, 0.0, pltpu.roll(z, 1, 0)) - z


TILE = 256


def blocks_of(ref, at):
    return jnp.concatenate(
        [ref[j, pl.ds(at, TILE), :].astype(F32) for j in range(ref.shape[0])], axis=1
    )


def mix_kernel(hx, par, shift, wt, down, rkv, low):
    @pl.loop(0, MINE // TILE)
    def _(m):
        at = pl.multiple_of(m * TILE, TILE)
        z = norm(blocks_of(hx, at), par[0:1, :], par[1:2, :])
        dz = step_back(z)
        for j in range(5):
            blend = (z + dz * shift[j : j + 1, :]).astype(BF16)
            if j < 3:
                weight = jnp.concatenate(
                    [wt[side, :, j * FEAT : (j + 1) * FEAT] for side in range(2)], axis=1
                )
                rkv[j, pl.ds(at, TILE), :] = dot(blend, weight)
            else:
                low[j - 3, pl.ds(at, TILE), :] = dot(blend, down[j - 3])


def core_kernel(lens, rkv, low, coef, up, att, final):
    length = lens[pl.program_id(0)]
    wide = SLICE
    heads = wide // HEAD
    live = (lax.broadcasted_iota(jnp.int32, (LMAX, wide), 0) < length).astype(F32)
    lane = lax.broadcasted_iota(jnp.int32, (LMAX, wide), 1) // HEAD
    t = lax.broadcasted_iota(jnp.int32, (LMAX, LMAX), 0)
    u = lax.broadcasted_iota(jnp.int32, (LMAX, LMAX), 1)
    seg = (
        lax.broadcasted_iota(jnp.int32, (wide, wide), 0) // HEAD
        == lax.broadcasted_iota(jnp.int32, (wide, wide), 1) // HEAD
    ).astype(F32).astype(BF16)
    lower = (t >= u).astype(F32).astype(BF16)

    def head_sum(x):
        high, low_part = split(x)
        return dot(high, seg) + dot(low_part, seg)

    def only(x, k):
        return jnp.where(lane == k, x, jnp.zeros_like(x))

    receptance, key, value = rkv[0], rkv[1], rkv[2]
    decay = (
        -0.606531
        * jax.nn.sigmoid(coef[0:1, :] + dot(jnp.tanh(low[0]).astype(BF16), up[0]))
        * live
    )
    rate = jax.nn.sigmoid(coef[1:2, :] + dot(low[1].astype(BF16), up[1]))
    kappa = key * coef[2:3, :]
    kappa = kappa * lax.rsqrt(head_sum(kappa * kappa) + 1e-05)
    remove = -kappa * live
    write = kappa * rate * live
    key = key * live
    value = value * live
    d_high, d_rest = split(decay)
    d_mid, d_low = split(decay - d_high.astype(F32))
    total = dot(lower, d_high) + (dot(lower, d_mid) + dot(lower, d_low))
    middle = total[LMAX // 2 - 1 : LMAX // 2, :]
    last = total[LMAX - 1 : LMAX, :]
    back = jnp.exp(middle - total)
    pull = split(remove * jnp.exp(total - decay - middle))
    read = split(receptance * jnp.exp(total - middle))
    write_back = split(write * back)
    key_back = split(key * back)
    value_parts = split(value)

    left = tuple(
        jnp.concatenate([x for k in range(heads) for x in (only(pull[i], k), only(read[i], k))])
        for i in range(2)
    )
    right = tuple(jnp.concatenate([write_back[i], key_back[i]]) for i in range(2))
    pairs = dot3(left, right, ((1,), (1,)))
    strict = t > u
    t2 = lax.broadcasted_iota(jnp.int32, (LMAX, 2 * LMAX), 0)
    u2 = lax.rem(lax.broadcasted_iota(jnp.int32, (LMAX, 2 * LMAX), 1), LMAX)
    upto = t2 >= u2
    solves, pull_key, reads = [], [], []
    for k in range(heads):
        base = k * 2 * LMAX
        system = jnp.where(strict, pairs[base : base + LMAX, :LMAX], 0.0)
        pull_key.append(split(jnp.where(strict, pairs[base : base + LMAX, LMAX:], 0.0)))
        reads.append(split(jnp.where(upto, pairs[base + LMAX : base + 2 * LMAX], 0.0)))
        solves.append(system)
    inverse = []
    for k in range(heads):
        near = (t // 2 == u // 2)
        inverse.append(
            jnp.where(near, solves[k], 0.0) + (t == u).astype(F32)
        )
    size = 2
    while size < LMAX:
        inside = (t // (2 * size) == u // (2 * size)) & (t // size != u // size)
        grown = []
        for k in range(heads):
            known = split(inverse[k])
            cross = split(jnp.where(inside, solves[k], 0.0))
            product = split(dot3(known, cross))
            grown.append(inverse[k] + dot3(product, known))
        inverse = grown
        size *= 2

    def across(mats, parts):
        wide_left = tuple(jnp.concatenate([mat[i] for mat in mats], axis=1) for i in range(2))
        tall = tuple(
            jnp.concatenate([only(part[i], k) for k in range(heads) for part in parts])
            for i in range(2)
        )
        return dot3(wide_left, tall)

    start = across(pull_key, [value_parts])
    pulled = split(across([split(x) for x in inverse], [split(start)]))
    output = across(reads, [pulled, value_parts])
    tail = jnp.exp(last - total)
    write_tail = split(write * tail)
    key_tail = split(key * tail)
    tall = tuple(jnp.concatenate([pulled[i], value_parts[i]]) for i in range(2))
    tails = tuple(jnp.concatenate([write_tail[i], key_tail[i]]) for i in range(2))
    state = dot3(tall, tails, ((0,), (0,)))
    for k in range(heads):
        final[0, k] = state[k * HEAD : (k + 1) * HEAD, k * HEAD : (k + 1) * HEAD]
    bonus = head_sum(receptance * key * coef[3:4, :])
    out = (output + bonus * value) * live
    center = head_sum(out) * (1.0 / HEAD)
    out = out - center
    spread = head_sum(out * out) * (1.0 / HEAD)
    att[...] = (out * lax.rsqrt(spread + 0.00064) * coef[4:5, :] + coef[5:6, :]).astype(BF16)


def project_kernel(attg, own, w3, mid):
    q = lax.div(lax.axis_index("row"), 2)

    @pl.loop(0, MINE // TILE)
    def _(m):
        at = pl.multiple_of(m * TILE, TILE)
        wide = jnp.concatenate([attg[j, pl.ds(at, TILE), :] for j in range(N_CHIP)], axis=1)
        hidden = jnp.concatenate(
            [own[2 * q + side, pl.ds(at, TILE), :] for side in range(2)], axis=1
        )
        mid[pl.ds(at, TILE), :] = (
            hidden.astype(F32) + dot(wide, w3[...], ((1,), (1,)))
        ).astype(BF16)


def mlp_kernel(midg, par, shift, mlpw, own, part, act_scr):
    q = lax.div(lax.axis_index("row"), 2)

    @pl.loop(0, MINE // TILE)
    def _(m):
        at = pl.multiple_of(m * TILE, TILE)
        z = norm(blocks_of(midg, at), par[2:3, :], par[3:4, :])
        blend = (z + step_back(z) * shift[5:6, :]).astype(BF16)
        for side in range(2):
            act = jnp.square(jnp.maximum(dot(blend, mlpw[side, :, :MINE]), 0.0))
            act_scr[side] = act.astype(BF16)

        @pl.loop(0, N_CHIP)
        def _(n):
            rows = pl.ds(pl.multiple_of(n * SLICE, SLICE), SLICE)
            total = dot(act_scr[0], mlpw[0, rows, MINE:], ((1,), (1,)))
            total += dot(act_scr[1], mlpw[1, rows, MINE:], ((1,), (1,)))
            total += jnp.where(n == q, own[pl.ds(at, TILE), :].astype(F32), 0.0)
            for side in range(2):
                part[2 * n + side, pl.ds(at, TILE), :] = total[
                    :, side * FEAT : (side + 1) * FEAT
                ].astype(BF16)


def last_kernel(nx, par, shift, weight, out):
    @pl.loop(0, MINE // TILE)
    def _(m):
        at = pl.multiple_of(m * TILE, TILE)
        z = norm(blocks_of(nx, at), par[4:5, :], par[5:6, :])
        dz = step_back(z)
        for j in range(3):
            blend = (z + dz * shift[6 + j : 7 + j, :]).astype(BF16)
            out[j, pl.ds(at, TILE), :] = dot(
                blend, weight[:, j * SLICE : (j + 1) * SLICE]
            ).astype(BF16)


def time_core(lens, rkv, low, coef, up):
    prompts = rkv.shape[1] // LMAX
    return compute(
        core_kernel,
        [((prompts * LMAX, SLICE), BF16), ((prompts, SLICE // HEAD, HEAD, HEAD), F32)],
        (lens, rkv, low, coef, up),
        grid=(prompts,),
        in_specs=[
            pl.BlockSpec(memory_space=pltpu.SMEM),
            pl.BlockSpec((3, LMAX, SLICE), lambda p: (0, p, 0)),
            pl.BlockSpec((2, LMAX, low.shape[2]), lambda p: (0, p, 0)),
            pl.BlockSpec(coef.shape, lambda p: (0, 0)),
            pl.BlockSpec(up.shape, lambda p: (0, 0, 0)),
        ],
        out_specs=[
            pl.BlockSpec((LMAX, SLICE), lambda p: (p, 0)),
            pl.BlockSpec((1, SLICE // HEAD, HEAD, HEAD), lambda p: (p, 0, 0, 0)),
        ],
        flops=4 * 10**9,
    )


def per_device(
    hidden,
    lengths,
    square_matrix_shards,
    channel_mix_shards,
    lowrank_down,
    lowrank_up,
    token_shift_weights,
    attention_coefficients,
    norm_parameters,
):
    r = lax.axis_index("row")
    c = lax.axis_index("col")
    h = lax.rem(r, 2)
    q = lax.div(r, 2)
    square = square_matrix_shards.astype(BF16)
    mlp = channel_mix_shards.astype(BF16)
    wa = square[0:3].reshape(3, 16, N_ROW, FEAT).transpose(2, 1, 0, 3).reshape(N_ROW, 16, 3 * FEAT)
    wm = mlp.reshape(2, 16, N_ROW, MINE).transpose(2, 1, 0, 3).reshape(N_ROW, 16, 2 * MINE)
    wn = square[4:7].reshape(3, 16, N_COL, SLICE).transpose(2, 1, 0, 3)
    wn = wn.reshape(N_COL, 16, 3 * SLICE)
    par = jnp.concatenate([norm_parameters, jnp.zeros((2, FEAT), F32)])
    w3 = lax.all_gather(square[3], "col", axis=0, tiled=True)
    hx, wt, wmr, wnr, parg = exchange(
        start_kernel,
        [
            ((N_ROW, MINE, FEAT), BF16),
            ((2, N_ROW, N_COL, 16, 3 * FEAT), BF16),
            ((N_ROW, 16, 2 * MINE), BF16),
            ((N_COL, 16, 3 * SLICE), BF16),
            ((N_ROW, 8, FEAT), F32),
        ],
        82,
        5,
        1,
        hidden,
        wa,
        wm,
        wn,
        par,
    )
    wmg = lax.all_gather(wmr, "col", axis=0)
    weight_next = lax.all_gather(wnr.reshape(FEAT, 3 * SLICE), "row", axis=0, tiled=True)
    params = parg.transpose(1, 0, 2).reshape(8, WIDTH)
    rkv, low = compute(
        mix_kernel,
        [((3, MINE, SLICE), F32), ((2, MINE, lowrank_down.shape[2]), F32)],
        (hx, params, token_shift_weights, wt.reshape(2, WIDTH, 3 * FEAT), lowrank_down),
        flops=4 * 10**9,
    )
    coef = lax.dynamic_slice_in_dim(attention_coefficients, q * SLICE, SLICE, 1)
    up = lax.dynamic_slice_in_dim(lowrank_up, q * SLICE, SLICE, 2)
    lens = lax.dynamic_slice_in_dim(lengths, c * 8 + h * 4, 4, 0)
    att, final = time_core(lens, rkv, low, coef, up)
    attg, w3x = exchange(
        att_kernel,
        [((N_CHIP, MINE, SLICE), BF16), ((2, FEAT, WIDTH), BF16)],
        8,
        2,
        2,
        att,
        w3,
    )
    moves = [
        ((2 * a + b) * N_COL + d, (2 * d + b) * N_COL + a)
        for a in range(N_CHIP)
        for b in range(2)
        for d in range(N_COL)
    ]
    final = lax.ppermute(final, ("row", "col"), moves)
    final_state = final.reshape(4, 4, HEAD * HEAD)
    (mid,) = compute(
        project_kernel,
        [((MINE, SLICE), BF16)],
        (attg, hx, w3x.reshape(SLICE, WIDTH)),
        flops=10**9,
    )
    midg, mlpw = exchange(
        mid_kernel,
        [((N_CHIP, MINE, SLICE), BF16), ((2, N_ROW, N_COL, 16, 2 * MINE), BF16)],
        15,
        9,
        3,
        mid,
        wmg,
    )
    (part,) = compute(
        mlp_kernel,
        [((N_ROW, MINE, FEAT), BF16)],
        (midg, params, token_shift_weights, mlpw.reshape(2, WIDTH, 2 * MINE), mid),
        scratch=[pltpu.VMEM((2, TILE, MINE), BF16)],
        flops=5 * 10**9,
    )
    (got,) = exchange(sum_kernel, [((N_ROW, MINE, FEAT), BF16)], 15, 1, 4, part)
    out_hidden = (
        jnp.sum(got.reshape(N_CHIP, 2 * MINE, FEAT).astype(F32), axis=0).astype(BF16)
    )
    (nx,) = exchange(next_kernel, [((N_ROW, MINE, FEAT), BF16)], 16, 1, 5, out_hidden)
    (next_rkv,) = compute(
        last_kernel,
        [((3, MINE, SLICE), BF16)],
        (nx, params, token_shift_weights, weight_next),
        flops=2 * 10**9,
    )
    return (out_hidden, next_rkv, final_state)


def solution(mesh):
    return jax.shard_map(
        per_device,
        mesh=mesh,
        in_specs=(
            P("col", "row"),
            P(),
            P(None, ("row", "col"), None),
            P(None, ("row", "col"), None),
            P(),
            P(),
            P(),
            P(),
            P(None, "row"),
        ),
        out_specs=(P("col", "row"), P(None, "row", "col"), P("row", "col", None)),
        check_vma=False,
    )
```

```python
import jax
import jax.numpy as jnp
from jax import lax
from jax.experimental import pallas as pl
from jax.experimental.pallas import tpu as pltpu
from jax.sharding import PartitionSpec as P

WIDTH = 2048
HEAD = 64
LMAX = 128
F32 = jnp.float32
BF16 = jnp.bfloat16
MESH = pl.DeviceIdType.MESH
ANY = pl.BlockSpec(memory_space=pl.ANY)
VMEM = pl.BlockSpec(memory_space=pltpu.VMEM)
N_ROW = 16
N_COL = 8
N_CHIP = 8
MINE = 512
FEAT = 128
SLICE = 256


def greet(devices):
    barrier = pltpu.get_barrier_semaphore()
    for device in devices:
        pl.semaphore_signal(barrier, inc=1, device_id=device, device_id_type=MESH)
    pl.semaphore_wait(barrier, len(devices))


def send(source, target, send_sem, recv_sem, device):
    copy = pltpu.make_async_remote_copy(
        src_ref=source,
        dst_ref=target,
        send_sem=send_sem,
        recv_sem=recv_sem,
        device_id=device,
        device_id_type=MESH,
    )
    copy.start()
    return copy


def keep(source, target, sem):
    copy = pltpu.make_async_copy(source, target, sem)
    copy.start()
    return copy


def exchange(kernel, outs, n_remote, n_local, collective_id, *operands):
    return pl.pallas_call(
        kernel,
        out_shape=[jax.ShapeDtypeStruct(*out) for out in outs],
        in_specs=[ANY] * len(operands),
        out_specs=[ANY] * len(outs),
        scratch_shapes=[
            pltpu.SemaphoreType.DMA((n_remote,)),
            pltpu.SemaphoreType.DMA((n_remote,)),
            pltpu.SemaphoreType.DMA((n_local,)),
        ],
        compiler_params=pltpu.CompilerParams(collective_id=collective_id, has_side_effects=True),
        cost_estimate=pl.CostEstimate(flops=0, bytes_accessed=48 * 2**20, transcendentals=0),
    )(*operands)


def place():
    r = lax.axis_index("row")
    c = lax.axis_index("col")
    h = lax.rem(r, 2)
    return r, c, h, lax.div(r, 2), r + 1 - 2 * h


class Links:
    def __init__(self, send_sem, recv_sem, first=0):
        self.send_sem = send_sem
        self.recv_sem = recv_sem
        self.slot = first
        self.copies = []

    def go(self, source, target, device):
        copy = send(
            source, target, self.send_sem.at[self.slot], self.recv_sem.at[self.slot], device
        )
        self.slot += 1
        self.copies.append(copy)
        return copy

    def finish(self, received=()):
        done = {id(copy) for copy in received}
        for copy in self.copies:
            if id(copy) not in done:
                copy.wait_recv()
        for copy in self.copies:
            copy.wait_send()


def ring_peers(r, c):
    h = lax.rem(r, 2)
    z_peer = h + 2 * (lax.div(r, 2) + 1 - 2 * lax.rem(lax.div(r, 2), 2))
    return (z_peer, c), (lax.rem(r + 4, N_ROW), c), (lax.rem(r + 12, N_ROW), c)


def ring_gather(links, own, got, ready):
    r, c, h, q, _ = place()
    z_peer, plus, minus = ring_peers(r, c)
    z_chip = q + 1 - 2 * lax.rem(q, 2)
    before = lax.rem(q + 6, N_CHIP)
    after = lax.rem(q + 2, N_CHIP)
    across = lax.rem(q + 4, N_CHIP)
    first = {}
    for side in own:
        ready(side)
        for name, device in (("p", plus), ("m", minus), ("z", z_peer)):
            which = own[side][1]
            first[name, side] = links.go(own[side][0], got.at[2 * q + which], device)
    sides = list(own)
    done = []

    def arrived(copy):
        copy.wait_recv()
        done.append(copy)

    def forward(chip, side, device):
        return links.go(got.at[2 * chip + side], got.at[2 * chip + side], device)

    for side in sides:
        arrived(first["p", side])
    low = forward(before, 0, plus)
    for side in sides:
        arrived(first["m", side])
    high = forward(after, 1, minus)
    for side in sides:
        arrived(first["z", side])
        which = own[side][1]
        forward(z_chip, which, plus)
        forward(z_chip, which, minus)
    arrived(low)
    forward(across, 0, z_peer)
    arrived(high)
    forward(across, 1, z_peer)
    return done


RING = 14


def swap_kernel(square, mlp, par, wa, wm, wn, parg, send_sem, recv_sem, local_sem):
    r, c, h, q, sibling = place()
    rows = [lax.rem(r + d, N_ROW) for d in range(1, N_ROW)]
    cols = [lax.rem(c + d, N_COL) for d in range(1, N_COL)]

    def time_part(p):
        return square.at[pl.ds(0, 3), :, pl.ds(pl.multiple_of(p * FEAT, FEAT), FEAT)]

    def mlp_part(p):
        return mlp.at[:, :, pl.ds(pl.multiple_of(p * MINE, MINE), MINE)]

    def next_part(p):
        return square.at[pl.ds(4, 3), :, pl.ds(pl.multiple_of(p * SLICE, SLICE), SLICE)]

    local = [
        keep(time_part(r), wa.at[:, r], local_sem.at[0]),
        keep(mlp_part(r), wm.at[r], local_sem.at[1]),
        keep(next_part(c), wn.at[c], local_sem.at[2]),
        keep(par, parg.at[r], local_sem.at[3]),
    ]
    greet([(p, c) for p in rows] + [(r, p) for p in cols])
    links = Links(send_sem, recv_sem)
    for p in rows:
        links.go(mlp_part(p), wm.at[r], (p, c))
    for p in rows:
        links.go(time_part(p), wa.at[:, r], (p, c))
    for p in cols:
        links.go(next_part(p), wn.at[c], (r, p))
    for p in rows:
        links.go(par, parg.at[r], (p, c))
    links.finish()
    for copy in local:
        copy.wait()


def start_kernel(hid, wa, hx, wt, send_sem, recv_sem, local_sem):
    r, c, h, q, sibling = place()
    cols = [lax.rem(c + d, N_COL) for d in range(1, N_COL)]
    mine = hid.at[pl.ds(pl.multiple_of(h * MINE, MINE), MINE)]
    local = [
        keep(mine, hx.at[r], local_sem.at[0]),
        keep(wa, wt.at[h, :, :, c], local_sem.at[1]),
    ]
    greet([(sibling, c), *ring_peers(r, c)] + [(r, p) for p in cols])
    links = Links(send_sem, recv_sem)
    theirs = links.go(
        hid.at[pl.ds(pl.multiple_of((1 - h) * MINE, MINE), MINE)], hx.at[r], (sibling, c)
    )
    spread = [links.go(wa, wt.at[h, :, :, c], (r, p)) for p in cols]
    links.go(wa, wt.at[h, :, :, c], (sibling, c))
    done = [theirs]

    def ready(side):
        if side == 1:
            theirs.wait_recv()

    done += ring_gather(links, {0: (mine, h), 1: (hx.at[sibling], 1 - h)}, hx, ready)
    for d in range(1, N_COL):
        spread[d - 1].wait_recv()
        done.append(spread[d - 1])
        origin = lax.rem(c - d + N_COL, N_COL)
        links.go(wt.at[h, :, :, origin], wt.at[h, :, :, origin], (sibling, c))
    links.finish(done)
    for copy in local:
        copy.wait()


def att_kernel(att, w3, attg, w3x, send_sem, recv_sem, local_sem):
    r, c, h, q, sibling = place()
    cols = [lax.rem(c + d, N_COL) for d in range(1, N_COL)]
    local = [
        keep(att.at[0], attg.at[2 * q], local_sem.at[0]),
        keep(att.at[1], attg.at[2 * q + 1], local_sem.at[1]),
        keep(w3, w3x.at[h, c], local_sem.at[2]),
    ]
    greet([(sibling, c), *ring_peers(r, c)] + [(r, p) for p in cols])
    links = Links(send_sem, recv_sem)
    spread = [links.go(w3, w3x.at[h, c], (r, p)) for p in cols]
    links.go(w3, w3x.at[h, c], (sibling, c))
    done = ring_gather(
        links, {0: (att.at[0], 0), 1: (att.at[1], 1)}, attg, lambda side: None
    )
    for d in range(1, N_COL):
        spread[d - 1].wait_recv()
        done.append(spread[d - 1])
        origin = lax.rem(c - d + N_COL, N_COL)
        links.go(w3x.at[h, origin], w3x.at[h, origin], (sibling, c))
    links.finish(done)
    for copy in local:
        copy.wait()


def mid_kernel(mid, wmg, midg, theirs, send_sem, recv_sem, local_sem):
    r, c, h, q, sibling = place()
    local = [
        keep(mid.at[0], midg.at[2 * q], local_sem.at[0]),
        keep(mid.at[1], midg.at[2 * q + 1], local_sem.at[1]),
    ]
    greet([(sibling, c), *ring_peers(r, c)])
    links = Links(send_sem, recv_sem)
    for k in range(N_COL):
        for m in range(2):
            links.go(wmg.at[k, :, m], theirs.at[m, :, k], (sibling, c))
    done = ring_gather(
        links, {0: (mid.at[0], 0), 1: (mid.at[1], 1)}, midg, lambda side: None
    )
    links.finish(done)
    for copy in local:
        copy.wait()


def sum_kernel(part, got, send_sem, recv_sem, local_sem):
    r, c, h, q, sibling = place()
    rows = [lax.rem(r + d, N_ROW) for d in range(1, N_ROW)]
    local = keep(part.at[r], got.at[r], local_sem.at[0])
    greet([(p, c) for p in rows])
    links = Links(send_sem, recv_sem)
    for p in rows:
        links.go(part.at[p], got.at[r], (p, c))
    links.finish()
    local.wait()


def next_kernel(out, got, send_sem, recv_sem, local_sem):
    r, c, h, q, sibling = place()
    cols = [lax.rem(c + d, N_COL) for d in range(1, N_COL)]
    barrier = pltpu.get_barrier_semaphore()

    def target(i):
        return (2 * c + lax.rem(h + i, 2), q)

    @pl.when(q != c)
    def _():
        pl.semaphore_signal(barrier, inc=1, device_id=target(0), device_id_type=MESH)

    for device in [target(1)] + [(r, p) for p in cols]:
        pl.semaphore_signal(barrier, inc=1, device_id=device, device_id_type=MESH)
    pl.semaphore_wait(barrier, N_COL + 1 - (q == c).astype(jnp.int32))

    def piece(i):
        half = lax.rem(h + i, 2)
        return out.at[pl.ds(pl.multiple_of(half * MINE, MINE), MINE)]

    def move(i):
        return pltpu.make_async_remote_copy(
            src_ref=piece(i),
            dst_ref=got.at[2 * q + h],
            send_sem=send_sem.at[i],
            recv_sem=recv_sem.at[h],
            device_id=target(i),
            device_id_type=MESH,
        )

    @pl.when(q == c)
    def _():
        keep(piece(0), got.at[r], recv_sem.at[h])

    @pl.when(q != c)
    def _():
        move(0).start()

    move(1).start()
    links = Links(send_sem, recv_sem, 2)
    for side in range(2):
        block = got.at[2 * c + side]
        pltpu.make_async_copy(block, block, recv_sem.at[side]).wait()
        for p in cols:
            links.go(block, block, (r, p))
    links.finish()

    @pl.when(q != c)
    def _():
        move(0).wait_send()

    move(1).wait_send()


def compute(kernel, outs, operands, scratch=(), grid=None, in_specs=None, out_specs=None, flops=0):
    return pl.pallas_call(
        kernel,
        grid=grid if grid is not None else (),
        out_shape=[jax.ShapeDtypeStruct(*out) for out in outs],
        in_specs=in_specs if in_specs is not None else [VMEM] * len(operands),
        out_specs=out_specs if out_specs is not None else [VMEM] * len(outs),
        scratch_shapes=list(scratch),
        compiler_params=pltpu.CompilerParams(vmem_limit_bytes=56 * 2**20),
        cost_estimate=pl.CostEstimate(flops=flops, bytes_accessed=16 * 2**20, transcendentals=0),
    )(*operands)


def dot(a, b, dims=((1,), (0,))):
    return lax.dot_general(a, b, (dims, ((), ())), preferred_element_type=F32)


def split(x):
    high = x.astype(BF16)
    return high, (x - high.astype(F32)).astype(BF16)


def dot3(a, b, dims=((1,), (0,))):
    a_high, a_low = a
    b_high, b_low = b
    return dot(a_high, b_high, dims) + (dot(a_high, b_low, dims) + dot(a_low, b_high, dims))


def norm(source, gain, bias):
    center = jnp.sum(source, axis=-1, keepdims=True) / WIDTH
    second = jnp.sum(source * source, axis=-1, keepdims=True) / WIDTH
    scaled = (source - center) * lax.rsqrt(second - center * center + 1e-05)
    return (scaled * gain + bias).astype(BF16).astype(F32)


def row_of(par, i):
    return jnp.concatenate([par[j, i : i + 1, :] for j in range(N_ROW)], axis=1)


def step_back(z):
    position = lax.rem(lax.broadcasted_iota(jnp.int32, z.shape, 0), LMAX)
    return jnp.where(position == 0, 0.0, pltpu.roll(z, 1, 0)) - z


TILE = 256


def blocks_of(ref, at):
    return jnp.concatenate(
        [ref[j, pl.ds(at, TILE), :].astype(F32) for j in range(ref.shape[0])], axis=1
    )


def mix_kernel(hx, par, shift, wt, down, rkv, low):
    @pl.loop(0, MINE // TILE)
    def _(m):
        at = pl.multiple_of(m * TILE, TILE)
        z = norm(blocks_of(hx, at), row_of(par, 0), row_of(par, 1))
        dz = step_back(z)
        for j in range(5):
            blend = (z + dz * shift[j : j + 1, :]).astype(BF16)
            if j < 3:
                weight = jnp.concatenate(
                    [wt[side, j].reshape(WIDTH, FEAT) for side in range(2)], axis=1
                )
                rkv[j, pl.ds(at, TILE), :] = dot(blend, weight)
            else:
                low[j - 3, pl.ds(at, TILE), :] = dot(blend, down[j - 3])


def core_kernel(lens, rkv, low, coef, up, att, final):
    length = lens[pl.program_id(0)]
    wide = SLICE
    heads = wide // HEAD
    live = (lax.broadcasted_iota(jnp.int32, (LMAX, wide), 0) < length).astype(F32)
    lane = lax.broadcasted_iota(jnp.int32, (LMAX, wide), 1) // HEAD
    t = lax.broadcasted_iota(jnp.int32, (LMAX, LMAX), 0)
    u = lax.broadcasted_iota(jnp.int32, (LMAX, LMAX), 1)
    seg = (
        lax.broadcasted_iota(jnp.int32, (wide, wide), 0) // HEAD
        == lax.broadcasted_iota(jnp.int32, (wide, wide), 1) // HEAD
    ).astype(F32).astype(BF16)
    lower = (t >= u).astype(F32).astype(BF16)

    def head_sum(x):
        high, low_part = split(x)
        return dot(high, seg) + dot(low_part, seg)

    def only(x, k):
        return jnp.where(lane == k, x, jnp.zeros_like(x))

    receptance, key, value = rkv[0], rkv[1], rkv[2]
    decay = (
        -0.606531
        * jax.nn.sigmoid(coef[0:1, :] + dot(jnp.tanh(low[0]).astype(BF16), up[0]))
        * live
    )
    rate = jax.nn.sigmoid(coef[1:2, :] + dot(low[1].astype(BF16), up[1]))
    kappa = key * coef[2:3, :]
    kappa = kappa * lax.rsqrt(head_sum(kappa * kappa) + 1e-05)
    remove = -kappa * live
    write = kappa * rate * live
    key = key * live
    value = value * live
    d_high, d_rest = split(decay)
    d_mid, d_low = split(decay - d_high.astype(F32))
    total = dot(lower, d_high) + (dot(lower, d_mid) + dot(lower, d_low))
    middle = total[LMAX // 2 - 1 : LMAX // 2, :]
    last = total[LMAX - 1 : LMAX, :]
    back = jnp.exp(middle - total)
    pull = split(remove * jnp.exp(total - decay - middle))
    read = split(receptance * jnp.exp(total - middle))
    write_back = split(write * back)
    key_back = split(key * back)
    value_parts = split(value)

    left = tuple(
        jnp.concatenate([x for k in range(heads) for x in (only(pull[i], k), only(read[i], k))])
        for i in range(2)
    )
    right = tuple(jnp.concatenate([write_back[i], key_back[i]]) for i in range(2))
    pairs = dot3(left, right, ((1,), (1,)))
    strict = t > u
    t2 = lax.broadcasted_iota(jnp.int32, (LMAX, 2 * LMAX), 0)
    u2 = lax.rem(lax.broadcasted_iota(jnp.int32, (LMAX, 2 * LMAX), 1), LMAX)
    upto = t2 >= u2
    solves, pull_key, reads = [], [], []
    for k in range(heads):
        base = k * 2 * LMAX
        system = jnp.where(strict, pairs[base : base + LMAX, :LMAX], 0.0)
        pull_key.append(split(jnp.where(strict, pairs[base : base + LMAX, LMAX:], 0.0)))
        reads.append(split(jnp.where(upto, pairs[base + LMAX : base + 2 * LMAX], 0.0)))
        solves.append(system)
    inverse = []
    for k in range(heads):
        near = (t // 2 == u // 2)
        inverse.append(
            jnp.where(near, solves[k], 0.0) + (t == u).astype(F32)
        )
    size = 2
    while size < LMAX:
        inside = (t // (2 * size) == u // (2 * size)) & (t // size != u // size)
        grown = []
        for k in range(heads):
            known = split(inverse[k])
            cross = split(jnp.where(inside, solves[k], 0.0))
            product = split(dot3(known, cross))
            grown.append(inverse[k] + dot3(product, known))
        inverse = grown
        size *= 2

    def across(mats, parts):
        wide_left = tuple(jnp.concatenate([mat[i] for mat in mats], axis=1) for i in range(2))
        tall = tuple(
            jnp.concatenate([only(part[i], k) for k in range(heads) for part in parts])
            for i in range(2)
        )
        return dot3(wide_left, tall)

    start = across(pull_key, [value_parts])
    pulled = split(across([split(x) for x in inverse], [split(start)]))
    output = across(reads, [pulled, value_parts])
    tail = jnp.exp(last - total)
    write_tail = split(write * tail)
    key_tail = split(key * tail)
    tall = tuple(jnp.concatenate([pulled[i], value_parts[i]]) for i in range(2))
    tails = tuple(jnp.concatenate([write_tail[i], key_tail[i]]) for i in range(2))
    state = dot3(tall, tails, ((0,), (0,)))
    for k in range(heads):
        final[0, k] = state[k * HEAD : (k + 1) * HEAD, k * HEAD : (k + 1) * HEAD]
    bonus = head_sum(receptance * key * coef[3:4, :])
    out = (output + bonus * value) * live
    center = head_sum(out) * (1.0 / HEAD)
    out = out - center
    spread = head_sum(out * out) * (1.0 / HEAD)
    out = (out * lax.rsqrt(spread + 0.00064) * coef[4:5, :] + coef[5:6, :]).astype(BF16)
    for side in range(2):
        att[side] = out[:, side * FEAT : (side + 1) * FEAT]


def project_kernel(attg, own, w3, mid):
    q = lax.div(lax.axis_index("row"), 2)

    @pl.loop(0, MINE // TILE)
    def _(m):
        rows = pl.ds(pl.multiple_of(m * TILE, TILE), TILE)
        wide = jnp.concatenate([attg[j, rows, :] for j in range(N_ROW)], axis=1)
        weight = w3[...].reshape(SLICE, WIDTH)
        total = dot(wide, weight, ((1,), (1,)))
        for side in range(2):
            mid[side, rows, :] = (
                own[2 * q + side, rows, :].astype(F32) + total[:, side * FEAT : (side + 1) * FEAT]
            ).astype(BF16)


def mlp_kernel(midg, par, shift, wmg, theirs, own, part, held, act_scr, sems):
    q = lax.div(lax.axis_index("row"), 2)
    copies = [
        pltpu.make_async_copy(wmg.at[k, :, m], held.at[m, :, k], sems.at[m, k])
        for m in range(2)
        for k in range(N_COL)
    ]
    for copy in copies:
        copy.start()
    for copy in copies:
        copy.wait()

    @pl.loop(0, MINE // TILE)
    def _(m):
        at = pl.multiple_of(m * TILE, TILE)
        z = norm(blocks_of(midg, at), row_of(par, 2), row_of(par, 3))
        blend = (z + step_back(z) * shift[5:6, :]).astype(BF16)
        for side, weights in enumerate((held, theirs)):
            act = jnp.square(jnp.maximum(dot(blend, weights[0].reshape(WIDTH, MINE)), 0.0))
            act_scr[side] = act.astype(BF16)

        @pl.loop(0, N_CHIP)
        def _(n):
            total = None
            for side, weights in enumerate((held, theirs)):
                weight = weights[1, pl.ds(2 * n, 2)].reshape(SLICE, MINE)
                term = dot(act_scr[side], weight, ((1,), (1,)))
                total = term if total is None else total + term
            for side in range(2):
                added = jnp.where(n == q, own[side, pl.ds(at, TILE), :].astype(F32), 0.0)
                part[2 * n + side, pl.ds(at, TILE), :] = (
                    total[:, side * FEAT : (side + 1) * FEAT] + added
                ).astype(BF16)


def last_kernel(nx, par, shift, weight, out):
    @pl.loop(0, MINE // TILE)
    def _(m):
        at = pl.multiple_of(m * TILE, TILE)
        z = norm(blocks_of(nx, at), row_of(par, 4), row_of(par, 5))
        dz = step_back(z)
        for j in range(3):
            blend = (z + dz * shift[6 + j : 7 + j, :]).astype(BF16)
            out[j, pl.ds(at, TILE), :] = dot(
                blend, weight[:, :, j].reshape(WIDTH, SLICE)
            ).astype(BF16)


def time_core(lens, rkv, low, coef, up):
    prompts = rkv.shape[1] // LMAX
    return compute(
        core_kernel,
        [((2, prompts * LMAX, FEAT), BF16), ((prompts, SLICE // HEAD, HEAD, HEAD), F32)],
        (lens, rkv, low, coef, up),
        grid=(prompts,),
        in_specs=[
            pl.BlockSpec(memory_space=pltpu.SMEM),
            pl.BlockSpec((3, LMAX, SLICE), lambda p: (0, p, 0)),
            pl.BlockSpec((2, LMAX, low.shape[2]), lambda p: (0, p, 0)),
            pl.BlockSpec(coef.shape, lambda p: (0, 0)),
            pl.BlockSpec(up.shape, lambda p: (0, 0, 0)),
        ],
        out_specs=[
            pl.BlockSpec((2, LMAX, FEAT), lambda p: (0, p, 0)),
            pl.BlockSpec((1, SLICE // HEAD, HEAD, HEAD), lambda p: (p, 0, 0, 0)),
        ],
        flops=4 * 10**9,
    )


def per_device(
    hidden,
    lengths,
    square_matrix_shards,
    channel_mix_shards,
    lowrank_down,
    lowrank_up,
    token_shift_weights,
    attention_coefficients,
    norm_parameters,
):
    r = lax.axis_index("row")
    c = lax.axis_index("col")
    h = lax.rem(r, 2)
    q = lax.div(r, 2)
    square = square_matrix_shards.astype(BF16)
    mlp = channel_mix_shards.astype(BF16)
    wa, wm, wn, parg = exchange(
        swap_kernel,
        [
            ((3, N_ROW, 16, FEAT), BF16),
            ((N_ROW, 2, 16, MINE), BF16),
            ((N_COL, 3, 16, SLICE), BF16),
            ((N_ROW, 6, FEAT), F32),
        ],
        52,
        4,
        1,
        square,
        mlp,
        norm_parameters,
    )
    wmg = lax.all_gather(wm, "col", axis=0)
    weight_next = lax.all_gather(wn, "row", axis=0)
    hx, wt = exchange(
        start_kernel,
        [((N_ROW, MINE, FEAT), BF16), ((2, 3, N_ROW, N_COL, 16, FEAT), BF16)],
        1 + 7 + 1 + RING + 7,
        2,
        6,
        hidden,
        wa,
    )
    rkv, low = compute(
        mix_kernel,
        [((3, MINE, SLICE), F32), ((2, MINE, lowrank_down.shape[2]), F32)],
        (hx, parg, token_shift_weights, wt, lowrank_down),
        flops=4 * 10**9,
    )
    coef = lax.dynamic_slice_in_dim(attention_coefficients, q * SLICE, SLICE, 1)
    up = lax.dynamic_slice_in_dim(lowrank_up, q * SLICE, SLICE, 2)
    lens = lax.dynamic_slice_in_dim(lengths, c * 8 + h * 4, 4, 0)
    att, final = time_core(lens, rkv, low, coef, up)
    attg, w3x = exchange(
        att_kernel,
        [((N_ROW, MINE, FEAT), BF16), ((2, N_COL, 16, WIDTH), BF16)],
        7 + 1 + RING + 7,
        3,
        2,
        att,
        square[3],
    )
    moves = [
        ((2 * a + b) * N_COL + d, (2 * d + b) * N_COL + a)
        for a in range(N_CHIP)
        for b in range(2)
        for d in range(N_COL)
    ]
    final = lax.ppermute(final, ("row", "col"), moves)
    final_state = final.reshape(4, 4, HEAD * HEAD)
    (mid,) = compute(
        project_kernel,
        [((2, MINE, FEAT), BF16)],
        (attg, hx, w3x),
        flops=10**9,
    )
    midg, theirs = exchange(
        mid_kernel,
        [((N_ROW, MINE, FEAT), BF16), ((2, N_ROW, N_COL, 16, MINE), BF16)],
        16 + RING,
        2,
        3,
        mid,
        wmg,
    )
    (part,) = compute(
        mlp_kernel,
        [((N_ROW, MINE, FEAT), BF16)],
        (midg, parg, token_shift_weights, wmg, theirs, mid),
        scratch=[
            pltpu.VMEM((2, N_ROW, N_COL, 16, MINE), BF16),
            pltpu.VMEM((2, TILE, MINE), BF16),
            pltpu.SemaphoreType.DMA((2, N_COL)),
        ],
        in_specs=[VMEM, VMEM, VMEM, ANY, VMEM, VMEM],
        flops=5 * 10**9,
    )
    (got,) = exchange(sum_kernel, [((N_ROW, MINE, FEAT), BF16)], 15, 1, 4, part)
    out_hidden = (
        jnp.sum(got.reshape(N_CHIP, 2 * MINE, FEAT).astype(F32), axis=0).astype(BF16)
    )
    (nx,) = exchange(next_kernel, [((N_ROW, MINE, FEAT), BF16)], 16, 1, 5, out_hidden)
    (next_rkv,) = compute(
        last_kernel,
        [((3, MINE, SLICE), BF16)],
        (nx, parg, token_shift_weights, weight_next),
        flops=2 * 10**9,
    )
    return (out_hidden, next_rkv, final_state)


def solution(mesh):
    return jax.shard_map(
        per_device,
        mesh=mesh,
        in_specs=(
            P("col", "row"),
            P(),
            P(None, ("row", "col"), None),
            P(None, ("row", "col"), None),
            P(),
            P(),
            P(),
            P(),
            P(None, "row"),
        ),
        out_specs=(P("col", "row"), P(None, "row", "col"), P("row", "col", None)),
        check_vma=False,
    )
```

```python
import jax
import jax.numpy as jnp
from jax import lax
from jax.experimental import pallas as pl
from jax.experimental.pallas import tpu as pltpu
from jax.sharding import PartitionSpec as P

WIDTH = 2048
HEAD = 64
LMAX = 128
F32 = jnp.float32
BF16 = jnp.bfloat16
MESH = pl.DeviceIdType.MESH
ANY = pl.BlockSpec(memory_space=pl.ANY)
VMEM = pl.BlockSpec(memory_space=pltpu.VMEM)
N_ROW = 16
N_COL = 8
N_CHIP = 8
MINE = 512
FEAT = 128
SLICE = 256


def greet(devices):
    barrier = pltpu.get_barrier_semaphore()
    for device in devices:
        pl.semaphore_signal(barrier, inc=1, device_id=device, device_id_type=MESH)
    pl.semaphore_wait(barrier, len(devices))


def send(source, target, send_sem, recv_sem, device):
    copy = pltpu.make_async_remote_copy(
        src_ref=source,
        dst_ref=target,
        send_sem=send_sem,
        recv_sem=recv_sem,
        device_id=device,
        device_id_type=MESH,
    )
    copy.start()
    return copy


def keep(source, target, sem):
    copy = pltpu.make_async_copy(source, target, sem)
    copy.start()
    return copy


def exchange(kernel, outs, n_remote, n_local, collective_id, *operands):
    return pl.pallas_call(
        kernel,
        out_shape=[jax.ShapeDtypeStruct(*out) for out in outs],
        in_specs=[ANY] * len(operands),
        out_specs=[ANY] * len(outs),
        scratch_shapes=[
            pltpu.SemaphoreType.DMA((n_remote,)),
            pltpu.SemaphoreType.DMA((n_remote,)),
            pltpu.SemaphoreType.DMA((n_local,)),
        ],
        compiler_params=pltpu.CompilerParams(collective_id=collective_id, has_side_effects=True),
        cost_estimate=pl.CostEstimate(flops=0, bytes_accessed=48 * 2**20, transcendentals=0),
    )(*operands)


def place():
    r = lax.axis_index("row")
    c = lax.axis_index("col")
    h = lax.rem(r, 2)
    return r, c, h, lax.div(r, 2), r + 1 - 2 * h


class Links:
    def __init__(self, send_sem, recv_sem, first=0):
        self.send_sem = send_sem
        self.recv_sem = recv_sem
        self.slot = first
        self.copies = []
        self.open = []

    def go(self, source, target, device):
        copy = send(
            source, target, self.send_sem.at[self.slot], self.recv_sem.at[self.slot], device
        )
        self.slot += 1
        self.copies.append(copy)
        self.open.append(copy)
        return copy

    def arrive(self, copy):
        copy.wait_recv()
        self.open = [other for other in self.open if other is not copy]

    def finish(self):
        for copy in self.open:
            copy.wait_recv()
        for copy in self.copies:
            copy.wait_send()


RING = 14


def ring_at(axis):
    r, c, h, q, _ = place()
    here = q if axis == "row" else c
    step_z = 1 - 2 * lax.rem(here, 2)
    chips = {
        "p": lax.rem(here + 2, 8),
        "m": lax.rem(here + 6, 8),
        "z": here + step_z,
        "o": lax.rem(here + 4, 8),
        "pz": lax.rem(here + 2, 8) + step_z,
        "mz": lax.rem(here + 6, 8) + step_z,
        "oz": lax.rem(here + 4, 8) + step_z,
    }
    devices = {
        side: (2 * chips[side] + h, c) if axis == "row" else (r, chips[side]) for side in "pmz"
    }
    return here, chips, devices


def ring_peers(axis):
    return list(ring_at(axis)[2].values())


def ring(links, axis, slot, own=None, which=(0, 1), ready=None, seen=None):
    here, chips, to = ring_at(axis)
    heavy = axis == "row"
    seen = seen or (lambda chip, half: None)

    def take(copy, chip, half):
        links.arrive(copy)
        seen(chip, half)

    def forward(chip, half, side):
        return links.go(slot(chip, half), slot(chip, half), to[side])

    first = {}
    for k in range(2):
        if ready is not None:
            ready(k)
        source = own(k) if own is not None else slot(here, which[k])
        for side in "pmz":
            first[side, k] = links.go(source, slot(here, which[k]), to[side])
    yield
    for k in range(2):
        take(first["p", k], chips["m"], which[k])
    low = forward(chips["m"], 0, "p")
    for k in range(2):
        take(first["m", k], chips["p"], which[k])
    high = forward(chips["p"], 1, "m")
    yield
    beside = {}
    for k in range(2):
        take(first["z", k], chips["z"], which[k])
        for side in "pm":
            beside[side, k] = forward(chips["z"], which[k], side)
    yield
    if heavy:
        take(low, chips["o"], 0)
        low = forward(chips["o"], 0, "z")
        take(high, chips["o"], 1)
        high = forward(chips["o"], 1, "z")
        yield
        for k in range(2):
            take(beside["p", k], chips["mz"], which[k])
            take(beside["m", k], chips["pz"], which[k])
    else:
        take(low, chips["o"], 0)
        take(high, chips["o"], 1)
        for k in range(2):
            take(beside["p", k], chips["mz"], which[k])
        low = forward(chips["mz"], 0, "p")
        for k in range(2):
            take(beside["m", k], chips["pz"], which[k])
        high = forward(chips["pz"], 1, "m")
        yield
    take(low, chips["oz"], 0)
    take(high, chips["oz"], 1)


def together(*steps):
    active = list(steps)
    while active:
        for step in list(active):
            if next(step, StopIteration) is StopIteration:
                active.remove(step)


def aligned(index, size):
    return pl.ds(pl.multiple_of(index * size, size), size)


def start_kernel(
    square, mlp, par, hid, hx, wt, w3, wk, wv, wn, parg, send_sem, recv_sem, local_sem
):
    r, c, h, q, sibling = place()
    rows = [lax.rem(r + d, N_ROW) for d in range(1, N_ROW)]
    cols = [lax.rem(c + d, N_COL) for d in range(1, N_COL)]

    def time_part(p):
        return square.at[pl.ds(0, 3), :, aligned(p, FEAT)]

    def key_part(p):
        return mlp.at[0, :, aligned(p, MINE)]

    def value_part(p):
        return mlp.at[1, :, aligned(p, MINE)]

    def next_part(p):
        return square.at[pl.ds(4, 3), :, aligned(p, SLICE)]

    mine = hid.at[aligned(h, MINE)]
    local = [
        keep(time_part(r), wt.at[h, :, r, c], local_sem.at[0]),
        keep(par, parg.at[r], local_sem.at[1]),
        keep(mine, hx.at[r], local_sem.at[2]),
        keep(square.at[3], w3.at[c], local_sem.at[3]),
        keep(key_part(r), wk.at[c, r], local_sem.at[4]),
        keep(value_part(r), wv.at[c, r], local_sem.at[5]),
        keep(next_part(c), wn.at[r, c], local_sem.at[6]),
    ]
    greet([(p, c) for p in rows] + [(r, p) for p in cols])
    links = Links(send_sem, recv_sem)
    times = [links.go(time_part(p), wt.at[lax.rem(p, 2), :, r, c], (p, c)) for p in rows]
    other = links.go(hid.at[aligned(1 - h, MINE)], hx.at[r], (sibling, c))

    def hid_own(k):
        return (mine, hx.at[sibling])[k]

    def hid_ready(k):
        if k == 1:
            links.arrive(other)

    def time_ready(k):
        if k == 0:
            for copy in times:
                links.arrive(copy)
            local[0].wait()
            links.go(wt.at[h, :, :, c], wt.at[h, :, :, c], (sibling, c))

    def time_slot(chip, half):
        return wt.at[h, :, pl.ds(8 * half, 8), chip]

    def time_seen(chip, half):
        links.go(time_slot(chip, half), time_slot(chip, half), (sibling, c))

    def out_slot(chip, half):
        return w3.at[chip, :, pl.ds(1024 * half, 1024)]

    def out_own(k):
        return square.at[3, :, pl.ds(1024 * k, 1024)]

    def rest():
        for p in rows:
            links.go(par, parg.at[r], (p, c))
        yield
        for p in rows:
            links.go(key_part(p), wk.at[c, r], (p, c))
        for p in cols:
            links.go(next_part(p), wn.at[r, c], (r, p))
        for p in rows:
            links.go(value_part(p), wv.at[c, r], (p, c))

    together(
        ring(
            links,
            "row",
            lambda chip, side: hx.at[2 * chip + side],
            own=hid_own,
            which=(h, 1 - h),
            ready=hid_ready,
        ),
        ring(links, "col", time_slot, ready=time_ready, seen=time_seen),
        rest(),
        ring(links, "col", out_slot, own=out_own),
    )
    links.finish()
    for copy in local[1:]:
        copy.wait()


def row_ring(links, source, target):
    return ring(
        links, "row", lambda chip, side: target.at[2 * chip + side], own=lambda k: source.at[k]
    )


def own_block(source, target, q, local_sem):
    return [keep(source.at[k], target.at[2 * q + k], local_sem.at[k]) for k in range(2)]


def att_kernel(att, w3, wk, attg, w3x, wkg, send_sem, recv_sem, local_sem):
    r, c, h, q, sibling = place()
    local = own_block(att, attg, q, local_sem)
    greet([(sibling, c)] + ring_peers("row") + ring_peers("col"))
    links = Links(send_sem, recv_sem)
    links.go(w3, w3x, (sibling, c))
    together(
        row_ring(links, att, attg),
        ring(
            links,
            "col",
            lambda chip, half: wkg.at[chip, pl.ds(8 * half, 8)],
            own=lambda k: wk.at[c, pl.ds(8 * k, 8)],
        ),
    )
    links.finish()
    for copy in local:
        copy.wait()


def mid_kernel(mid, wk, wkg, wv, midg, wvg, theirs, send_sem, recv_sem, local_sem):
    r, c, h, q, sibling = place()
    local = own_block(mid, midg, q, local_sem)
    greet([(sibling, c)] + ring_peers("row") + ring_peers("col"))
    links = Links(send_sem, recv_sem)

    def value_slot(chip, half):
        return wvg.at[chip, pl.ds(8 * half, 8)]

    def value_seen(chip, half):
        links.go(
            value_slot(chip, half), theirs.at[1, pl.ds(8 * half, 8), chip], (sibling, c)
        )

    def across():
        links.go(wk.at[c], theirs.at[0, :, c], (sibling, c))
        links.go(wv.at[c], theirs.at[1, :, c], (sibling, c))
        for d in range(1, N_COL):
            p = lax.rem(c + d, N_COL)
            links.go(wkg.at[p], theirs.at[0, :, p], (sibling, c))
        yield

    together(
        row_ring(links, mid, midg),
        ring(
            links,
            "col",
            value_slot,
            own=lambda k: wv.at[c, pl.ds(8 * k, 8)],
            seen=value_seen,
        ),
        across(),
    )
    links.finish()
    for copy in local:
        copy.wait()


def sum_kernel(part, got, send_sem, recv_sem, local_sem):
    r, c, h, q, sibling = place()
    rows = [lax.rem(r + d, N_ROW) for d in range(1, N_ROW)]
    local = keep(part.at[r], got.at[r], local_sem.at[0])
    greet([(p, c) for p in rows])
    links = Links(send_sem, recv_sem)
    for p in rows:
        links.go(part.at[p], got.at[r], (p, c))
    links.finish()
    local.wait()


def next_kernel(out, wn, got, wng, send_sem, recv_sem, local_sem):
    r, c, h, q, sibling = place()
    barrier = pltpu.get_barrier_semaphore()

    def target(i):
        return (2 * c + lax.rem(h + i, 2), q)

    peers = ring_peers("row") + ring_peers("col") + [(sibling, c)]

    @pl.when(q != c)
    def _():
        for i in range(2):
            pl.semaphore_signal(barrier, inc=1, device_id=target(i), device_id_type=MESH)

    for device in peers:
        pl.semaphore_signal(barrier, inc=1, device_id=device, device_id_type=MESH)
    pl.semaphore_wait(barrier, len(peers) + 2 * (q != c).astype(jnp.int32))

    def piece(i):
        return out.at[aligned(lax.rem(h + i, 2), MINE)]

    def move(i):
        return pltpu.make_async_remote_copy(
            src_ref=piece(i),
            dst_ref=got.at[2 * q + h],
            send_sem=send_sem.at[i],
            recv_sem=recv_sem.at[h],
            device_id=target(i),
            device_id_type=MESH,
        )

    @pl.when(q == c)
    def _():
        keep(piece(0), got.at[r], recv_sem.at[h])

    @pl.when(q != c)
    def _():
        move(0).start()

    move(1).start()
    local = keep(wn.at[r], wng.at[r], local_sem.at[0])
    links = Links(send_sem, recv_sem, 2)

    def out_ready(k):
        block = got.at[2 * c + k]
        pltpu.make_async_copy(block, block, recv_sem.at[k]).wait()

    def weight_slot(chip, half):
        return wng.at[2 * chip + h, pl.ds(4 * half, 4)]

    def weight_seen(chip, half):
        links.go(weight_slot(chip, half), weight_slot(chip, half), (sibling, c))

    def across():
        links.go(wn.at[r], wng.at[r], (sibling, c))
        yield

    together(
        across(),
        ring(
            links,
            "row",
            weight_slot,
            own=lambda k: wn.at[r, pl.ds(4 * k, 4)],
            seen=weight_seen,
        ),
        ring(links, "col", lambda chip, side: got.at[2 * chip + side], ready=out_ready),
    )
    links.finish()
    local.wait()

    @pl.when(q != c)
    def _():
        move(0).wait_send()

    move(1).wait_send()


def compute(kernel, outs, operands, scratch=(), grid=None, in_specs=None, out_specs=None, flops=0):
    return pl.pallas_call(
        kernel,
        grid=grid if grid is not None else (),
        out_shape=[jax.ShapeDtypeStruct(*out) for out in outs],
        in_specs=in_specs if in_specs is not None else [VMEM] * len(operands),
        out_specs=out_specs if out_specs is not None else [VMEM] * len(outs),
        scratch_shapes=list(scratch),
        compiler_params=pltpu.CompilerParams(vmem_limit_bytes=56 * 2**20),
        cost_estimate=pl.CostEstimate(flops=flops, bytes_accessed=16 * 2**20, transcendentals=0),
    )(*operands)


def dot(a, b, dims=((1,), (0,))):
    return lax.dot_general(a, b, (dims, ((), ())), preferred_element_type=F32)


def split(x):
    high = x.astype(BF16)
    return high, (x - high.astype(F32)).astype(BF16)


def dot3(a, b, dims=((1,), (0,))):
    a_high, a_low = a
    b_high, b_low = b
    return dot(a_high, b_high, dims) + (dot(a_high, b_low, dims) + dot(a_low, b_high, dims))


def norm(source, gain, bias):
    center = jnp.sum(source, axis=-1, keepdims=True) / WIDTH
    second = jnp.sum(source * source, axis=-1, keepdims=True) / WIDTH
    scaled = (source - center) * lax.rsqrt(second - center * center + 1e-05)
    return (scaled * gain + bias).astype(BF16).astype(F32)


def row_of(par, i):
    return jnp.concatenate([par[j, i : i + 1, :] for j in range(N_ROW)], axis=1)


def step_back(z):
    position = lax.rem(lax.broadcasted_iota(jnp.int32, z.shape, 0), LMAX)
    return jnp.where(position == 0, 0.0, pltpu.roll(z, 1, 0)) - z


TILE = 256


def blocks_of(ref, at):
    return jnp.concatenate(
        [ref[j, pl.ds(at, TILE), :].astype(F32) for j in range(ref.shape[0])], axis=1
    )


def mix_kernel(hx, par, shift, wt, down, rkv, low):
    @pl.loop(0, MINE // TILE)
    def _(m):
        at = pl.multiple_of(m * TILE, TILE)
        z = norm(blocks_of(hx, at), row_of(par, 0), row_of(par, 1))
        dz = step_back(z)
        for j in range(5):
            blend = (z + dz * shift[j : j + 1, :]).astype(BF16)
            if j < 3:
                weight = jnp.concatenate(
                    [wt[side, j].reshape(WIDTH, FEAT) for side in range(2)], axis=1
                )
                rkv[j, pl.ds(at, TILE), :] = dot(blend, weight)
            else:
                low[j - 3, pl.ds(at, TILE), :] = dot(blend, down[j - 3])


def core_kernel(lens, rkv, low, coef, up, att, final):
    length = lens[pl.program_id(0)]
    wide = SLICE
    heads = wide // HEAD
    live = (lax.broadcasted_iota(jnp.int32, (LMAX, wide), 0) < length).astype(F32)
    lane = lax.broadcasted_iota(jnp.int32, (LMAX, wide), 1) // HEAD
    t = lax.broadcasted_iota(jnp.int32, (LMAX, LMAX), 0)
    u = lax.broadcasted_iota(jnp.int32, (LMAX, LMAX), 1)
    seg = (
        lax.broadcasted_iota(jnp.int32, (wide, wide), 0) // HEAD
        == lax.broadcasted_iota(jnp.int32, (wide, wide), 1) // HEAD
    ).astype(F32).astype(BF16)
    lower = (t >= u).astype(F32).astype(BF16)

    def head_sum(x):
        high, low_part = split(x)
        return dot(high, seg) + dot(low_part, seg)

    def only(x, k):
        return jnp.where(lane == k, x, jnp.zeros_like(x))

    receptance, key, value = rkv[0], rkv[1], rkv[2]
    decay = (
        -0.606531
        * jax.nn.sigmoid(coef[0:1, :] + dot(jnp.tanh(low[0]).astype(BF16), up[0]))
        * live
    )
    rate = jax.nn.sigmoid(coef[1:2, :] + dot(low[1].astype(BF16), up[1]))
    kappa = key * coef[2:3, :]
    kappa = kappa * lax.rsqrt(head_sum(kappa * kappa) + 1e-05)
    remove = -kappa * live
    write = kappa * rate * live
    key = key * live
    value = value * live
    d_high, d_rest = split(decay)
    d_mid, d_low = split(decay - d_high.astype(F32))
    total = dot(lower, d_high) + (dot(lower, d_mid) + dot(lower, d_low))
    middle = total[LMAX // 2 - 1 : LMAX // 2, :]
    last = total[LMAX - 1 : LMAX, :]
    back = jnp.exp(middle - total)
    pull = split(remove * jnp.exp(total - decay - middle))
    read = split(receptance * jnp.exp(total - middle))
    write_back = split(write * back)
    key_back = split(key * back)
    value_parts = split(value)

    left = tuple(
        jnp.concatenate([x for k in range(heads) for x in (only(pull[i], k), only(read[i], k))])
        for i in range(2)
    )
    right = tuple(jnp.concatenate([write_back[i], key_back[i]]) for i in range(2))
    pairs = dot3(left, right, ((1,), (1,)))
    strict = t > u
    t2 = lax.broadcasted_iota(jnp.int32, (LMAX, 2 * LMAX), 0)
    u2 = lax.rem(lax.broadcasted_iota(jnp.int32, (LMAX, 2 * LMAX), 1), LMAX)
    upto = t2 >= u2
    solves, pull_key, reads = [], [], []
    for k in range(heads):
        base = k * 2 * LMAX
        system = jnp.where(strict, pairs[base : base + LMAX, :LMAX], 0.0)
        pull_key.append(split(jnp.where(strict, pairs[base : base + LMAX, LMAX:], 0.0)))
        reads.append(split(jnp.where(upto, pairs[base + LMAX : base + 2 * LMAX], 0.0)))
        solves.append(system)
    inverse = []
    for k in range(heads):
        near = (t // 2 == u // 2)
        inverse.append(
            jnp.where(near, solves[k], 0.0) + (t == u).astype(F32)
        )
    size = 2
    while size < LMAX:
        inside = (t // (2 * size) == u // (2 * size)) & (t // size != u // size)
        grown = []
        for k in range(heads):
            known = split(inverse[k])
            cross = split(jnp.where(inside, solves[k], 0.0))
            product = split(dot3(known, cross))
            grown.append(inverse[k] + dot3(product, known))
        inverse = grown
        size *= 2

    def across(mats, parts):
        wide_left = tuple(jnp.concatenate([mat[i] for mat in mats], axis=1) for i in range(2))
        tall = tuple(
            jnp.concatenate([only(part[i], k) for k in range(heads) for part in parts])
            for i in range(2)
        )
        return dot3(wide_left, tall)

    start = across(pull_key, [value_parts])
    pulled = split(across([split(x) for x in inverse], [split(start)]))
    output = across(reads, [pulled, value_parts])
    tail = jnp.exp(last - total)
    write_tail = split(write * tail)
    key_tail = split(key * tail)
    tall = tuple(jnp.concatenate([pulled[i], value_parts[i]]) for i in range(2))
    tails = tuple(jnp.concatenate([write_tail[i], key_tail[i]]) for i in range(2))
    state = dot3(tall, tails, ((0,), (0,)))
    for k in range(heads):
        final[0, k] = state[k * HEAD : (k + 1) * HEAD, k * HEAD : (k + 1) * HEAD]
    bonus = head_sum(receptance * key * coef[3:4, :])
    out = (output + bonus * value) * live
    center = head_sum(out) * (1.0 / HEAD)
    out = out - center
    spread = head_sum(out * out) * (1.0 / HEAD)
    out = (out * lax.rsqrt(spread + 0.00064) * coef[4:5, :] + coef[5:6, :]).astype(BF16)
    for side in range(2):
        att[side] = out[:, side * FEAT : (side + 1) * FEAT]


def project_kernel(attg, own, w3, w3x, mid):
    r = lax.axis_index("row")
    h = lax.rem(r, 2)

    @pl.loop(0, MINE // TILE)
    def _(m):
        rows = pl.ds(pl.multiple_of(m * TILE, TILE), TILE)
        wide = jnp.concatenate([attg[j, rows, :] for j in range(N_ROW)], axis=1)
        weight = jnp.concatenate([w[...].reshape(FEAT, WIDTH) for w in (w3, w3x)])
        total = dot(wide, weight, ((1,), (1,)))
        for k, side in enumerate((h, 1 - h)):
            mid[side, rows, :] = (
                own[r - h + side, rows, :].astype(F32) + total[:, k * FEAT : (k + 1) * FEAT]
            ).astype(BF16)


def mlp_kernel(midg, par, shift, wk, wkg, wv, wvg, theirs, own, part, held, act_scr, sems):
    q = lax.div(lax.axis_index("row"), 2)
    c = lax.axis_index("col")
    copies = []
    for m, (near, far) in enumerate(((wk, wkg), (wv, wvg))):
        copies.append(pltpu.make_async_copy(near.at[c], held.at[m, :, c], sems.at[m, 0]))
        for d in range(1, N_COL):
            p = lax.rem(c + d, N_COL)
            copies.append(pltpu.make_async_copy(far.at[p], held.at[m, :, p], sems.at[m, d]))
    for copy in copies:
        copy.start()
    for copy in copies:
        copy.wait()

    @pl.loop(0, MINE // TILE)
    def _(m):
        at = pl.multiple_of(m * TILE, TILE)
        z = norm(blocks_of(midg, at), row_of(par, 2), row_of(par, 3))
        blend = (z + step_back(z) * shift[5:6, :]).astype(BF16)
        for side, weights in enumerate((held, theirs)):
            act = jnp.square(jnp.maximum(dot(blend, weights[0].reshape(WIDTH, MINE)), 0.0))
            act_scr[side] = act.astype(BF16)

        @pl.loop(0, N_CHIP)
        def _(n):
            total = None
            for side, weights in enumerate((held, theirs)):
                weight = weights[1, pl.ds(2 * n, 2)].reshape(SLICE, MINE)
                term = dot(act_scr[side], weight, ((1,), (1,)))
                total = term if total is None else total + term
            for side in range(2):
                added = jnp.where(n == q, own[side, pl.ds(at, TILE), :].astype(F32), 0.0)
                part[2 * n + side, pl.ds(at, TILE), :] = (
                    total[:, side * FEAT : (side + 1) * FEAT] + added
                ).astype(BF16)


def last_kernel(nx, par, shift, weight, out):
    @pl.loop(0, MINE // TILE)
    def _(m):
        at = pl.multiple_of(m * TILE, TILE)
        z = norm(blocks_of(nx, at), row_of(par, 4), row_of(par, 5))
        dz = step_back(z)
        for j in range(3):
            blend = (z + dz * shift[6 + j : 7 + j, :]).astype(BF16)
            out[j, pl.ds(at, TILE), :] = dot(
                blend, weight[:, :, j].reshape(WIDTH, SLICE)
            ).astype(BF16)


def time_core(lens, rkv, low, coef, up):
    prompts = rkv.shape[1] // LMAX
    return compute(
        core_kernel,
        [((2, prompts * LMAX, FEAT), BF16), ((prompts, SLICE // HEAD, HEAD, HEAD), F32)],
        (lens, rkv, low, coef, up),
        grid=(prompts,),
        in_specs=[
            pl.BlockSpec(memory_space=pltpu.SMEM),
            pl.BlockSpec((3, LMAX, SLICE), lambda p: (0, p, 0)),
            pl.BlockSpec((2, LMAX, low.shape[2]), lambda p: (0, p, 0)),
            pl.BlockSpec(coef.shape, lambda p: (0, 0)),
            pl.BlockSpec(up.shape, lambda p: (0, 0, 0)),
        ],
        out_specs=[
            pl.BlockSpec((2, LMAX, FEAT), lambda p: (0, p, 0)),
            pl.BlockSpec((1, SLICE // HEAD, HEAD, HEAD), lambda p: (p, 0, 0, 0)),
        ],
        flops=4 * 10**9,
    )


def per_device(
    hidden,
    lengths,
    square_matrix_shards,
    channel_mix_shards,
    lowrank_down,
    lowrank_up,
    token_shift_weights,
    attention_coefficients,
    norm_parameters,
):
    r = lax.axis_index("row")
    c = lax.axis_index("col")
    h = lax.rem(r, 2)
    q = lax.div(r, 2)
    square = square_matrix_shards.astype(BF16)
    mlp = channel_mix_shards.astype(BF16)
    hx, wt, w3, wk, wv, wn, parg = exchange(
        start_kernel,
        [
            ((N_ROW, MINE, FEAT), BF16),
            ((2, 3, N_ROW, N_COL, 16, FEAT), BF16),
            ((N_COL, 16, WIDTH), BF16),
            ((N_COL, N_ROW, 16, MINE), BF16),
            ((N_COL, N_ROW, 16, MINE), BF16),
            ((N_ROW, N_COL, 3, 16, SLICE), BF16),
            ((N_ROW, 6, FEAT), F32),
        ],
        15 + 1 + 3 * RING + 1 + 14 + 15 + 15 + 7 + 15,
        7,
        1,
        square,
        mlp,
        norm_parameters,
        hidden,
    )
    rkv, low = compute(
        mix_kernel,
        [((3, MINE, SLICE), F32), ((2, MINE, lowrank_down.shape[2]), F32)],
        (hx, parg, token_shift_weights, wt, lowrank_down),
        flops=4 * 10**9,
    )
    coef = lax.dynamic_slice_in_dim(attention_coefficients, q * SLICE, SLICE, 1)
    up = lax.dynamic_slice_in_dim(lowrank_up, q * SLICE, SLICE, 2)
    lens = lax.dynamic_slice_in_dim(lengths, c * 8 + h * 4, 4, 0)
    att, final = time_core(lens, rkv, low, coef, up)
    attg, w3x, wkg = exchange(
        att_kernel,
        [
            ((N_ROW, MINE, FEAT), BF16),
            ((N_COL, 16, WIDTH), BF16),
            ((N_COL, N_ROW, 16, MINE), BF16),
        ],
        1 + 2 * RING,
        2,
        2,
        att,
        w3,
        wk,
    )
    moves = [
        ((2 * a + b) * N_COL + d, (2 * d + b) * N_COL + a)
        for a in range(N_CHIP)
        for b in range(2)
        for d in range(N_COL)
    ]
    final = lax.ppermute(final, ("row", "col"), moves)
    final_state = final.reshape(4, 4, HEAD * HEAD)
    (mid,) = compute(
        project_kernel,
        [((2, MINE, FEAT), BF16)],
        (attg, hx, w3, w3x),
        flops=10**9,
    )
    midg, wvg, theirs = exchange(
        mid_kernel,
        [
            ((N_ROW, MINE, FEAT), BF16),
            ((N_COL, N_ROW, 16, MINE), BF16),
            ((2, N_ROW, N_COL, 16, MINE), BF16),
        ],
        9 + 14 + 2 * RING,
        2,
        3,
        mid,
        wk,
        wkg,
        wv,
    )
    (part,) = compute(
        mlp_kernel,
        [((N_ROW, MINE, FEAT), BF16)],
        (midg, parg, token_shift_weights, wk, wkg, wv, wvg, theirs, mid),
        scratch=[
            pltpu.VMEM((2, N_ROW, N_COL, 16, MINE), BF16),
            pltpu.VMEM((2, TILE, MINE), BF16),
            pltpu.SemaphoreType.DMA((2, N_COL)),
        ],
        in_specs=[VMEM] * 3 + [ANY] * 4 + [VMEM] * 2,
        flops=5 * 10**9,
    )
    (got,) = exchange(sum_kernel, [((N_ROW, MINE, FEAT), BF16)], 15, 1, 4, part)
    out_hidden = (
        jnp.sum(got.reshape(N_CHIP, 2 * MINE, FEAT).astype(F32), axis=0).astype(BF16)
    )
    nx, weight_next = exchange(
        next_kernel,
        [((N_ROW, MINE, FEAT), BF16), ((N_ROW, N_COL, 3, 16, SLICE), BF16)],
        2 + 1 + 14 + 2 * RING,
        1,
        5,
        out_hidden,
        wn,
    )
    (next_rkv,) = compute(
        last_kernel,
        [((3, MINE, SLICE), BF16)],
        (nx, parg, token_shift_weights, weight_next),
        flops=2 * 10**9,
    )
    return (out_hidden, next_rkv, final_state)


def solution(mesh):
    return jax.shard_map(
        per_device,
        mesh=mesh,
        in_specs=(
            P("col", "row"),
            P(),
            P(None, ("row", "col"), None),
            P(None, ("row", "col"), None),
            P(),
            P(),
            P(),
            P(),
            P(None, "row"),
        ),
        out_specs=(P("col", "row"), P(None, "row", "col"), P("row", "col", None)),
        check_vma=False,
    )
```

```python
import jax
import jax.numpy as jnp
from jax import lax
from jax.experimental import pallas as pl
from jax.experimental.pallas import tpu as pltpu
from jax.sharding import PartitionSpec as P

WIDTH = 2048
HEAD = 64
LMAX = 128
F32 = jnp.float32
BF16 = jnp.bfloat16
MESH = pl.DeviceIdType.MESH
ANY = pl.BlockSpec(memory_space=pl.ANY)
VMEM = pl.BlockSpec(memory_space=pltpu.VMEM)
N_ROW = 16
N_COL = 8
N_CHIP = 8
MINE = 512
FEAT = 128
SLICE = 256


def greet(devices):
    barrier = pltpu.get_barrier_semaphore()
    for device in devices:
        pl.semaphore_signal(barrier, inc=1, device_id=device, device_id_type=MESH)
    pl.semaphore_wait(barrier, len(devices))


def send(source, target, send_sem, recv_sem, device):
    copy = pltpu.make_async_remote_copy(
        src_ref=source,
        dst_ref=target,
        send_sem=send_sem,
        recv_sem=recv_sem,
        device_id=device,
        device_id_type=MESH,
    )
    copy.start()
    return copy


def keep(source, target, sem):
    copy = pltpu.make_async_copy(source, target, sem)
    copy.start()
    return copy


def exchange(
    kernel,
    outs,
    n_remote,
    n_local,
    collective_id,
    *operands,
    scratch=(),
    in_specs=None,
    out_specs=None,
):
    return pl.pallas_call(
        kernel,
        out_shape=[jax.ShapeDtypeStruct(*out) for out in outs],
        in_specs=in_specs or [ANY] * len(operands),
        out_specs=out_specs or [ANY] * len(outs),
        scratch_shapes=[
            pltpu.SemaphoreType.DMA((n_remote,)),
            pltpu.SemaphoreType.DMA((n_remote,)),
            pltpu.SemaphoreType.DMA((n_local,)),
            *scratch,
        ],
        compiler_params=pltpu.CompilerParams(
            collective_id=collective_id, has_side_effects=True, vmem_limit_bytes=56 * 2**20
        ),
        cost_estimate=pl.CostEstimate(flops=0, bytes_accessed=48 * 2**20, transcendentals=0),
    )(*operands)


def place():
    r = lax.axis_index("row")
    c = lax.axis_index("col")
    h = lax.rem(r, 2)
    return r, c, h, lax.div(r, 2), r + 1 - 2 * h


class Links:
    def __init__(self, send_sem, recv_sem, first=0):
        self.send_sem = send_sem
        self.recv_sem = recv_sem
        self.slot = first
        self.copies = []
        self.open = []

    def go(self, source, target, device):
        copy = send(
            source, target, self.send_sem.at[self.slot], self.recv_sem.at[self.slot], device
        )
        self.slot += 1
        self.copies.append(copy)
        self.open.append(copy)
        return copy

    def arrive(self, copy):
        copy.wait_recv()
        self.open = [other for other in self.open if other is not copy]

    def finish(self):
        for copy in self.open:
            copy.wait_recv()
        for copy in self.copies:
            copy.wait_send()


RING = 14


def ring_at(axis):
    r, c, h, q, _ = place()
    here = q if axis == "row" else c
    step_z = 1 - 2 * lax.rem(here, 2)
    chips = {
        "p": lax.rem(here + 2, 8),
        "m": lax.rem(here + 6, 8),
        "z": here + step_z,
        "o": lax.rem(here + 4, 8),
        "pz": lax.rem(here + 2, 8) + step_z,
        "mz": lax.rem(here + 6, 8) + step_z,
        "oz": lax.rem(here + 4, 8) + step_z,
    }
    devices = {
        side: (2 * chips[side] + h, c) if axis == "row" else (r, chips[side]) for side in "pmz"
    }
    return here, chips, devices


def ring_peers(axis):
    return list(ring_at(axis)[2].values())


def ring(links, axis, slot, own=None, which=(0, 1), ready=None, seen=None):
    here, chips, to = ring_at(axis)
    heavy = axis == "row"
    seen = seen or (lambda chip, half: None)

    def take(copy, chip, half):
        links.arrive(copy)
        seen(chip, half)

    def forward(chip, half, side):
        return links.go(slot(chip, half), slot(chip, half), to[side])

    first = {}
    for k in range(2):
        if ready is not None:
            ready(k)
        source = own(k) if own is not None else slot(here, which[k])
        for side in "pmz":
            first[side, k] = links.go(source, slot(here, which[k]), to[side])
    yield
    for k in range(2):
        take(first["p", k], chips["m"], which[k])
    low = forward(chips["m"], 0, "p")
    for k in range(2):
        take(first["m", k], chips["p"], which[k])
    high = forward(chips["p"], 1, "m")
    yield
    beside = {}
    for k in range(2):
        take(first["z", k], chips["z"], which[k])
        for side in "pm":
            beside[side, k] = forward(chips["z"], which[k], side)
    yield
    if heavy:
        take(low, chips["o"], 0)
        low = forward(chips["o"], 0, "z")
        take(high, chips["o"], 1)
        high = forward(chips["o"], 1, "z")
        yield
        for k in range(2):
            take(beside["p", k], chips["mz"], which[k])
            take(beside["m", k], chips["pz"], which[k])
    else:
        take(low, chips["o"], 0)
        take(high, chips["o"], 1)
        for k in range(2):
            take(beside["p", k], chips["mz"], which[k])
        low = forward(chips["mz"], 0, "p")
        for k in range(2):
            take(beside["m", k], chips["pz"], which[k])
        high = forward(chips["pz"], 1, "m")
        yield
    take(low, chips["oz"], 0)
    take(high, chips["oz"], 1)


def together(*steps):
    active = list(steps)
    while active:
        for step in list(active):
            if next(step, StopIteration) is StopIteration:
                active.remove(step)


def aligned(index, size):
    return pl.ds(pl.multiple_of(index * size, size), size)


def start_kernel(
    square_in,
    mlp_in,
    par,
    hid,
    hx,
    wt,
    w3,
    wk,
    wv,
    wn,
    parg,
    send_sem,
    recv_sem,
    local_sem,
    square_wide,
    mlp_wide,
    square,
    mlp,
):
    r, c, h, q, sibling = place()
    rows = [lax.rem(r + d, N_ROW) for d in range(1, N_ROW)]
    cols = [lax.rem(c + d, N_COL) for d in range(1, N_COL)]

    def time_part(p):
        return square.at[pl.ds(0, 3), :, aligned(p, FEAT)]

    def key_part(p):
        return mlp.at[0, :, aligned(p, MINE)]

    def value_part(p):
        return mlp.at[1, :, aligned(p, MINE)]

    def next_part(p):
        return square.at[pl.ds(4, 3), :, aligned(p, SLICE)]

    mine = hid.at[aligned(h, MINE)]
    square_load = keep(square_in, square_wide, local_sem.at[7])
    mlp_load = keep(mlp_in, mlp_wide, local_sem.at[8])
    local = [
        keep(par, parg.at[r], local_sem.at[1]),
        keep(mine, hx.at[r], local_sem.at[2]),
    ]
    greet([(p, c) for p in rows] + [(r, p) for p in cols])
    links = Links(send_sem, recv_sem)
    times = []
    other = links.go(hid.at[aligned(1 - h, MINE)], hx.at[r], (sibling, c))

    def hid_own(k):
        return (mine, hx.at[sibling])[k]

    def hid_ready(k):
        if k == 1:
            links.arrive(other)

    def time_ready(k):
        if k == 0:
            for copy in times:
                links.arrive(copy)
            links.go(wt.at[h, :, :, c], wt.at[h, :, :, c], (sibling, c))

    def time_slot(chip, half):
        return wt.at[h, :, pl.ds(8 * half, 8), chip]

    def time_seen(chip, half):
        links.go(time_slot(chip, half), time_slot(chip, half), (sibling, c))

    def out_slot(chip, half):
        return w3.at[chip, :, pl.ds(1024 * half, 1024)]

    def out_own(k):
        return square.at[3, :, pl.ds(1024 * k, 1024)]

    def feed():
        square_load.wait()
        for j in range(3):
            square[j] = square_wide[j].astype(BF16)
        for p in rows:
            times.append(links.go(time_part(p), wt.at[lax.rem(p, 2), :, r, c], (p, c)))
        own_time = keep(time_part(r), wt.at[h, :, r, c], local_sem.at[0])
        for j in range(3, 7):
            square[j] = square_wide[j].astype(BF16)
        mlp_load.wait()
        mlp[...] = mlp_wide[...].astype(BF16)
        own_time.wait()
        yield

    def rest():
        local.extend(
            [
                keep(square.at[3], w3.at[c], local_sem.at[3]),
                keep(key_part(r), wk.at[c, r], local_sem.at[4]),
                keep(value_part(r), wv.at[c, r], local_sem.at[5]),
                keep(next_part(c), wn.at[r, c], local_sem.at[6]),
            ]
        )
        for p in rows:
            links.go(par, parg.at[r], (p, c))
        yield
        for p in rows:
            links.go(key_part(p), wk.at[c, r], (p, c))
        for p in cols:
            links.go(next_part(p), wn.at[r, c], (r, p))
        for p in rows:
            links.go(value_part(p), wv.at[c, r], (p, c))

    together(
        ring(
            links,
            "row",
            lambda chip, side: hx.at[2 * chip + side],
            own=hid_own,
            which=(h, 1 - h),
            ready=hid_ready,
        ),
        feed(),
        ring(links, "col", time_slot, ready=time_ready, seen=time_seen),
        rest(),
        ring(links, "col", out_slot, own=out_own),
    )
    links.finish()
    for copy in local:
        copy.wait()


def row_ring(links, source, target):
    return ring(
        links, "row", lambda chip, side: target.at[2 * chip + side], own=lambda k: source.at[k]
    )


def own_block(source, target, q, local_sem):
    return [keep(source.at[k], target.at[2 * q + k], local_sem.at[k]) for k in range(2)]


def att_kernel(att, w3, wk, attg, w3x, wkg, send_sem, recv_sem, local_sem):
    r, c, h, q, sibling = place()
    local = own_block(att, attg, q, local_sem)
    greet([(sibling, c)] + ring_peers("row") + ring_peers("col"))
    links = Links(send_sem, recv_sem)
    links.go(w3, w3x, (sibling, c))
    together(
        row_ring(links, att, attg),
        ring(
            links,
            "col",
            lambda chip, half: wkg.at[chip, pl.ds(8 * half, 8)],
            own=lambda k: wk.at[c, pl.ds(8 * k, 8)],
        ),
    )
    links.finish()
    for copy in local:
        copy.wait()


def mid_kernel(mid, wk, wkg, wv, midg, wvg, theirs, send_sem, recv_sem, local_sem):
    r, c, h, q, sibling = place()
    local = own_block(mid, midg, q, local_sem)
    greet([(sibling, c)] + ring_peers("row") + ring_peers("col"))
    links = Links(send_sem, recv_sem)

    def value_slot(chip, half):
        return wvg.at[chip, pl.ds(8 * half, 8)]

    def value_seen(chip, half):
        links.go(
            value_slot(chip, half), theirs.at[1, pl.ds(8 * half, 8), chip], (sibling, c)
        )

    def across():
        links.go(wk.at[c], theirs.at[0, :, c], (sibling, c))
        links.go(wv.at[c], theirs.at[1, :, c], (sibling, c))
        for d in range(1, N_COL):
            p = lax.rem(c + d, N_COL)
            links.go(wkg.at[p], theirs.at[0, :, p], (sibling, c))
        yield

    together(
        row_ring(links, mid, midg),
        ring(
            links,
            "col",
            value_slot,
            own=lambda k: wv.at[c, pl.ds(8 * k, 8)],
            seen=value_seen,
        ),
        across(),
    )
    links.finish()
    for copy in local:
        copy.wait()


def next_kernel(out, wn, got, wng, send_sem, recv_sem, local_sem):
    r, c, h, q, sibling = place()
    barrier = pltpu.get_barrier_semaphore()

    def target(i):
        return (2 * c + lax.rem(h + i, 2), q)

    peers = ring_peers("row") + ring_peers("col") + [(sibling, c)]

    @pl.when(q != c)
    def _():
        for i in range(2):
            pl.semaphore_signal(barrier, inc=1, device_id=target(i), device_id_type=MESH)

    for device in peers:
        pl.semaphore_signal(barrier, inc=1, device_id=device, device_id_type=MESH)
    pl.semaphore_wait(barrier, len(peers) + 2 * (q != c).astype(jnp.int32))

    def piece(i):
        return out.at[aligned(lax.rem(h + i, 2), MINE)]

    def move(i):
        return pltpu.make_async_remote_copy(
            src_ref=piece(i),
            dst_ref=got.at[2 * q + h],
            send_sem=send_sem.at[i],
            recv_sem=recv_sem.at[h],
            device_id=target(i),
            device_id_type=MESH,
        )

    @pl.when(q == c)
    def _():
        keep(piece(0), got.at[r], recv_sem.at[h])

    @pl.when(q != c)
    def _():
        move(0).start()

    move(1).start()
    local = keep(wn.at[r], wng.at[r], local_sem.at[0])
    links = Links(send_sem, recv_sem, 2)

    def out_ready(k):
        block = got.at[2 * c + k]
        pltpu.make_async_copy(block, block, recv_sem.at[k]).wait()

    def weight_slot(chip, half):
        return wng.at[2 * chip + h, pl.ds(4 * half, 4)]

    def weight_seen(chip, half):
        links.go(weight_slot(chip, half), weight_slot(chip, half), (sibling, c))

    def across():
        links.go(wn.at[r], wng.at[r], (sibling, c))
        yield

    together(
        ring(links, "col", lambda chip, side: got.at[2 * chip + side], ready=out_ready),
        across(),
        ring(
            links,
            "row",
            weight_slot,
            own=lambda k: wn.at[r, pl.ds(4 * k, 4)],
            seen=weight_seen,
        ),
    )
    links.finish()
    local.wait()

    @pl.when(q != c)
    def _():
        move(0).wait_send()

    move(1).wait_send()


def compute(kernel, outs, operands, scratch=(), grid=None, in_specs=None, out_specs=None, flops=0):
    return pl.pallas_call(
        kernel,
        grid=grid if grid is not None else (),
        out_shape=[jax.ShapeDtypeStruct(*out) for out in outs],
        in_specs=in_specs if in_specs is not None else [VMEM] * len(operands),
        out_specs=out_specs if out_specs is not None else [VMEM] * len(outs),
        scratch_shapes=list(scratch),
        compiler_params=pltpu.CompilerParams(vmem_limit_bytes=56 * 2**20),
        cost_estimate=pl.CostEstimate(flops=flops, bytes_accessed=16 * 2**20, transcendentals=0),
    )(*operands)


def dot(a, b, dims=((1,), (0,))):
    return lax.dot_general(a, b, (dims, ((), ())), preferred_element_type=F32)


def split(x):
    high = x.astype(BF16)
    return high, (x - high.astype(F32)).astype(BF16)


def dot3(a, b, dims=((1,), (0,))):
    a_high, a_low = a
    b_high, b_low = b
    return dot(a_high, b_high, dims) + (dot(a_high, b_low, dims) + dot(a_low, b_high, dims))


def norm(source, gain, bias):
    center = jnp.sum(source, axis=-1, keepdims=True) / WIDTH
    second = jnp.sum(source * source, axis=-1, keepdims=True) / WIDTH
    scaled = (source - center) * lax.rsqrt(second - center * center + 1e-05)
    return (scaled * gain + bias).astype(BF16).astype(F32)


def row_of(par, i):
    return jnp.concatenate([par[j, i : i + 1, :] for j in range(N_ROW)], axis=1)


def step_back(z):
    position = lax.rem(lax.broadcasted_iota(jnp.int32, z.shape, 0), LMAX)
    return jnp.where(position == 0, 0.0, pltpu.roll(z, 1, 0)) - z


TILE = 256


def blocks_of(ref, at):
    return jnp.concatenate(
        [ref[j, pl.ds(at, TILE), :].astype(F32) for j in range(ref.shape[0])], axis=1
    )


def mix_kernel(hx, par, shift, wt, down, rkv, low):
    @pl.loop(0, MINE // TILE)
    def _(m):
        at = pl.multiple_of(m * TILE, TILE)
        z = norm(blocks_of(hx, at), row_of(par, 0), row_of(par, 1))
        dz = step_back(z)
        for j in range(5):
            blend = (z + dz * shift[j : j + 1, :]).astype(BF16)
            if j < 3:
                weight = jnp.concatenate(
                    [wt[side, j].reshape(WIDTH, FEAT) for side in range(2)], axis=1
                )
                rkv[j, pl.ds(at, TILE), :] = dot(blend, weight)
            else:
                low[j - 3, pl.ds(at, TILE), :] = dot(blend, down[j - 3], ((1,), (1,)))


def core_kernel(lens, rkv, low, coef, up, att, final):
    r, c, h, q, _ = place()
    length = lens[c * 8 + h * 4 + pl.program_id(0)]
    wide = SLICE
    channels = aligned(q, SLICE)
    heads = wide // HEAD
    live = (lax.broadcasted_iota(jnp.int32, (LMAX, wide), 0) < length).astype(F32)
    lane = lax.broadcasted_iota(jnp.int32, (LMAX, wide), 1) // HEAD
    t = lax.broadcasted_iota(jnp.int32, (LMAX, LMAX), 0)
    u = lax.broadcasted_iota(jnp.int32, (LMAX, LMAX), 1)
    seg = (
        lax.broadcasted_iota(jnp.int32, (wide, wide), 0) // HEAD
        == lax.broadcasted_iota(jnp.int32, (wide, wide), 1) // HEAD
    ).astype(F32).astype(BF16)
    lower = (t >= u).astype(F32).astype(BF16)

    def head_sum(x):
        high, low_part = split(x)
        return dot(high, seg) + dot(low_part, seg)

    def only(x, k):
        return jnp.where(lane == k, x, jnp.zeros_like(x))

    receptance, key, value = rkv[0], rkv[1], rkv[2]
    decay = (
        -0.606531
        * jax.nn.sigmoid(coef[0:1, channels] + dot(jnp.tanh(low[0]).astype(BF16), up[0, :, channels]))
        * live
    )
    rate = jax.nn.sigmoid(coef[1:2, channels] + dot(low[1].astype(BF16), up[1, :, channels]))
    kappa = key * coef[2:3, channels]
    kappa = kappa * lax.rsqrt(head_sum(kappa * kappa) + 1e-05)
    remove = -kappa * live
    write = kappa * rate * live
    key = key * live
    value = value * live
    d_high, d_rest = split(decay)
    d_mid, d_low = split(decay - d_high.astype(F32))
    total = dot(lower, d_high) + (dot(lower, d_mid) + dot(lower, d_low))
    middle = total[LMAX // 2 - 1 : LMAX // 2, :]
    last = total[LMAX - 1 : LMAX, :]
    back = jnp.exp(middle - total)
    pull = split(remove * jnp.exp(total - decay - middle))
    read = split(receptance * jnp.exp(total - middle))
    write_back = split(write * back)
    key_back = split(key * back)
    value_parts = split(value)

    left = tuple(
        jnp.concatenate([x for k in range(heads) for x in (only(pull[i], k), only(read[i], k))])
        for i in range(2)
    )
    right = tuple(jnp.concatenate([write_back[i], key_back[i]]) for i in range(2))
    pairs = dot3(left, right, ((1,), (1,)))
    strict = t > u
    t2 = lax.broadcasted_iota(jnp.int32, (LMAX, 2 * LMAX), 0)
    u2 = lax.rem(lax.broadcasted_iota(jnp.int32, (LMAX, 2 * LMAX), 1), LMAX)
    upto = t2 >= u2
    solves, pull_key, reads = [], [], []
    for k in range(heads):
        base = k * 2 * LMAX
        system = jnp.where(strict, pairs[base : base + LMAX, :LMAX], 0.0)
        pull_key.append(split(jnp.where(strict, pairs[base : base + LMAX, LMAX:], 0.0)))
        reads.append(split(jnp.where(upto, pairs[base + LMAX : base + 2 * LMAX], 0.0)))
        solves.append(system)
    inverse = []
    for k in range(heads):
        near = (t // 2 == u // 2)
        inverse.append(
            jnp.where(near, solves[k], 0.0) + (t == u).astype(F32)
        )
    size = 2
    while size < LMAX:
        inside = (t // (2 * size) == u // (2 * size)) & (t // size != u // size)
        grown = []
        for k in range(heads):
            known = split(inverse[k])
            cross = split(jnp.where(inside, solves[k], 0.0))
            product = split(dot3(known, cross))
            grown.append(inverse[k] + dot3(product, known))
        inverse = grown
        size *= 2

    def across(mats, parts):
        wide_left = tuple(jnp.concatenate([mat[i] for mat in mats], axis=1) for i in range(2))
        tall = tuple(
            jnp.concatenate([only(part[i], k) for k in range(heads) for part in parts])
            for i in range(2)
        )
        return dot3(wide_left, tall)

    start = across(pull_key, [value_parts])
    pulled = split(across([split(x) for x in inverse], [split(start)]))
    output = across(reads, [pulled, value_parts])
    tail = jnp.exp(last - total)
    write_tail = split(write * tail)
    key_tail = split(key * tail)
    tall = tuple(jnp.concatenate([pulled[i], value_parts[i]]) for i in range(2))
    tails = tuple(jnp.concatenate([write_tail[i], key_tail[i]]) for i in range(2))
    state = dot3(tall, tails, ((0,), (0,)))
    even = lax.broadcasted_iota(jnp.int32, (HEAD, FEAT), 1) < HEAD
    for k in range(heads // 2):
        lanes = slice(k * FEAT, (k + 1) * FEAT)
        final[0, k] = jnp.where(
            even,
            state[k * FEAT : k * FEAT + HEAD, lanes],
            state[k * FEAT + HEAD : (k + 1) * FEAT, lanes],
        ).astype(BF16)
    bonus = head_sum(receptance * key * coef[3:4, channels])
    out = (output + bonus * value) * live
    center = head_sum(out) * (1.0 / HEAD)
    out = out - center
    spread = head_sum(out * out) * (1.0 / HEAD)
    out = (out * lax.rsqrt(spread + 0.00064) * coef[4:5, channels] + coef[5:6, channels]).astype(BF16)
    for side in range(2):
        att[side] = out[:, side * FEAT : (side + 1) * FEAT]


def project_kernel(attg, own, w3, w3x, mid):
    r = lax.axis_index("row")
    h = lax.rem(r, 2)

    @pl.loop(0, MINE // TILE)
    def _(m):
        rows = pl.ds(pl.multiple_of(m * TILE, TILE), TILE)
        wide = jnp.concatenate([attg[j, rows, :] for j in range(N_ROW)], axis=1)
        weight = jnp.concatenate([w[...].reshape(FEAT, WIDTH) for w in (w3, w3x)])
        total = dot(wide, weight, ((1,), (1,)))
        for k, side in enumerate((h, 1 - h)):
            mid[side, rows, :] = (
                own[r - h + side, rows, :].astype(F32) + total[:, k * FEAT : (k + 1) * FEAT]
            ).astype(BF16)


STEP = 128


def mlp_kernel(
    midg,
    par,
    shift,
    wk,
    wkg,
    wv,
    wvg,
    theirs,
    own,
    out,
    send_sem,
    recv_sem,
    local_sem,
    held,
    act_scr,
    part,
    got,
):
    r, c, h, q, sibling = place()
    copies = []
    for m, (near, far) in enumerate(((wk, wkg), (wv, wvg))):
        copies.append(keep(near.at[c], held.at[m, :, c], local_sem.at[8 * m]))
        for d in range(1, N_COL):
            p = lax.rem(c + d, N_COL)
            copies.append(keep(far.at[p], held.at[m, :, p], local_sem.at[8 * m + d]))
    rows = [lax.rem(r + d, N_ROW) for d in range(1, N_ROW)]
    greet([(p, c) for p in rows])
    for copy in copies:
        copy.wait()

    def moves(m):
        tokens = pl.ds(pl.multiple_of(m * STEP, STEP), STEP)
        return [
            pltpu.make_async_remote_copy(
                src_ref=part.at[p, tokens],
                dst_ref=got.at[r, tokens],
                send_sem=send_sem.at[m * (N_ROW - 1) + i],
                recv_sem=recv_sem.at[m * (N_ROW - 1) + i],
                device_id=(p, c),
                device_id_type=MESH,
            )
            for i, p in enumerate(rows)
        ]

    @pl.loop(0, MINE // STEP)
    def _(m):
        tokens = pl.ds(pl.multiple_of(m * STEP, STEP), STEP)
        z = norm(
            jnp.concatenate([midg[j, tokens, :].astype(F32) for j in range(N_ROW)], axis=1),
            row_of(par, 2),
            row_of(par, 3),
        )
        blend = (z + step_back(z) * shift[5:6, :]).astype(BF16)
        for side, weights in enumerate((held, theirs)):
            act = jnp.square(jnp.maximum(dot(blend, weights[0].reshape(WIDTH, MINE)), 0.0))
            act_scr[side] = act.astype(BF16)

        @pl.loop(0, N_CHIP)
        def _(n):
            total = None
            for side, weights in enumerate((held, theirs)):
                weight = weights[1, pl.ds(2 * n, 2)].reshape(SLICE, MINE)
                term = dot(act_scr[side], weight, ((1,), (1,)))
                total = term if total is None else total + term
            for side in range(2):
                added = jnp.where(n == q, own[side, tokens, :].astype(F32), 0.0)
                part[2 * n + side, tokens, :] = (
                    total[:, side * FEAT : (side + 1) * FEAT] + added
                ).astype(BF16)

        for copy in moves(m):
            copy.start()
        got[r, tokens, :] = part[r, tokens, :]

    @pl.loop(0, MINE // STEP)
    def _(m):
        for copy in moves(m):
            copy.wait()

    for side in range(2):
        total = got[side].astype(F32)
        for k in range(1, N_CHIP):
            total += got[2 * k + side].astype(F32)
        out[pl.ds(side * MINE, MINE), :] = total.astype(BF16)


def last_kernel(nx, par, shift, weight, out):
    @pl.loop(0, MINE // TILE)
    def _(m):
        at = pl.multiple_of(m * TILE, TILE)
        z = norm(blocks_of(nx, at), row_of(par, 4), row_of(par, 5))
        dz = step_back(z)
        for j in range(3):
            blend = (z + dz * shift[6 + j : 7 + j, :]).astype(BF16)
            out[j, pl.ds(at, TILE), :] = dot(
                blend, weight[:, :, j].reshape(WIDTH, SLICE)
            ).astype(BF16)


def time_core(lens, rkv, low, coef, up):
    prompts = rkv.shape[1] // LMAX
    return compute(
        core_kernel,
        [((2, prompts * LMAX, FEAT), BF16), ((prompts, 2, HEAD, FEAT), BF16)],
        (lens, rkv, low, coef, up),
        grid=(prompts,),
        in_specs=[
            pl.BlockSpec(memory_space=pltpu.SMEM),
            pl.BlockSpec((3, LMAX, SLICE), lambda p: (0, p, 0)),
            pl.BlockSpec((2, LMAX, low.shape[2]), lambda p: (0, p, 0)),
            pl.BlockSpec(coef.shape, lambda p: (0, 0)),
            pl.BlockSpec(up.shape, lambda p: (0, 0, 0)),
        ],
        out_specs=[
            pl.BlockSpec((2, LMAX, FEAT), lambda p: (0, p, 0)),
            pl.BlockSpec((1, 2, HEAD, FEAT), lambda p: (p, 0, 0, 0)),
        ],
        flops=4 * 10**9,
    )


def per_device(
    hidden,
    lengths,
    square_matrix_shards,
    channel_mix_shards,
    lowrank_down,
    lowrank_up,
    token_shift_weights,
    attention_coefficients,
    norm_parameters,
):
    hx, wt, w3, wk, wv, wn, parg = exchange(
        start_kernel,
        [
            ((N_ROW, MINE, FEAT), BF16),
            ((2, 3, N_ROW, N_COL, 16, FEAT), BF16),
            ((N_COL, 16, WIDTH), BF16),
            ((N_COL, N_ROW, 16, MINE), BF16),
            ((N_COL, N_ROW, 16, MINE), BF16),
            ((N_ROW, N_COL, 3, 16, SLICE), BF16),
            ((N_ROW, 6, FEAT), F32),
        ],
        15 + 1 + 3 * RING + 1 + 14 + 15 + 15 + 7 + 15,
        9,
        1,
        square_matrix_shards,
        channel_mix_shards,
        norm_parameters,
        hidden,
        scratch=[
            pltpu.VMEM(square_matrix_shards.shape, F32),
            pltpu.VMEM(channel_mix_shards.shape, F32),
            pltpu.VMEM(square_matrix_shards.shape, BF16),
            pltpu.VMEM(channel_mix_shards.shape, BF16),
        ],
    )
    rkv, low = compute(
        mix_kernel,
        [((3, MINE, SLICE), F32), ((2, MINE, lowrank_down.shape[2]), F32)],
        (hx, parg, token_shift_weights, wt, lowrank_down.transpose(0, 2, 1)),
        flops=4 * 10**9,
    )
    att, final = time_core(
        lengths, rkv, low, attention_coefficients, lowrank_up
    )
    attg, w3x, wkg = exchange(
        att_kernel,
        [
            ((N_ROW, MINE, FEAT), BF16),
            ((N_COL, 16, WIDTH), BF16),
            ((N_COL, N_ROW, 16, MINE), BF16),
        ],
        1 + 2 * RING,
        2,
        2,
        att,
        w3,
        wk,
    )
    moves = [
        ((2 * a + b) * N_COL + d, (2 * d + b) * N_COL + a)
        for a in range(N_CHIP)
        for b in range(2)
        for d in range(N_COL)
    ]
    (mid,) = compute(
        project_kernel,
        [((2, MINE, FEAT), BF16)],
        (attg, hx, w3, w3x),
        flops=10**9,
    )
    midg, wvg, theirs = exchange(
        mid_kernel,
        [
            ((N_ROW, MINE, FEAT), BF16),
            ((N_COL, N_ROW, 16, MINE), BF16),
            ((2, N_ROW, N_COL, 16, MINE), BF16),
        ],
        9 + 14 + 2 * RING,
        2,
        3,
        mid,
        wk,
        wkg,
        wv,
    )
    final, midg = lax.optimization_barrier((final, midg))
    final = lax.ppermute(final, ("row", "col"), moves)
    final = final.reshape(4, 2, HEAD, 2, HEAD).transpose(0, 1, 3, 2, 4).astype(F32)
    final_state = final.reshape(4, 4, HEAD * HEAD)
    (out_hidden,) = exchange(
        mlp_kernel,
        [((2 * MINE, FEAT), BF16)],
        15 * MINE // STEP,
        16,
        4,
        midg,
        parg,
        token_shift_weights,
        wk,
        wkg,
        wv,
        wvg,
        theirs,
        mid,
        scratch=[
            pltpu.VMEM((2, N_ROW, N_COL, 16, MINE), BF16),
            pltpu.VMEM((2, STEP, MINE), BF16),
            pltpu.VMEM((N_ROW, MINE, FEAT), BF16),
            pltpu.VMEM((N_ROW, MINE, FEAT), BF16),
        ],
        in_specs=[VMEM] * 3 + [ANY] * 4 + [VMEM] * 2,
        out_specs=[VMEM],
    )
    nx, weight_next = exchange(
        next_kernel,
        [((N_ROW, MINE, FEAT), BF16), ((N_ROW, N_COL, 3, 16, SLICE), BF16)],
        2 + 1 + 14 + 2 * RING,
        1,
        5,
        out_hidden,
        wn,
    )
    (next_rkv,) = compute(
        last_kernel,
        [((3, MINE, SLICE), BF16)],
        (nx, parg, token_shift_weights, weight_next),
        flops=2 * 10**9,
    )
    return (out_hidden, next_rkv, final_state)


def solution(mesh):
    return jax.shard_map(
        per_device,
        mesh=mesh,
        in_specs=(
            P("col", "row"),
            P(),
            P(None, ("row", "col"), None),
            P(None, ("row", "col"), None),
            P(),
            P(),
            P(),
            P(),
            P(None, "row"),
        ),
        out_specs=(P("col", "row"), P(None, "row", "col"), P("row", "col", None)),
        check_vma=False,
    )
```

```python
import functools

import jax
import jax.numpy as jnp
from jax import lax
from jax.experimental import pallas as pl
from jax.experimental.pallas import tpu as pltpu
from jax.sharding import PartitionSpec as P

WIDTH = 2048
HEAD = 64
LMAX = 128
F32 = jnp.float32
BF16 = jnp.bfloat16
MESH = pl.DeviceIdType.MESH
ANY = pl.BlockSpec(memory_space=pl.ANY)
VMEM = pl.BlockSpec(memory_space=pltpu.VMEM)
N_ROW = 16
N_COL = 8
N_CHIP = 8
MINE = 512
FEAT = 128
SLICE = 256


def greet(devices):
    barrier = pltpu.get_barrier_semaphore()
    for device in devices:
        pl.semaphore_signal(barrier, inc=1, device_id=device, device_id_type=MESH)
    pl.semaphore_wait(barrier, len(devices))


class Copy:
    def __init__(self, source, target, send_sem, recv_sem, slot, device):
        self.made = lambda: pltpu.make_async_remote_copy(
            src_ref=source() if callable(source) else source,
            dst_ref=target() if callable(target) else target,
            send_sem=send_sem.at[slot],
            recv_sem=recv_sem.at[slot],
            device_id=device,
            device_id_type=MESH,
        )

    def start(self):
        self.made().start()

    def wait_recv(self):
        self.made().wait_recv()

    def wait_send(self):
        self.made().wait_send()


def keep(source, target, sem):
    copy = pltpu.make_async_copy(source, target, sem)
    copy.start()
    return copy


def exchange(
    kernel,
    outs,
    n_remote,
    n_local,
    collective_id,
    *operands,
    scratch=(),
    in_specs=None,
    out_specs=None,
):
    return pl.pallas_call(
        kernel,
        out_shape=[jax.ShapeDtypeStruct(*out) for out in outs],
        in_specs=in_specs or [ANY] * len(operands),
        out_specs=out_specs or [ANY] * len(outs),
        scratch_shapes=[
            pltpu.SemaphoreType.DMA((n_remote,)),
            pltpu.SemaphoreType.DMA((n_remote,)),
            pltpu.SemaphoreType.DMA((n_local,)),
            *scratch,
        ],
        compiler_params=pltpu.CompilerParams(
            collective_id=collective_id, has_side_effects=True, vmem_limit_bytes=56 * 2**20
        ),
        cost_estimate=pl.CostEstimate(flops=0, bytes_accessed=48 * 2**20, transcendentals=0),
    )(*operands)


def place():
    r = lax.axis_index("row")
    c = lax.axis_index("col")
    h = lax.rem(r, 2)
    return r, c, h, lax.div(r, 2), r + 1 - 2 * h


class Links:
    def __init__(self, send_sem, recv_sem, first=0):
        self.send_sem = send_sem
        self.recv_sem = recv_sem
        self.slot = first
        self.copies = []
        self.open = []

    def go(self, source, target, device):
        copy = Copy(source, target, self.send_sem, self.recv_sem, self.slot, device)
        copy.start()
        self.slot += 1
        self.copies.append(copy)
        self.open.append(copy)
        return copy

    def arrive(self, copy):
        copy.wait_recv()
        self.open = [other for other in self.open if other is not copy]

    def finish(self):
        for copy in self.open:
            copy.wait_recv()
        for copy in self.copies:
            copy.wait_send()


RING = 14


def ring_at(axis):
    r, c, h, q, _ = place()
    here = q if axis == "row" else c
    step_z = 1 - 2 * lax.rem(here, 2)
    chips = {
        "p": lax.rem(here + 2, 8),
        "m": lax.rem(here + 6, 8),
        "z": here + step_z,
        "o": lax.rem(here + 4, 8),
        "pz": lax.rem(here + 2, 8) + step_z,
        "mz": lax.rem(here + 6, 8) + step_z,
        "oz": lax.rem(here + 4, 8) + step_z,
    }
    devices = {
        side: (2 * chips[side] + h, c) if axis == "row" else (r, chips[side]) for side in "pmz"
    }
    return here, chips, devices


def ring_peers(axis):
    return list(ring_at(axis)[2].values())


def ring(links, axis, slot, own=None, which=(0, 1), ready=None, seen=None):
    here, chips, to = ring_at(axis)
    heavy = axis == "row"
    seen = seen or (lambda chip, half: None)

    def take(copy, chip, half):
        links.arrive(copy)
        seen(chip, half)

    def forward(chip, half, side):
        return links.go(lambda: slot(chip, half), lambda: slot(chip, half), to[side])

    first = {}
    for k in range(2):
        if ready is not None:
            ready(k)
        target = functools.partial(slot, here, which[k])
        source = functools.partial(own, k) if own is not None else target
        for side in "pmz":
            first[side, k] = links.go(source, target, to[side])
    yield
    for k in range(2):
        take(first["p", k], chips["m"], which[k])
    low = forward(chips["m"], 0, "p")
    for k in range(2):
        take(first["m", k], chips["p"], which[k])
    high = forward(chips["p"], 1, "m")
    yield
    beside = {}
    for k in range(2):
        take(first["z", k], chips["z"], which[k])
        for side in "pm":
            beside[side, k] = forward(chips["z"], which[k], side)
    yield
    if heavy:
        take(low, chips["o"], 0)
        low = forward(chips["o"], 0, "z")
        take(high, chips["o"], 1)
        high = forward(chips["o"], 1, "z")
        yield
        for k in range(2):
            take(beside["p", k], chips["mz"], which[k])
            take(beside["m", k], chips["pz"], which[k])
    else:
        take(low, chips["o"], 0)
        take(high, chips["o"], 1)
        for k in range(2):
            take(beside["p", k], chips["mz"], which[k])
        low = forward(chips["mz"], 0, "p")
        for k in range(2):
            take(beside["m", k], chips["pz"], which[k])
        high = forward(chips["pz"], 1, "m")
        yield
    take(low, chips["oz"], 0)
    take(high, chips["oz"], 1)


def together(*steps):
    active = list(steps)
    while active:
        for step in list(active):
            if next(step, StopIteration) is StopIteration:
                active.remove(step)


def aligned(index, size):
    return pl.ds(pl.multiple_of(index * size, size), size)


def start_kernel(
    square_in,
    mlp_in,
    par,
    hid,
    hx,
    wt,
    w3,
    wk,
    wv,
    wn,
    parg,
    send_sem,
    recv_sem,
    local_sem,
    square_wide,
    mlp_wide,
    square,
    mlp,
):
    r, c, h, q, sibling = place()
    rows = [lax.rem(r + d, N_ROW) for d in range(1, N_ROW)]
    cols = [lax.rem(c + d, N_COL) for d in range(1, N_COL)]

    def time_part(p):
        return square.at[pl.ds(0, 3), :, aligned(p, FEAT)]

    def key_part(p):
        return mlp.at[0, :, aligned(p, MINE)]

    def value_part(p):
        return mlp.at[1, :, aligned(p, MINE)]

    def next_part(p):
        return square.at[pl.ds(4, 3), :, aligned(p, SLICE)]

    mine = hid.at[aligned(h, MINE)]
    square_load = keep(square_in, square_wide, local_sem.at[7])
    mlp_load = keep(mlp_in, mlp_wide, local_sem.at[8])
    local = [
        keep(par, parg.at[r], local_sem.at[1]),
        keep(mine, hx.at[r], local_sem.at[2]),
    ]
    greet([(p, c) for p in rows] + [(r, p) for p in cols])
    links = Links(send_sem, recv_sem)
    times = []
    other = links.go(hid.at[aligned(1 - h, MINE)], hx.at[r], (sibling, c))

    def hid_own(k):
        return (mine, hx.at[sibling])[k]

    def hid_ready(k):
        if k == 1:
            links.arrive(other)

    def time_ready(k):
        if k == 0:
            for copy in times:
                links.arrive(copy)
            links.go(wt.at[h, :, :, c], wt.at[h, :, :, c], (sibling, c))

    def time_slot(chip, half):
        return wt.at[h, :, pl.ds(8 * half, 8), chip]

    def time_seen(chip, half):
        links.go(time_slot(chip, half), time_slot(chip, half), (sibling, c))

    def out_slot(chip, half):
        return w3.at[chip, :, pl.ds(1024 * half, 1024)]

    def out_own(k):
        return square.at[3, :, pl.ds(1024 * k, 1024)]

    def feed():
        square_load.wait()
        for j in range(3):
            square[j] = square_wide[j].astype(BF16)
        for p in rows:
            times.append(links.go(time_part(p), wt.at[lax.rem(p, 2), :, r, c], (p, c)))
        own_time = keep(time_part(r), wt.at[h, :, r, c], local_sem.at[0])
        for j in range(3, 7):
            square[j] = square_wide[j].astype(BF16)
        mlp_load.wait()
        mlp[...] = mlp_wide[...].astype(BF16)
        own_time.wait()
        yield

    def rest():
        local.extend(
            [
                keep(square.at[3], w3.at[c], local_sem.at[3]),
                keep(key_part(r), wk.at[c, r], local_sem.at[4]),
                keep(value_part(r), wv.at[c, r], local_sem.at[5]),
                keep(next_part(c), wn.at[r, c], local_sem.at[6]),
            ]
        )
        for p in rows:
            links.go(par, parg.at[r], (p, c))
        yield
        for p in rows:
            links.go(key_part(p), wk.at[c, r], (p, c))
        for p in cols:
            links.go(next_part(p), wn.at[r, c], (r, p))
        for p in rows:
            links.go(value_part(p), wv.at[c, r], (p, c))

    together(
        ring(
            links,
            "row",
            lambda chip, side: hx.at[2 * chip + side],
            own=hid_own,
            which=(h, 1 - h),
            ready=hid_ready,
        ),
        feed(),
        ring(links, "col", time_slot, ready=time_ready, seen=time_seen),
        rest(),
        ring(links, "col", out_slot, own=out_own),
    )
    links.finish()
    for copy in local:
        copy.wait()


def row_ring(links, source, target):
    return ring(
        links, "row", lambda chip, side: target.at[2 * chip + side], own=lambda k: source.at[k]
    )


def own_block(source, target, q, local_sem):
    return [keep(source.at[k], target.at[2 * q + k], local_sem.at[k]) for k in range(2)]


def mid_kernel(mid, wk, wkg, wv, midg, wvg, theirs, send_sem, recv_sem, local_sem):
    r, c, h, q, sibling = place()
    local = own_block(mid, midg, q, local_sem)
    greet([(sibling, c)] + ring_peers("row") + ring_peers("col"))
    links = Links(send_sem, recv_sem)

    def value_slot(chip, half):
        return wvg.at[chip, pl.ds(8 * half, 8)]

    def value_seen(chip, half):
        links.go(
            value_slot(chip, half), theirs.at[1, pl.ds(8 * half, 8), chip], (sibling, c)
        )

    def across():
        links.go(wk.at[c], theirs.at[0, :, c], (sibling, c))
        links.go(wv.at[c], theirs.at[1, :, c], (sibling, c))
        for d in range(1, N_COL):
            p = lax.rem(c + d, N_COL)
            links.go(wkg.at[p], theirs.at[0, :, p], (sibling, c))
        yield

    together(
        row_ring(links, mid, midg),
        ring(
            links,
            "col",
            value_slot,
            own=lambda k: wv.at[c, pl.ds(8 * k, 8)],
            seen=value_seen,
        ),
        across(),
    )
    links.finish()
    for copy in local:
        copy.wait()


def next_kernel(out, wn, got, wng, send_sem, recv_sem, local_sem):
    r, c, h, q, sibling = place()
    barrier = pltpu.get_barrier_semaphore()

    def target(i):
        return (2 * c + lax.rem(h + i, 2), q)

    peers = ring_peers("row") + ring_peers("col") + [(sibling, c)]

    @pl.when(q != c)
    def _():
        for i in range(2):
            pl.semaphore_signal(barrier, inc=1, device_id=target(i), device_id_type=MESH)

    for device in peers:
        pl.semaphore_signal(barrier, inc=1, device_id=device, device_id_type=MESH)
    pl.semaphore_wait(barrier, len(peers) + 2 * (q != c).astype(jnp.int32))

    def piece(i):
        return out.at[aligned(lax.rem(h + i, 2), MINE)]

    def move(i):
        return pltpu.make_async_remote_copy(
            src_ref=piece(i),
            dst_ref=got.at[2 * q + h],
            send_sem=send_sem.at[i],
            recv_sem=recv_sem.at[h],
            device_id=target(i),
            device_id_type=MESH,
        )

    @pl.when(q == c)
    def _():
        keep(piece(0), got.at[r], recv_sem.at[h])

    @pl.when(q != c)
    def _():
        move(0).start()

    move(1).start()
    local = keep(wn.at[r], wng.at[r], local_sem.at[0])
    links = Links(send_sem, recv_sem, 2)

    def out_ready(k):
        block = got.at[2 * c + k]
        pltpu.make_async_copy(block, block, recv_sem.at[k]).wait()

    def weight_slot(chip, half):
        return wng.at[2 * chip + h, pl.ds(4 * half, 4)]

    def weight_seen(chip, half):
        links.go(weight_slot(chip, half), weight_slot(chip, half), (sibling, c))

    def across():
        links.go(wn.at[r], wng.at[r], (sibling, c))
        yield

    together(
        ring(links, "col", lambda chip, side: got.at[2 * chip + side], ready=out_ready),
        across(),
        ring(
            links,
            "row",
            weight_slot,
            own=lambda k: wn.at[r, pl.ds(4 * k, 4)],
            seen=weight_seen,
        ),
    )
    links.finish()
    local.wait()

    @pl.when(q != c)
    def _():
        move(0).wait_send()

    move(1).wait_send()


def compute(kernel, outs, operands, scratch=(), grid=None, in_specs=None, out_specs=None, flops=0):
    return pl.pallas_call(
        kernel,
        grid=grid if grid is not None else (),
        out_shape=[jax.ShapeDtypeStruct(*out) for out in outs],
        in_specs=in_specs if in_specs is not None else [VMEM] * len(operands),
        out_specs=out_specs if out_specs is not None else [VMEM] * len(outs),
        scratch_shapes=list(scratch),
        compiler_params=pltpu.CompilerParams(vmem_limit_bytes=56 * 2**20),
        cost_estimate=pl.CostEstimate(flops=flops, bytes_accessed=16 * 2**20, transcendentals=0),
    )(*operands)


def dot(a, b, dims=((1,), (0,))):
    return lax.dot_general(a, b, (dims, ((), ())), preferred_element_type=F32)


def split(x):
    high = x.astype(BF16)
    return high, (x - high.astype(F32)).astype(BF16)


def dot3(a, b, dims=((1,), (0,))):
    a_high, a_low = a
    b_high, b_low = b
    return dot(a_high, b_high, dims) + (dot(a_high, b_low, dims) + dot(a_low, b_high, dims))


def norm(source, gain, bias):
    center = jnp.sum(source, axis=-1, keepdims=True) / WIDTH
    second = jnp.sum(source * source, axis=-1, keepdims=True) / WIDTH
    scaled = (source - center) * lax.rsqrt(second - center * center + 1e-05)
    return (scaled * gain + bias).astype(BF16).astype(F32)


def row_of(par, i):
    return jnp.concatenate([par[j, i : i + 1, :] for j in range(N_ROW)], axis=1)


def step_back(z):
    position = lax.rem(lax.broadcasted_iota(jnp.int32, z.shape, 0), LMAX)
    return jnp.where(position == 0, 0.0, pltpu.roll(z, 1, 0)) - z


TILE = 256


def blocks_of(ref, at):
    return jnp.concatenate(
        [ref[j, pl.ds(at, TILE), :].astype(F32) for j in range(ref.shape[0])], axis=1
    )


def mix_kernel(hx, par, shift, wt, down, rkv, low):
    @pl.loop(0, MINE // TILE)
    def _(m):
        at = pl.multiple_of(m * TILE, TILE)
        z = norm(blocks_of(hx, at), row_of(par, 0), row_of(par, 1))
        dz = step_back(z)
        for j in range(5):
            blend = (z + dz * shift[j : j + 1, :]).astype(BF16)
            if j < 3:
                weight = jnp.concatenate(
                    [wt[side, j].reshape(WIDTH, FEAT) for side in range(2)], axis=1
                )
                rkv[j, pl.ds(at, TILE), :] = dot(blend, weight)
            else:
                low[j - 3, pl.ds(at, TILE), :] = dot(blend, down[j - 3], ((1,), (1,)))


def one_prompt(prompt, lens, rkv, low, coef, up, att, final):
    r, c, h, q, _ = place()
    length = lens[c * 8 + h * 4 + prompt]
    tokens = aligned(prompt, LMAX)
    wide = SLICE
    channels = aligned(q, SLICE)
    heads = wide // HEAD
    live = (lax.broadcasted_iota(jnp.int32, (LMAX, wide), 0) < length).astype(F32)
    lane = lax.broadcasted_iota(jnp.int32, (LMAX, wide), 1) // HEAD
    t = lax.broadcasted_iota(jnp.int32, (LMAX, LMAX), 0)
    u = lax.broadcasted_iota(jnp.int32, (LMAX, LMAX), 1)
    seg = (
        lax.broadcasted_iota(jnp.int32, (wide, wide), 0) // HEAD
        == lax.broadcasted_iota(jnp.int32, (wide, wide), 1) // HEAD
    ).astype(F32).astype(BF16)
    lower = (t >= u).astype(F32).astype(BF16)

    def head_sum(x):
        high, low_part = split(x)
        return dot(high, seg) + dot(low_part, seg)

    def only(x, k):
        return jnp.where(lane == k, x, jnp.zeros_like(x))

    receptance, key, value = rkv[0, tokens], rkv[1, tokens], rkv[2, tokens]
    decay = (
        -0.606531
        * jax.nn.sigmoid(coef[0:1, channels] + dot(jnp.tanh(low[0, tokens]).astype(BF16), up[0, :, channels]))
        * live
    )
    rate = jax.nn.sigmoid(coef[1:2, channels] + dot(low[1, tokens].astype(BF16), up[1, :, channels]))
    kappa = key * coef[2:3, channels]
    kappa = kappa * lax.rsqrt(head_sum(kappa * kappa) + 1e-05)
    remove = -kappa * live
    write = kappa * rate * live
    key = key * live
    value = value * live
    d_high, d_rest = split(decay)
    d_mid, d_low = split(decay - d_high.astype(F32))
    total = dot(lower, d_high) + (dot(lower, d_mid) + dot(lower, d_low))
    middle = total[LMAX // 2 - 1 : LMAX // 2, :]
    last = total[LMAX - 1 : LMAX, :]
    back = jnp.exp(middle - total)
    pull = split(remove * jnp.exp(total - decay - middle))
    read = split(receptance * jnp.exp(total - middle))
    write_back = split(write * back)
    key_back = split(key * back)
    value_parts = split(value)

    left = tuple(
        jnp.concatenate([x for k in range(heads) for x in (only(pull[i], k), only(read[i], k))])
        for i in range(2)
    )
    right = tuple(jnp.concatenate([write_back[i], key_back[i]]) for i in range(2))
    pairs = dot3(left, right, ((1,), (1,)))
    strict = t > u
    t2 = lax.broadcasted_iota(jnp.int32, (LMAX, 2 * LMAX), 0)
    u2 = lax.rem(lax.broadcasted_iota(jnp.int32, (LMAX, 2 * LMAX), 1), LMAX)
    upto = t2 >= u2
    solves, pull_key, reads = [], [], []
    for k in range(heads):
        base = k * 2 * LMAX
        system = jnp.where(strict, pairs[base : base + LMAX, :LMAX], 0.0)
        pull_key.append(split(jnp.where(strict, pairs[base : base + LMAX, LMAX:], 0.0)))
        reads.append(split(jnp.where(upto, pairs[base + LMAX : base + 2 * LMAX], 0.0)))
        solves.append(system)
    inverse = []
    for k in range(heads):
        near = (t // 2 == u // 2)
        inverse.append(
            jnp.where(near, solves[k], 0.0) + (t == u).astype(F32)
        )
    size = 2
    while size < LMAX:
        inside = (t // (2 * size) == u // (2 * size)) & (t // size != u // size)
        grown = []
        for k in range(heads):
            known = split(inverse[k])
            cross = split(jnp.where(inside, solves[k], 0.0))
            product = split(dot3(known, cross))
            grown.append(inverse[k] + dot3(product, known))
        inverse = grown
        size *= 2

    def across(mats, parts):
        wide_left = tuple(jnp.concatenate([mat[i] for mat in mats], axis=1) for i in range(2))
        tall = tuple(
            jnp.concatenate([only(part[i], k) for k in range(heads) for part in parts])
            for i in range(2)
        )
        return dot3(wide_left, tall)

    start = across(pull_key, [value_parts])
    pulled = split(across([split(x) for x in inverse], [split(start)]))
    output = across(reads, [pulled, value_parts])
    tail = jnp.exp(last - total)
    write_tail = split(write * tail)
    key_tail = split(key * tail)
    tall = tuple(jnp.concatenate([pulled[i], value_parts[i]]) for i in range(2))
    tails = tuple(jnp.concatenate([write_tail[i], key_tail[i]]) for i in range(2))
    state = dot3(tall, tails, ((0,), (0,)))
    even = lax.broadcasted_iota(jnp.int32, (HEAD, FEAT), 1) < HEAD
    for k in range(heads // 2):
        lanes = slice(k * FEAT, (k + 1) * FEAT)
        final[prompt, k] = jnp.where(
            even,
            state[k * FEAT : k * FEAT + HEAD, lanes],
            state[k * FEAT + HEAD : (k + 1) * FEAT, lanes],
        ).astype(BF16)
    bonus = head_sum(receptance * key * coef[3:4, channels])
    out = (output + bonus * value) * live
    center = head_sum(out) * (1.0 / HEAD)
    out = out - center
    spread = head_sum(out * out) * (1.0 / HEAD)
    out = (out * lax.rsqrt(spread + 0.00064) * coef[4:5, channels] + coef[5:6, channels]).astype(BF16)
    for side in range(2):
        att[side, tokens] = out[:, side * FEAT : (side + 1) * FEAT]


PROMPTS = MINE // LMAX
HOPS = 9


def attend_kernel(
    lens,
    rkv,
    low,
    coef,
    up,
    own,
    w3,
    wk,
    mid,
    final,
    wkg,
    send_sem,
    recv_sem,
    local_sem,
    att,
    attg,
    w3x,
):
    r, c, h, q, sibling = place()
    _, chips, to = ring_at("row")
    greet([(sibling, c)] + ring_peers("row") + ring_peers("col"))
    links = Links(send_sem, recv_sem, PROMPTS * HOPS)
    links.go(w3, w3x, (sibling, c))
    near = keep(own.at[pl.ds(pl.multiple_of(r - h, 2), 2)], attg.at[pl.ds(N_ROW, 2)], local_sem.at[0])
    keys = ring(
        links,
        "col",
        lambda chip, half: wkg.at[chip, pl.ds(8 * half, 8)],
        own=lambda k: wk.at[c, pl.ds(8 * k, 8)],
    )
    next(keys)

    def hop(prompt, slot, chip, side, half=None):
        def block():
            tokens = aligned(prompt, LMAX)
            if half is None:
                return attg.at[pl.ds(2 * chips.get(chip, q), 2), tokens]
            return attg.at[2 * chips[chip] + half, tokens]

        def source():
            return att.at[:, aligned(prompt, LMAX)] if chip == "own" else block()

        return Copy(source, block, send_sem, recv_sem, prompt * HOPS + slot, to[side])

    def hops(prompt):
        return [
            hop(prompt, 0, "own", "p"),
            hop(prompt, 1, "own", "m"),
            hop(prompt, 2, "own", "z"),
            hop(prompt, 3, "m", "p", 0),
            hop(prompt, 4, "p", "m", 1),
            hop(prompt, 5, "z", "p"),
            hop(prompt, 6, "z", "m"),
            hop(prompt, 7, "o", "z", 0),
            hop(prompt, 8, "o", "z", 1),
        ]

    @pl.loop(0, PROMPTS + 2)
    def _(step):
        @pl.when(step < PROMPTS)
        def _():
            one_prompt(step, lens, rkv, low, coef, up, att, final)
            copies = hops(step)
            for k in range(3):
                copies[k].start()
            tokens = aligned(step, LMAX)
            for side in range(2):
                attg[2 * q + side, tokens] = att[side, tokens]

        @pl.when((step >= 1) & (step <= PROMPTS))
        def _():
            copies = hops(step - 1)
            copies[0].wait_recv()
            copies[3].start()
            copies[1].wait_recv()
            copies[4].start()
            copies[2].wait_recv()
            copies[5].start()
            copies[6].start()

        @pl.when(step >= 2)
        def _():
            copies = hops(step - 2)
            copies[3].wait_recv()
            copies[7].start()
            copies[4].wait_recv()
            copies[8].start()

        @pl.when(step == 1)
        def _():
            next(keys)

        @pl.when(step == 2)
        def _():
            next(keys)

        @pl.when(step == 3)
        def _():
            next(keys)

    @pl.loop(0, PROMPTS)
    def _(prompt):
        copies = hops(prompt)
        for k in (5, 6, 7, 8):
            copies[k].wait_recv()
        for copy in copies:
            copy.wait_send()

    together(keys)
    links.finish()
    near.wait()

    @pl.loop(0, MINE // TILE)
    def _(m):
        rows = aligned(m, TILE)
        wide = jnp.concatenate([attg[j, rows, :] for j in range(N_ROW)], axis=1)
        weight = jnp.concatenate([w[...].reshape(FEAT, WIDTH) for w in (w3, w3x)])
        total = dot(wide, weight, ((1,), (1,)))
        for k, side in enumerate((h, 1 - h)):
            mid[side, rows, :] = (
                attg[N_ROW + side, rows, :].astype(F32) + total[:, k * FEAT : (k + 1) * FEAT]
            ).astype(BF16)


STEP = 128


def mlp_kernel(
    midg,
    par,
    shift,
    wk,
    wkg,
    wv,
    wvg,
    theirs,
    own,
    out,
    send_sem,
    recv_sem,
    local_sem,
    held,
    act_scr,
    part,
    got,
):
    r, c, h, q, sibling = place()
    copies = []
    for m, (near, far) in enumerate(((wk, wkg), (wv, wvg))):
        copies.append(keep(near.at[c], held.at[m, :, c], local_sem.at[8 * m]))
        for d in range(1, N_COL):
            p = lax.rem(c + d, N_COL)
            copies.append(keep(far.at[p], held.at[m, :, p], local_sem.at[8 * m + d]))
    rows = [lax.rem(r + d, N_ROW) for d in range(1, N_ROW)]
    greet([(p, c) for p in rows])
    for copy in copies:
        copy.wait()

    def moves(m):
        tokens = pl.ds(pl.multiple_of(m * STEP, STEP), STEP)
        return [
            pltpu.make_async_remote_copy(
                src_ref=part.at[p, tokens],
                dst_ref=got.at[r, tokens],
                send_sem=send_sem.at[m * (N_ROW - 1) + i],
                recv_sem=recv_sem.at[m * (N_ROW - 1) + i],
                device_id=(p, c),
                device_id_type=MESH,
            )
            for i, p in enumerate(rows)
        ]

    @pl.loop(0, MINE // STEP)
    def _(m):
        tokens = pl.ds(pl.multiple_of(m * STEP, STEP), STEP)
        z = norm(
            jnp.concatenate([midg[j, tokens, :].astype(F32) for j in range(N_ROW)], axis=1),
            row_of(par, 2),
            row_of(par, 3),
        )
        blend = (z + step_back(z) * shift[5:6, :]).astype(BF16)
        for side, weights in enumerate((held, theirs)):
            act = jnp.square(jnp.maximum(dot(blend, weights[0].reshape(WIDTH, MINE)), 0.0))
            act_scr[side] = act.astype(BF16)

        @pl.loop(0, N_CHIP)
        def _(n):
            total = None
            for side, weights in enumerate((held, theirs)):
                weight = weights[1, pl.ds(2 * n, 2)].reshape(SLICE, MINE)
                term = dot(act_scr[side], weight, ((1,), (1,)))
                total = term if total is None else total + term
            for side in range(2):
                added = jnp.where(n == q, own[side, tokens, :].astype(F32), 0.0)
                part[2 * n + side, tokens, :] = (
                    total[:, side * FEAT : (side + 1) * FEAT] + added
                ).astype(BF16)

        for copy in moves(m):
            copy.start()
        got[r, tokens, :] = part[r, tokens, :]

    @pl.loop(0, MINE // STEP)
    def _(m):
        for copy in moves(m):
            copy.wait()

    for side in range(2):
        total = got[side].astype(F32)
        for k in range(1, N_CHIP):
            total += got[2 * k + side].astype(F32)
        out[pl.ds(side * MINE, MINE), :] = total.astype(BF16)


def last_kernel(nx, par, shift, weight, out):
    @pl.loop(0, MINE // TILE)
    def _(m):
        at = pl.multiple_of(m * TILE, TILE)
        z = norm(blocks_of(nx, at), row_of(par, 4), row_of(par, 5))
        dz = step_back(z)
        for j in range(3):
            blend = (z + dz * shift[6 + j : 7 + j, :]).astype(BF16)
            out[j, pl.ds(at, TILE), :] = dot(
                blend, weight[:, :, j].reshape(WIDTH, SLICE)
            ).astype(BF16)


def per_device(
    hidden,
    lengths,
    square_matrix_shards,
    channel_mix_shards,
    lowrank_down,
    lowrank_up,
    token_shift_weights,
    attention_coefficients,
    norm_parameters,
):
    hx, wt, w3, wk, wv, wn, parg = exchange(
        start_kernel,
        [
            ((N_ROW, MINE, FEAT), BF16),
            ((2, 3, N_ROW, N_COL, 16, FEAT), BF16),
            ((N_COL, 16, WIDTH), BF16),
            ((N_COL, N_ROW, 16, MINE), BF16),
            ((N_COL, N_ROW, 16, MINE), BF16),
            ((N_ROW, N_COL, 3, 16, SLICE), BF16),
            ((N_ROW, 6, FEAT), F32),
        ],
        15 + 1 + 3 * RING + 1 + 14 + 15 + 15 + 7 + 15,
        9,
        1,
        square_matrix_shards,
        channel_mix_shards,
        norm_parameters,
        hidden,
        scratch=[
            pltpu.VMEM(square_matrix_shards.shape, F32),
            pltpu.VMEM(channel_mix_shards.shape, F32),
            pltpu.VMEM(square_matrix_shards.shape, BF16),
            pltpu.VMEM(channel_mix_shards.shape, BF16),
        ],
    )
    rkv, low = compute(
        mix_kernel,
        [((3, MINE, SLICE), F32), ((2, MINE, lowrank_down.shape[2]), F32)],
        (hx, parg, token_shift_weights, wt, lowrank_down.transpose(0, 2, 1)),
        flops=4 * 10**9,
    )
    mid, final, wkg = exchange(
        attend_kernel,
        [
            ((2, MINE, FEAT), BF16),
            ((PROMPTS, 2, HEAD, FEAT), BF16),
            ((N_COL, N_ROW, 16, MINE), BF16),
        ],
        PROMPTS * HOPS + 1 + RING,
        1,
        2,
        lengths,
        rkv,
        low,
        attention_coefficients,
        lowrank_up,
        hx,
        w3,
        wk,
        scratch=[
            pltpu.VMEM((2, MINE, FEAT), BF16),
            pltpu.VMEM((N_ROW + 2, MINE, FEAT), BF16),
            pltpu.VMEM((N_COL, 16, WIDTH), BF16),
        ],
        in_specs=[pl.BlockSpec(memory_space=pltpu.SMEM)] + [VMEM] * 4 + [ANY, VMEM, ANY],
        out_specs=[VMEM, VMEM, ANY],
    )
    moves = [
        ((2 * a + b) * N_COL + d, (2 * d + b) * N_COL + a)
        for a in range(N_CHIP)
        for b in range(2)
        for d in range(N_COL)
    ]
    midg, wvg, theirs = exchange(
        mid_kernel,
        [
            ((N_ROW, MINE, FEAT), BF16),
            ((N_COL, N_ROW, 16, MINE), BF16),
            ((2, N_ROW, N_COL, 16, MINE), BF16),
        ],
        9 + 14 + 2 * RING,
        2,
        3,
        mid,
        wk,
        wkg,
        wv,
    )
    final, midg = lax.optimization_barrier((final, midg))
    final = lax.ppermute(final, ("row", "col"), moves)
    final = final.reshape(4, 2, HEAD, 2, HEAD).transpose(0, 1, 3, 2, 4).astype(F32)
    final_state = final.reshape(4, 4, HEAD * HEAD)
    (out_hidden,) = exchange(
        mlp_kernel,
        [((2 * MINE, FEAT), BF16)],
        15 * MINE // STEP,
        16,
        4,
        midg,
        parg,
        token_shift_weights,
        wk,
        wkg,
        wv,
        wvg,
        theirs,
        mid,
        scratch=[
            pltpu.VMEM((2, N_ROW, N_COL, 16, MINE), BF16),
            pltpu.VMEM((2, STEP, MINE), BF16),
            pltpu.VMEM((N_ROW, MINE, FEAT), BF16),
            pltpu.VMEM((N_ROW, MINE, FEAT), BF16),
        ],
        in_specs=[VMEM] * 3 + [ANY] * 4 + [VMEM] * 2,
        out_specs=[VMEM],
    )
    nx, weight_next = exchange(
        next_kernel,
        [((N_ROW, MINE, FEAT), BF16), ((N_ROW, N_COL, 3, 16, SLICE), BF16)],
        2 + 1 + 14 + 2 * RING,
        1,
        5,
        out_hidden,
        wn,
    )
    (next_rkv,) = compute(
        last_kernel,
        [((3, MINE, SLICE), BF16)],
        (nx, parg, token_shift_weights, weight_next),
        flops=2 * 10**9,
    )
    return (out_hidden, next_rkv, final_state)


def solution(mesh):
    return jax.shard_map(
        per_device,
        mesh=mesh,
        in_specs=(
            P("col", "row"),
            P(),
            P(None, ("row", "col"), None),
            P(None, ("row", "col"), None),
            P(),
            P(),
            P(),
            P(),
            P(None, "row"),
        ),
        out_specs=(P("col", "row"), P(None, "row", "col"), P("row", "col", None)),
        check_vma=False,
    )
```

```python
import functools

import jax
import jax.numpy as jnp
from jax import lax
from jax.experimental import pallas as pl
from jax.experimental.pallas import tpu as pltpu
from jax.sharding import PartitionSpec as P

WIDTH = 2048
HEAD = 64
LMAX = 128
F32 = jnp.float32
BF16 = jnp.bfloat16
MESH = pl.DeviceIdType.MESH
ANY = pl.BlockSpec(memory_space=pl.ANY)
VMEM = pl.BlockSpec(memory_space=pltpu.VMEM)
N_ROW = 16
N_COL = 8
N_CHIP = 8
MINE = 512
FEAT = 128
SLICE = 256


def greet(devices):
    barrier = pltpu.get_barrier_semaphore()
    for device in devices:
        pl.semaphore_signal(barrier, inc=1, device_id=device, device_id_type=MESH)
    pl.semaphore_wait(barrier, len(devices))


class Copy:
    def __init__(self, source, target, send_sem, recv_sem, slot, device):
        self.made = lambda: pltpu.make_async_remote_copy(
            src_ref=source() if callable(source) else source,
            dst_ref=target() if callable(target) else target,
            send_sem=send_sem.at[slot],
            recv_sem=recv_sem.at[slot],
            device_id=device,
            device_id_type=MESH,
        )

    def start(self):
        self.made().start()

    def wait_recv(self):
        self.made().wait_recv()

    def wait_send(self):
        self.made().wait_send()


def keep(source, target, sem):
    copy = pltpu.make_async_copy(source, target, sem)
    copy.start()
    return copy


def exchange(
    kernel,
    outs,
    n_remote,
    n_local,
    collective_id,
    *operands,
    scratch=(),
    in_specs=None,
    out_specs=None,
):
    return pl.pallas_call(
        kernel,
        out_shape=[jax.ShapeDtypeStruct(*out) for out in outs],
        in_specs=in_specs or [ANY] * len(operands),
        out_specs=out_specs or [ANY] * len(outs),
        scratch_shapes=[
            pltpu.SemaphoreType.DMA((n_remote,)),
            pltpu.SemaphoreType.DMA((n_remote,)),
            pltpu.SemaphoreType.DMA((n_local,)),
            *scratch,
        ],
        compiler_params=pltpu.CompilerParams(
            collective_id=collective_id, has_side_effects=True, vmem_limit_bytes=56 * 2**20
        ),
        cost_estimate=pl.CostEstimate(flops=0, bytes_accessed=48 * 2**20, transcendentals=0),
    )(*operands)


def place():
    r = lax.axis_index("row")
    c = lax.axis_index("col")
    h = lax.rem(r, 2)
    return r, c, h, lax.div(r, 2), r + 1 - 2 * h


class Links:
    def __init__(self, send_sem, recv_sem, first=0):
        self.send_sem = send_sem
        self.recv_sem = recv_sem
        self.slot = first
        self.copies = []
        self.open = []

    def go(self, source, target, device):
        copy = Copy(source, target, self.send_sem, self.recv_sem, self.slot, device)
        copy.start()
        self.slot += 1
        self.copies.append(copy)
        self.open.append(copy)
        return copy

    def arrive(self, copy):
        copy.wait_recv()
        self.open = [other for other in self.open if other is not copy]

    def finish(self):
        for copy in self.open:
            copy.wait_recv()
        for copy in self.copies:
            copy.wait_send()


RING = 14


def ring_at(axis):
    r, c, h, q, _ = place()
    here = q if axis == "row" else c
    step_z = 1 - 2 * lax.rem(here, 2)
    chips = {
        "p": lax.rem(here + 2, 8),
        "m": lax.rem(here + 6, 8),
        "z": here + step_z,
        "o": lax.rem(here + 4, 8),
        "pz": lax.rem(here + 2, 8) + step_z,
        "mz": lax.rem(here + 6, 8) + step_z,
        "oz": lax.rem(here + 4, 8) + step_z,
    }
    devices = {
        side: (2 * chips[side] + h, c) if axis == "row" else (r, chips[side]) for side in "pmz"
    }
    return here, chips, devices


def ring_peers(axis):
    return list(ring_at(axis)[2].values())


def ring(links, axis, slot, own=None, which=(0, 1), ready=None, seen=None, heavy=None):
    here, chips, to = ring_at(axis)
    heavy = axis == "row" if heavy is None else heavy
    seen = seen or (lambda chip, half: None)

    def take(copy, chip, half):
        links.arrive(copy)
        seen(chip, half)

    def forward(chip, half, side):
        return links.go(lambda: slot(chip, half), lambda: slot(chip, half), to[side])

    first = {}
    for k in range(2):
        if ready is not None:
            ready(k)
        target = functools.partial(slot, here, which[k])
        source = functools.partial(own, k) if own is not None else target
        for side in "zpm":
            first[side, k] = links.go(source, target, to[side])
    yield
    for k in range(2):
        take(first["p", k], chips["m"], which[k])
    low = forward(chips["m"], 0, "p")
    for k in range(2):
        take(first["m", k], chips["p"], which[k])
    high = forward(chips["p"], 1, "m")
    yield
    beside = {}
    for k in range(2):
        take(first["z", k], chips["z"], which[k])
        for side in "pm":
            beside[side, k] = forward(chips["z"], which[k], side)
    yield
    if heavy:
        take(low, chips["o"], 0)
        low = forward(chips["o"], 0, "z")
        take(high, chips["o"], 1)
        high = forward(chips["o"], 1, "z")
        yield
        for k in range(2):
            take(beside["p", k], chips["mz"], which[k])
            take(beside["m", k], chips["pz"], which[k])
    else:
        take(low, chips["o"], 0)
        take(high, chips["o"], 1)
        for k in range(2):
            take(beside["p", k], chips["mz"], which[k])
        low = forward(chips["mz"], 0, "p")
        for k in range(2):
            take(beside["m", k], chips["pz"], which[k])
        high = forward(chips["pz"], 1, "m")
        yield
    take(low, chips["oz"], 0)
    take(high, chips["oz"], 1)


def together(*steps):
    active = list(steps)
    while active:
        for step in list(active):
            if next(step, StopIteration) is StopIteration:
                active.remove(step)


def aligned(index, size):
    return pl.ds(pl.multiple_of(index * size, size), size)


def start_kernel(
    square_in,
    mlp_in,
    par,
    hid,
    hx,
    wt,
    w3,
    wk,
    wv,
    wn,
    parg,
    send_sem,
    recv_sem,
    local_sem,
    square_wide,
    mlp_wide,
    square,
    mlp,
):
    r, c, h, q, sibling = place()
    rows = [lax.rem(r + d, N_ROW) for d in range(1, N_ROW)]
    cols = [lax.rem(c + d, N_COL) for d in range(1, N_COL)]

    def time_part(p):
        return square.at[pl.ds(0, 3), :, aligned(p, FEAT)]

    def key_part(p):
        return mlp.at[0, :, aligned(p, MINE)]

    def value_part(p):
        return mlp.at[1, :, aligned(p, MINE)]

    def next_part(p):
        return square.at[pl.ds(4, 3), :, aligned(p, SLICE)]

    mine = hid.at[aligned(h, MINE)]
    square_load = keep(square_in, square_wide, local_sem.at[7])
    mlp_load = keep(mlp_in, mlp_wide, local_sem.at[8])
    local = [
        keep(par, parg.at[r], local_sem.at[1]),
        keep(mine, hx.at[r], local_sem.at[2]),
    ]
    greet([(p, c) for p in rows] + [(r, p) for p in cols])
    links = Links(send_sem, recv_sem)
    times = []
    own_time = []
    other = links.go(hid.at[aligned(1 - h, MINE)], hx.at[r], (sibling, c))

    def hid_own(k):
        return (mine, hx.at[sibling])[k]

    def hid_ready(k):
        if k == 1:
            links.arrive(other)

    def time_ready(k):
        if k == 0:
            for copy in times:
                links.arrive(copy)
            links.go(wt.at[h, :, :, c], wt.at[h, :, :, c], (sibling, c))

    def time_slot(chip, half):
        return wt.at[h, :, pl.ds(8 * half, 8), chip]

    def time_seen(chip, half):
        links.go(time_slot(chip, half), time_slot(chip, half), (sibling, c))

    def out_slot(chip, half):
        return w3.at[chip, :, pl.ds(1024 * half, 1024)]

    def out_own(k):
        return square.at[3, :, pl.ds(1024 * k, 1024)]

    def feed():
        square_load.wait()
        for j in range(3):
            square[j] = square_wide[j].astype(BF16)
        for p in rows:
            times.append(links.go(time_part(p), wt.at[lax.rem(p, 2), :, r, c], (p, c)))
        own_time.append(keep(time_part(r), wt.at[h, :, r, c], local_sem.at[0]))
        yield

    def casts():
        for j in range(3, 7):
            square[j] = square_wide[j].astype(BF16)
        mlp_load.wait()
        mlp[...] = mlp_wide[...].astype(BF16)
        own_time[0].wait()
        yield

    def rest():
        local.extend(
            [
                keep(square.at[3], w3.at[c], local_sem.at[3]),
                keep(key_part(r), wk.at[c, r], local_sem.at[4]),
                keep(value_part(r), wv.at[c, r], local_sem.at[5]),
                keep(next_part(c), wn.at[r, c], local_sem.at[6]),
            ]
        )
        for p in rows:
            links.go(par, parg.at[r], (p, c))
        yield
        for p in rows:
            links.go(key_part(p), wk.at[c, r], (p, c))
        for p in cols:
            links.go(next_part(p), wn.at[r, c], (r, p))
        for p in rows:
            links.go(value_part(p), wv.at[c, r], (p, c))

    together(
        feed(),
        ring(
            links,
            "row",
            lambda chip, side: hx.at[2 * chip + side],
            own=hid_own,
            which=(h, 1 - h),
            ready=hid_ready,
        ),
        casts(),
        ring(links, "col", time_slot, ready=time_ready, seen=time_seen),
        rest(),
        ring(links, "col", out_slot, own=out_own),
    )
    links.finish()
    for copy in local:
        copy.wait()


def row_ring(links, source, target):
    return ring(
        links, "row", lambda chip, side: target.at[2 * chip + side], own=lambda k: source.at[k]
    )


def own_block(source, target, q, local_sem):
    return [keep(source.at[k], target.at[2 * q + k], local_sem.at[k]) for k in range(2)]


def mid_kernel(mid, wk, wkg, wv, midg, wvg, theirs, send_sem, recv_sem, local_sem):
    r, c, h, q, sibling = place()
    local = own_block(mid, midg, q, local_sem)
    greet([(sibling, c)] + ring_peers("row") + ring_peers("col"))
    links = Links(send_sem, recv_sem)

    def value_slot(chip, half):
        return wvg.at[chip, pl.ds(8 * half, 8)]

    def value_seen(chip, half):
        links.go(
            value_slot(chip, half), theirs.at[1, pl.ds(8 * half, 8), chip], (sibling, c)
        )

    def across():
        links.go(wk.at[c], theirs.at[0, :, c], (sibling, c))
        links.go(wv.at[c], theirs.at[1, :, c], (sibling, c))
        for d in range(1, N_COL):
            p = lax.rem(c + d, N_COL)
            links.go(wkg.at[p], theirs.at[0, :, p], (sibling, c))
        yield

    together(
        row_ring(links, mid, midg),
        ring(
            links,
            "col",
            value_slot,
            own=lambda k: wv.at[c, pl.ds(8 * k, 8)],
            seen=value_seen,
        ),
        across(),
    )
    links.finish()
    for copy in local:
        copy.wait()


def compute(kernel, outs, operands, scratch=(), grid=None, in_specs=None, out_specs=None, flops=0):
    return pl.pallas_call(
        kernel,
        grid=grid if grid is not None else (),
        out_shape=[jax.ShapeDtypeStruct(*out) for out in outs],
        in_specs=in_specs if in_specs is not None else [VMEM] * len(operands),
        out_specs=out_specs if out_specs is not None else [VMEM] * len(outs),
        scratch_shapes=list(scratch),
        compiler_params=pltpu.CompilerParams(vmem_limit_bytes=56 * 2**20),
        cost_estimate=pl.CostEstimate(flops=flops, bytes_accessed=16 * 2**20, transcendentals=0),
    )(*operands)


def dot(a, b, dims=((1,), (0,))):
    return lax.dot_general(a, b, (dims, ((), ())), preferred_element_type=F32)


def split(x):
    high = x.astype(BF16)
    return high, (x - high.astype(F32)).astype(BF16)


def dot3(a, b, dims=((1,), (0,))):
    a_high, a_low = a
    b_high, b_low = b
    return dot(a_high, b_high, dims) + (dot(a_high, b_low, dims) + dot(a_low, b_high, dims))


def norm(source, gain, bias):
    center = jnp.sum(source, axis=-1, keepdims=True) / WIDTH
    second = jnp.sum(source * source, axis=-1, keepdims=True) / WIDTH
    scaled = (source - center) * lax.rsqrt(second - center * center + 1e-05)
    return (scaled * gain + bias).astype(BF16).astype(F32)


def row_of(par, i):
    return jnp.concatenate([par[j, i : i + 1, :] for j in range(N_ROW)], axis=1)


def step_back(z):
    position = lax.rem(lax.broadcasted_iota(jnp.int32, z.shape, 0), LMAX)
    return jnp.where(position == 0, 0.0, pltpu.roll(z, 1, 0)) - z


TILE = 256


def blocks_of(ref, at):
    return jnp.concatenate(
        [ref[j, pl.ds(at, TILE), :].astype(F32) for j in range(ref.shape[0])], axis=1
    )


def mix_kernel(hx, par, shift, wt, down, rkv, low):
    @pl.loop(0, MINE // TILE)
    def _(m):
        at = pl.multiple_of(m * TILE, TILE)
        z = norm(blocks_of(hx, at), row_of(par, 0), row_of(par, 1))
        dz = step_back(z)
        for j in range(5):
            blend = (z + dz * shift[j : j + 1, :]).astype(BF16)
            if j < 3:
                weight = jnp.concatenate(
                    [wt[side, j].reshape(WIDTH, FEAT) for side in range(2)], axis=1
                )
                rkv[j, pl.ds(at, TILE), :] = dot(blend, weight)
            else:
                low[j - 3, pl.ds(at, TILE), :] = dot(blend, down[j - 3], ((1,), (1,)))


def one_prompt(prompt, lens, rkv, low, coef, up, att, final):
    r, c, h, q, _ = place()
    length = lens[c * 8 + h * 4 + prompt]
    tokens = aligned(prompt, LMAX)
    wide = SLICE
    channels = aligned(q, SLICE)
    heads = wide // HEAD
    live = (lax.broadcasted_iota(jnp.int32, (LMAX, wide), 0) < length).astype(F32)
    lane = lax.broadcasted_iota(jnp.int32, (LMAX, wide), 1) // HEAD
    t = lax.broadcasted_iota(jnp.int32, (LMAX, LMAX), 0)
    u = lax.broadcasted_iota(jnp.int32, (LMAX, LMAX), 1)
    seg = (
        lax.broadcasted_iota(jnp.int32, (wide, wide), 0) // HEAD
        == lax.broadcasted_iota(jnp.int32, (wide, wide), 1) // HEAD
    ).astype(F32).astype(BF16)
    lower = (t >= u).astype(F32).astype(BF16)

    def head_sum(x):
        high, low_part = split(x)
        return dot(high, seg) + dot(low_part, seg)

    def only(x, k):
        return jnp.where(lane == k, x, jnp.zeros_like(x))

    receptance, key, value = rkv[0, tokens], rkv[1, tokens], rkv[2, tokens]
    decay = (
        -0.606531
        * jax.nn.sigmoid(coef[0:1, channels] + dot(jnp.tanh(low[0, tokens]).astype(BF16), up[0, :, channels]))
        * live
    )
    rate = jax.nn.sigmoid(coef[1:2, channels] + dot(low[1, tokens].astype(BF16), up[1, :, channels]))
    kappa = key * coef[2:3, channels]
    kappa = kappa * lax.rsqrt(head_sum(kappa * kappa) + 1e-05)
    remove = -kappa * live
    write = kappa * rate * live
    key = key * live
    value = value * live
    d_high, d_rest = split(decay)
    d_mid, d_low = split(decay - d_high.astype(F32))
    total = dot(lower, d_high) + (dot(lower, d_mid) + dot(lower, d_low))
    middle = total[LMAX // 2 - 1 : LMAX // 2, :]
    last = total[LMAX - 1 : LMAX, :]
    back = jnp.exp(middle - total)
    pull = split(remove * jnp.exp(total - decay - middle))
    read = split(receptance * jnp.exp(total - middle))
    write_back = split(write * back)
    key_back = split(key * back)
    value_parts = split(value)

    left = tuple(
        jnp.concatenate([x for k in range(heads) for x in (only(pull[i], k), only(read[i], k))])
        for i in range(2)
    )
    right = tuple(jnp.concatenate([write_back[i], key_back[i]]) for i in range(2))
    pairs = dot3(left, right, ((1,), (1,)))
    strict = t > u
    t2 = lax.broadcasted_iota(jnp.int32, (LMAX, 2 * LMAX), 0)
    u2 = lax.rem(lax.broadcasted_iota(jnp.int32, (LMAX, 2 * LMAX), 1), LMAX)
    upto = t2 >= u2
    solves, pull_key, reads = [], [], []
    for k in range(heads):
        base = k * 2 * LMAX
        system = jnp.where(strict, pairs[base : base + LMAX, :LMAX], 0.0)
        pull_key.append(split(jnp.where(strict, pairs[base : base + LMAX, LMAX:], 0.0)))
        reads.append(split(jnp.where(upto, pairs[base + LMAX : base + 2 * LMAX], 0.0)))
        solves.append(system)
    inverse = []
    for k in range(heads):
        near = (t // 2 == u // 2)
        inverse.append(
            jnp.where(near, solves[k], 0.0) + (t == u).astype(F32)
        )
    size = 2
    while size < LMAX:
        inside = (t // (2 * size) == u // (2 * size)) & (t // size != u // size)
        grown = []
        for k in range(heads):
            known = split(inverse[k])
            cross = split(jnp.where(inside, solves[k], 0.0))
            product = split(dot3(known, cross))
            grown.append(inverse[k] + dot3(product, known))
        inverse = grown
        size *= 2

    def across(mats, parts):
        wide_left = tuple(jnp.concatenate([mat[i] for mat in mats], axis=1) for i in range(2))
        tall = tuple(
            jnp.concatenate([only(part[i], k) for k in range(heads) for part in parts])
            for i in range(2)
        )
        return dot3(wide_left, tall)

    start = across(pull_key, [value_parts])
    pulled = split(across([split(x) for x in inverse], [split(start)]))
    output = across(reads, [pulled, value_parts])
    tail = jnp.exp(last - total)
    write_tail = split(write * tail)
    key_tail = split(key * tail)
    tall = tuple(jnp.concatenate([pulled[i], value_parts[i]]) for i in range(2))
    tails = tuple(jnp.concatenate([write_tail[i], key_tail[i]]) for i in range(2))
    state = dot3(tall, tails, ((0,), (0,)))
    even = lax.broadcasted_iota(jnp.int32, (HEAD, FEAT), 1) < HEAD
    for k in range(heads // 2):
        lanes = slice(k * FEAT, (k + 1) * FEAT)
        final[prompt, k] = jnp.where(
            even,
            state[k * FEAT : k * FEAT + HEAD, lanes],
            state[k * FEAT + HEAD : (k + 1) * FEAT, lanes],
        ).astype(BF16)
    bonus = head_sum(receptance * key * coef[3:4, channels])
    out = (output + bonus * value) * live
    center = head_sum(out) * (1.0 / HEAD)
    out = out - center
    spread = head_sum(out * out) * (1.0 / HEAD)
    out = (out * lax.rsqrt(spread + 0.00064) * coef[4:5, channels] + coef[5:6, channels]).astype(BF16)
    for side in range(2):
        att[side, tokens] = out[:, side * FEAT : (side + 1) * FEAT]


PROMPTS = MINE // LMAX
HOPS = 9


def attend_kernel(
    lens,
    rkv,
    low,
    coef,
    up,
    own,
    w3,
    wk,
    wn,
    mid,
    final,
    wkg,
    wng,
    send_sem,
    recv_sem,
    local_sem,
    att,
    attg,
    w3x,
):
    r, c, h, q, sibling = place()
    _, chips, to = ring_at("row")
    greet([(sibling, c)] + ring_peers("row") + ring_peers("col"))
    links = Links(send_sem, recv_sem, PROMPTS * HOPS)
    links.go(w3, w3x, (sibling, c))
    near = keep(own.at[pl.ds(pl.multiple_of(r - h, 2), 2)], attg.at[pl.ds(N_ROW, 2)], local_sem.at[0])
    keys = ring(
        links,
        "col",
        lambda chip, half: wkg.at[chip, pl.ds(8 * half, 8)],
        own=lambda k: wk.at[c, pl.ds(8 * k, 8)],
    )
    far = keep(wn.at[r], wng.at[r], local_sem.at[1])
    links.go(wn.at[r], wng.at[r], (sibling, c))

    def weight_slot(chip, half):
        return wng.at[2 * chip + h, pl.ds(4 * half, 4)]

    def weight_seen(chip, half):
        links.go(
            lambda: weight_slot(chip, half), lambda: weight_slot(chip, half), (sibling, c)
        )

    weights = ring(
        links,
        "row",
        weight_slot,
        own=lambda k: wn.at[r, pl.ds(4 * k, 4)],
        seen=weight_seen,
    )

    def advance():
        for steps in (keys, weights):
            next(steps)

    advance()

    def hop(prompt, slot, chip, side, half=None):
        def block():
            tokens = aligned(prompt, LMAX)
            if half is None:
                return attg.at[pl.ds(2 * chips.get(chip, q), 2), tokens]
            return attg.at[2 * chips[chip] + half, tokens]

        def source():
            return att.at[:, aligned(prompt, LMAX)] if chip == "own" else block()

        return Copy(source, block, send_sem, recv_sem, prompt * HOPS + slot, to[side])

    def hops(prompt):
        return [
            hop(prompt, 0, "own", "p"),
            hop(prompt, 1, "own", "m"),
            hop(prompt, 2, "own", "z"),
            hop(prompt, 3, "m", "p", 0),
            hop(prompt, 4, "p", "m", 1),
            hop(prompt, 5, "z", "p"),
            hop(prompt, 6, "z", "m"),
            hop(prompt, 7, "o", "z", 0),
            hop(prompt, 8, "o", "z", 1),
        ]

    @pl.loop(0, PROMPTS + 2)
    def _(step):
        @pl.when(step < PROMPTS)
        def _():
            one_prompt(step, lens, rkv, low, coef, up, att, final)
            copies = hops(step)
            for k in range(3):
                copies[k].start()
            tokens = aligned(step, LMAX)
            for side in range(2):
                attg[2 * q + side, tokens] = att[side, tokens]

        @pl.when((step >= 1) & (step <= PROMPTS))
        def _():
            copies = hops(step - 1)
            copies[0].wait_recv()
            copies[3].start()
            copies[1].wait_recv()
            copies[4].start()
            copies[2].wait_recv()
            copies[5].start()
            copies[6].start()

        @pl.when(step >= 2)
        def _():
            copies = hops(step - 2)
            copies[3].wait_recv()
            copies[7].start()
            copies[4].wait_recv()
            copies[8].start()

        @pl.when(step == 1)
        def _():
            advance()

        @pl.when(step == 2)
        def _():
            advance()

        @pl.when(step == 3)
        def _():
            advance()

    @pl.loop(0, PROMPTS)
    def _(prompt):
        copies = hops(prompt)
        for k in (5, 6, 7, 8):
            copies[k].wait_recv()
        for copy in copies:
            copy.wait_send()

    together(keys, weights)
    links.finish()
    near.wait()
    far.wait()

    @pl.loop(0, MINE // TILE)
    def _(m):
        rows = aligned(m, TILE)
        wide = jnp.concatenate([attg[j, rows, :] for j in range(N_ROW)], axis=1)
        weight = jnp.concatenate([w[...].reshape(FEAT, WIDTH) for w in (w3, w3x)])
        total = dot(wide, weight, ((1,), (1,)))
        for k, side in enumerate((h, 1 - h)):
            mid[side, rows, :] = (
                attg[N_ROW + side, rows, :].astype(F32) + total[:, k * FEAT : (k + 1) * FEAT]
            ).astype(BF16)


def tail_kernel(
    midg,
    par,
    shift,
    wk,
    wkg,
    wv,
    wvg,
    theirs,
    own,
    wng,
    state,
    out,
    rkv,
    final,
    send_sem,
    recv_sem,
    local_sem,
    held,
    act_scr,
    part,
    got,
    nx,
    weight,
):
    r, c, h, q, sibling = place()
    _, chips, to = ring_at("col")
    copies = []
    for m, (near, far) in enumerate(((wk, wkg), (wv, wvg))):
        copies.append(keep(near.at[c], held.at[m, :, c], local_sem.at[8 * m]))
        for d in range(1, N_COL):
            p = lax.rem(c + d, N_COL)
            copies.append(keep(far.at[p], held.at[m, :, p], local_sem.at[8 * m + d]))
    load = keep(wng, weight, local_sem.at[16])
    rows = [lax.rem(r + d, N_ROW) for d in range(1, N_ROW)]
    n_sum = PROMPTS * (N_ROW - 1)
    n_turn = n_sum + 2 * PROMPTS
    n_ring = n_turn + PROMPTS * HOPS

    def target(i):
        return (2 * c + lax.rem(h + i, 2), q)

    barrier = pltpu.get_barrier_semaphore()
    peers = [(p, c) for p in rows] + ring_peers("col")

    @pl.when(q != c)
    def _():
        for i in range(2):
            pl.semaphore_signal(barrier, inc=1, device_id=target(i), device_id_type=MESH)

    for device in peers:
        pl.semaphore_signal(barrier, inc=1, device_id=device, device_id_type=MESH)
    pl.semaphore_wait(barrier, len(peers) + 2 * (q != c).astype(jnp.int32))

    move_state = Copy(state, final, send_sem, recv_sem, n_ring, target(0))

    @pl.when(q == c)
    def _():
        keep(state, final, recv_sem.at[n_ring])

    @pl.when(q != c)
    def _():
        move_state.start()

    for copy in copies:
        copy.wait()

    def sums(m):
        def copy_of(i, p):
            return Copy(
                lambda: part.at[p, aligned(m, LMAX)],
                lambda: got.at[r, aligned(m, LMAX)],
                send_sem,
                recv_sem,
                m * (N_ROW - 1) + i,
                (p, c),
            )

        return [copy_of(i, p) for i, p in enumerate(rows)]

    def source_rows(m, i):
        return pl.ds(pl.multiple_of(lax.rem(h + i, 2) * MINE + m * LMAX, LMAX), LMAX)

    def turn(m, i):
        return pltpu.make_async_remote_copy(
            src_ref=out.at[source_rows(m, i)],
            dst_ref=nx.at[2 * q + h, aligned(m, LMAX)],
            send_sem=send_sem.at[n_sum + 2 * m + i],
            recv_sem=recv_sem.at[n_sum + 2 * m + h],
            device_id=target(i),
            device_id_type=MESH,
        )

    def hop(m, slot, chip, side, half=None):
        def block():
            at = chips.get(chip, c)
            if half is None:
                return nx.at[pl.ds(2 * at, 2), aligned(m, LMAX)]
            return nx.at[2 * at + half, aligned(m, LMAX)]

        return Copy(block, block, send_sem, recv_sem, n_turn + m * HOPS + slot, to[side])

    def hops(m):
        return [
            hop(m, 0, "own", "p"),
            hop(m, 1, "own", "m"),
            hop(m, 2, "own", "z"),
            hop(m, 3, "m", "p", 0),
            hop(m, 4, "p", "m", 1),
            hop(m, 5, "z", "p"),
            hop(m, 6, "z", "m"),
            hop(m, 7, "o", "z", 0),
            hop(m, 8, "o", "z", 1),
        ]

    def normed(ref, m, k):
        tokens = aligned(m, LMAX)
        return norm(
            jnp.concatenate([ref[j, tokens, :].astype(F32) for j in range(N_ROW)], axis=1),
            row_of(par, k),
            row_of(par, k + 1),
        )

    def channel(m):
        tokens = aligned(m, LMAX)
        z = normed(midg, m, 2)
        blend = (z + step_back(z) * shift[5:6, :]).astype(BF16)
        for side, weights in enumerate((held, theirs)):
            act = jnp.square(jnp.maximum(dot(blend, weights[0].reshape(WIDTH, MINE)), 0.0))
            act_scr[side] = act.astype(BF16)

        @pl.loop(0, N_CHIP)
        def _(n):
            total = None
            for side, weights in enumerate((held, theirs)):
                rows_n = weights[1, pl.ds(2 * n, 2)].reshape(SLICE, MINE)
                term = dot(act_scr[side], rows_n, ((1,), (1,)))
                total = term if total is None else total + term
            for side in range(2):
                added = jnp.where(n == q, own[side, tokens, :].astype(F32), 0.0)
                part[2 * n + side, tokens, :] = (
                    total[:, side * FEAT : (side + 1) * FEAT] + added
                ).astype(BF16)

        for copy in sums(m):
            copy.start()
        got[r, tokens, :] = part[r, tokens, :]

    def add_up(m):
        for copy in sums(m):
            copy.wait_recv()
        tokens = aligned(m, LMAX)
        for side in range(2):
            total = got[side, tokens, :].astype(F32)
            for k in range(1, N_CHIP):
                total += got[2 * k + side, tokens, :].astype(F32)
            rows_m = pl.ds(pl.multiple_of(side * MINE + m * LMAX, LMAX), LMAX)
            out[rows_m, :] = total.astype(BF16)

        @pl.when(q == c)
        def _():
            keep(
                out.at[source_rows(m, 0)],
                nx.at[r, aligned(m, LMAX)],
                recv_sem.at[n_sum + 2 * m + h],
            )

        @pl.when(q != c)
        def _():
            turn(m, 0).start()

        turn(m, 1).start()

    def spread(m):
        for k in range(2):
            block = nx.at[2 * c + k, aligned(m, LMAX)]
            pltpu.make_async_copy(block, block, recv_sem.at[n_sum + 2 * m + k]).wait()
        for k in (2, 0, 1):
            hops(m)[k].start()

    def forward(m):
        ring_m = hops(m)
        ring_m[0].wait_recv()
        ring_m[3].start()
        ring_m[1].wait_recv()
        ring_m[4].start()
        ring_m[2].wait_recv()
        ring_m[5].start()
        ring_m[6].start()

    def close(m):
        ring_m = hops(m)
        ring_m[3].wait_recv()
        ring_m[7].start()
        ring_m[4].wait_recv()
        ring_m[8].start()

    def project(m):
        ring_m = hops(m)
        for k in (5, 6, 7, 8):
            ring_m[k].wait_recv()
        z = normed(nx, m, 4)
        dz = step_back(z)
        for j in range(3):
            blend = (z + dz * shift[6 + j : 7 + j, :]).astype(BF16)
            rkv[j, aligned(m, LMAX), :] = dot(
                blend, weight[:, :, j].reshape(WIDTH, SLICE)
            ).astype(BF16)

    stages = (channel, add_up, spread, forward, close, project)

    @pl.loop(0, PROMPTS + len(stages) - 1)
    def _(step):
        @pl.when(step == len(stages) - 1)
        def _():
            load.wait()

        for lag, stage in enumerate(stages):

            @pl.when((step >= lag) & (step < PROMPTS + lag))
            def _():
                stage(step - lag)

    @pl.loop(0, PROMPTS)
    def _(m):
        for copy in sums(m) + hops(m):
            copy.wait_send()

        @pl.when(q != c)
        def _():
            turn(m, 0).wait_send()

        turn(m, 1).wait_send()

    pltpu.make_async_copy(state, final, recv_sem.at[n_ring]).wait()

    @pl.when(q != c)
    def _():
        move_state.wait_send()


def per_device(
    hidden,
    lengths,
    square_matrix_shards,
    channel_mix_shards,
    lowrank_down,
    lowrank_up,
    token_shift_weights,
    attention_coefficients,
    norm_parameters,
):
    hx, wt, w3, wk, wv, wn, parg = exchange(
        start_kernel,
        [
            ((N_ROW, MINE, FEAT), BF16),
            ((2, 3, N_ROW, N_COL, 16, FEAT), BF16),
            ((N_COL, 16, WIDTH), BF16),
            ((N_COL, N_ROW, 16, MINE), BF16),
            ((N_COL, N_ROW, 16, MINE), BF16),
            ((N_ROW, N_COL, 3, 16, SLICE), BF16),
            ((N_ROW, 6, FEAT), F32),
        ],
        15 + 1 + 3 * RING + 1 + 14 + 15 + 15 + 7 + 15,
        9,
        1,
        square_matrix_shards,
        channel_mix_shards,
        norm_parameters,
        hidden,
        scratch=[
            pltpu.VMEM(square_matrix_shards.shape, F32),
            pltpu.VMEM(channel_mix_shards.shape, F32),
            pltpu.VMEM(square_matrix_shards.shape, BF16),
            pltpu.VMEM(channel_mix_shards.shape, BF16),
        ],
    )
    rkv, low = compute(
        mix_kernel,
        [((3, MINE, SLICE), F32), ((2, MINE, lowrank_down.shape[2]), F32)],
        (hx, parg, token_shift_weights, wt, lowrank_down.transpose(0, 2, 1)),
        flops=4 * 10**9,
    )
    mid, state, wkg, wng = exchange(
        attend_kernel,
        [
            ((2, MINE, FEAT), BF16),
            ((PROMPTS, 2, HEAD, FEAT), BF16),
            ((N_COL, N_ROW, 16, MINE), BF16),
            ((N_ROW, N_COL, 3, 16, SLICE), BF16),
        ],
        PROMPTS * HOPS + 2 + 14 + 2 * RING,
        2,
        2,
        lengths,
        rkv,
        low,
        attention_coefficients,
        lowrank_up,
        hx,
        w3,
        wk,
        wn,
        scratch=[
            pltpu.VMEM((2, MINE, FEAT), BF16),
            pltpu.VMEM((N_ROW + 2, MINE, FEAT), BF16),
            pltpu.VMEM((N_COL, 16, WIDTH), BF16),
        ],
        in_specs=[pl.BlockSpec(memory_space=pltpu.SMEM)] + [VMEM] * 4 + [ANY, VMEM, ANY, ANY],
        out_specs=[VMEM, VMEM, ANY, ANY],
    )
    midg, wvg, theirs = exchange(
        mid_kernel,
        [
            ((N_ROW, MINE, FEAT), BF16),
            ((N_COL, N_ROW, 16, MINE), BF16),
            ((2, N_ROW, N_COL, 16, MINE), BF16),
        ],
        9 + 14 + 2 * RING,
        2,
        3,
        mid,
        wk,
        wkg,
        wv,
    )
    out_hidden, next_rkv, final = exchange(
        tail_kernel,
        [
            ((2 * MINE, FEAT), BF16),
            ((3, MINE, SLICE), BF16),
            ((PROMPTS, 2, HEAD, FEAT), BF16),
        ],
        PROMPTS * (N_ROW - 1) + 2 * PROMPTS + PROMPTS * HOPS + 1,
        17,
        4,
        midg,
        parg,
        token_shift_weights,
        wk,
        wkg,
        wv,
        wvg,
        theirs,
        mid,
        wng,
        state,
        scratch=[
            pltpu.VMEM((2, N_ROW, N_COL, 16, MINE), BF16),
            pltpu.VMEM((2, LMAX, MINE), BF16),
            pltpu.VMEM((N_ROW, MINE, FEAT), BF16),
            pltpu.VMEM((N_ROW, MINE, FEAT), BF16),
            pltpu.VMEM((N_ROW, MINE, FEAT), BF16),
            pltpu.VMEM((N_ROW, N_COL, 3, 16, SLICE), BF16),
        ],
        in_specs=[VMEM] * 3 + [ANY] * 4 + [VMEM] * 2 + [ANY] * 2,
        out_specs=[VMEM, VMEM, ANY],
    )
    final = final.reshape(4, 2, HEAD, 2, HEAD).transpose(0, 1, 3, 2, 4).astype(F32)
    final_state = final.reshape(4, 4, HEAD * HEAD)
    return (out_hidden, next_rkv, final_state)


def solution(mesh):
    return jax.shard_map(
        per_device,
        mesh=mesh,
        in_specs=(
            P("col", "row"),
            P(),
            P(None, ("row", "col"), None),
            P(None, ("row", "col"), None),
            P(),
            P(),
            P(),
            P(),
            P(None, "row"),
        ),
        out_specs=(P("col", "row"), P(None, "row", "col"), P("row", "col", None)),
        check_vma=False,
    )
```

```python
import functools

import jax
import jax.numpy as jnp
from jax import lax
from jax.experimental import pallas as pl
from jax.experimental.pallas import tpu as pltpu
from jax.sharding import PartitionSpec as P

WIDTH = 2048
HEAD = 64
LMAX = 128
F32 = jnp.float32
BF16 = jnp.bfloat16
MESH = pl.DeviceIdType.MESH
ANY = pl.BlockSpec(memory_space=pl.ANY)
VMEM = pl.BlockSpec(memory_space=pltpu.VMEM)
N_ROW = 16
N_COL = 8
N_CHIP = 8
MINE = 512
FEAT = 128
SLICE = 256


def greet(devices):
    barrier = pltpu.get_barrier_semaphore()
    for device in devices:
        pl.semaphore_signal(barrier, inc=1, device_id=device, device_id_type=MESH)
    pl.semaphore_wait(barrier, len(devices))


class Copy:
    def __init__(self, source, target, send_sem, recv_sem, slot, device):
        self.made = lambda: pltpu.make_async_remote_copy(
            src_ref=source() if callable(source) else source,
            dst_ref=target() if callable(target) else target,
            send_sem=send_sem.at[slot],
            recv_sem=recv_sem.at[slot],
            device_id=device,
            device_id_type=MESH,
        )

    def start(self):
        self.made().start()

    def wait_recv(self):
        self.made().wait_recv()

    def wait_send(self):
        self.made().wait_send()


def keep(source, target, sem):
    copy = pltpu.make_async_copy(source, target, sem)
    copy.start()
    return copy


def exchange(
    kernel,
    outs,
    n_remote,
    n_local,
    collective_id,
    *operands,
    scratch=(),
    in_specs=None,
    out_specs=None,
):
    return pl.pallas_call(
        kernel,
        out_shape=[jax.ShapeDtypeStruct(*out) for out in outs],
        in_specs=in_specs or [ANY] * len(operands),
        out_specs=out_specs or [ANY] * len(outs),
        scratch_shapes=[
            pltpu.SemaphoreType.DMA((n_remote,)),
            pltpu.SemaphoreType.DMA((n_remote,)),
            pltpu.SemaphoreType.DMA((n_local,)),
            *scratch,
        ],
        compiler_params=pltpu.CompilerParams(
            collective_id=collective_id, has_side_effects=True, vmem_limit_bytes=56 * 2**20
        ),
        cost_estimate=pl.CostEstimate(flops=0, bytes_accessed=48 * 2**20, transcendentals=0),
    )(*operands)


def place():
    r = lax.axis_index("row")
    c = lax.axis_index("col")
    h = lax.rem(r, 2)
    return r, c, h, lax.div(r, 2), r + 1 - 2 * h


class Links:
    def __init__(self, send_sem, recv_sem, first=0):
        self.send_sem = send_sem
        self.recv_sem = recv_sem
        self.slot = first
        self.copies = []
        self.open = []

    def go(self, source, target, device):
        copy = Copy(source, target, self.send_sem, self.recv_sem, self.slot, device)
        copy.start()
        self.slot += 1
        self.copies.append(copy)
        self.open.append(copy)
        return copy

    def arrive(self, copy):
        copy.wait_recv()
        self.open = [other for other in self.open if other is not copy]

    def finish(self):
        for copy in self.open:
            copy.wait_recv()
        for copy in self.copies:
            copy.wait_send()


RING = 14


def ring_at(axis):
    r, c, h, q, _ = place()
    here = q if axis == "row" else c
    step_z = 1 - 2 * lax.rem(here, 2)
    chips = {
        "p": lax.rem(here + 2, 8),
        "m": lax.rem(here + 6, 8),
        "z": here + step_z,
        "o": lax.rem(here + 4, 8),
        "pz": lax.rem(here + 2, 8) + step_z,
        "mz": lax.rem(here + 6, 8) + step_z,
        "oz": lax.rem(here + 4, 8) + step_z,
    }
    devices = {
        side: (2 * chips[side] + h, c) if axis == "row" else (r, chips[side]) for side in "pmz"
    }
    return here, chips, devices


def ring_peers(axis):
    return list(ring_at(axis)[2].values())


def ring(links, axis, slot, own=None, which=(0, 1), ready=None, seen=None, heavy=None, at=None):
    here, chips, to = at or ring_at(axis)
    heavy = axis == "row" if heavy is None else heavy
    seen = seen or (lambda chip, half: None)

    def take(copy, chip, half):
        links.arrive(copy)
        seen(chip, half)

    def forward(chip, half, side):
        return links.go(lambda: slot(chip, half), lambda: slot(chip, half), to[side])

    first = {}
    for k in range(2):
        if ready is not None:
            ready(k)
        target = functools.partial(slot, here, which[k])
        source = functools.partial(own, k) if own is not None else target
        for side in "zpm":
            first[side, k] = links.go(source, target, to[side])
    yield
    for k in range(2):
        take(first["p", k], chips["m"], which[k])
    low = forward(chips["m"], 0, "p")
    for k in range(2):
        take(first["m", k], chips["p"], which[k])
    high = forward(chips["p"], 1, "m")
    yield
    beside = {}
    for k in range(2):
        take(first["z", k], chips["z"], which[k])
        for side in "pm":
            beside[side, k] = forward(chips["z"], which[k], side)
    yield
    if heavy:
        take(low, chips["o"], 0)
        low = forward(chips["o"], 0, "z")
        take(high, chips["o"], 1)
        high = forward(chips["o"], 1, "z")
        yield
        for k in range(2):
            take(beside["p", k], chips["mz"], which[k])
            take(beside["m", k], chips["pz"], which[k])
    else:
        take(low, chips["o"], 0)
        take(high, chips["o"], 1)
        for k in range(2):
            take(beside["p", k], chips["mz"], which[k])
        low = forward(chips["mz"], 0, "p")
        for k in range(2):
            take(beside["m", k], chips["pz"], which[k])
        high = forward(chips["pz"], 1, "m")
        yield
    take(low, chips["oz"], 0)
    take(high, chips["oz"], 1)


def together(*steps):
    active = list(steps)
    while active:
        for step in list(active):
            if next(step, StopIteration) is StopIteration:
                active.remove(step)


def aligned(index, size):
    return pl.ds(pl.multiple_of(index * size, size), size)


def start_kernel(
    square_in,
    mlp_in,
    par,
    hid,
    hx,
    wt,
    w3,
    wk,
    wv,
    wn,
    parg,
    send_sem,
    recv_sem,
    local_sem,
    square_wide,
    mlp_wide,
    square,
    mlp,
):
    r, c, h, q, sibling = place()
    rows = [lax.rem(r + d, N_ROW) for d in range(1, N_ROW)]
    cols = [lax.rem(c + d, N_COL) for d in range(1, N_COL)]

    def time_part(p):
        return square.at[pl.ds(0, 3), :, aligned(p, FEAT)]

    def key_part(p):
        return mlp.at[0, :, aligned(p, MINE)]

    def value_part(p):
        return mlp.at[1, :, aligned(p, MINE)]

    def next_part(p):
        return square.at[pl.ds(4, 3), :, aligned(p, SLICE)]

    mine = hid.at[aligned(h, MINE)]
    square_load = keep(square_in, square_wide, local_sem.at[7])
    mlp_load = keep(mlp_in, mlp_wide, local_sem.at[8])
    local = [
        keep(par, parg.at[r], local_sem.at[1]),
        keep(mine, hx.at[r], local_sem.at[2]),
    ]
    greet([(p, c) for p in rows] + [(r, p) for p in cols])
    links = Links(send_sem, recv_sem)
    times = []
    own_time = []
    other = links.go(hid.at[aligned(1 - h, MINE)], hx.at[r], (sibling, c))

    def hid_own(k):
        return (mine, hx.at[sibling])[k]

    def hid_ready(k):
        if k == 1:
            links.arrive(other)

    def time_ready(k):
        if k == 0:
            for copy in times:
                links.arrive(copy)
            links.go(wt.at[h, :, :, c], wt.at[h, :, :, c], (sibling, c))

    def time_slot(chip, half):
        return wt.at[h, :, pl.ds(8 * half, 8), chip]

    def time_seen(chip, half):
        links.go(time_slot(chip, half), time_slot(chip, half), (sibling, c))

    def out_slot(chip, half):
        return w3.at[chip, :, pl.ds(1024 * half, 1024)]

    def out_own(k):
        return square.at[3, :, pl.ds(1024 * k, 1024)]

    def feed():
        square_load.wait()
        for j in range(3):
            square[j] = square_wide[j].astype(BF16)
        for p in rows:
            times.append(links.go(time_part(p), wt.at[lax.rem(p, 2), :, r, c], (p, c)))
        own_time.append(keep(time_part(r), wt.at[h, :, r, c], local_sem.at[0]))
        yield

    def casts():
        for j in range(3, 7):
            square[j] = square_wide[j].astype(BF16)
        mlp_load.wait()
        mlp[...] = mlp_wide[...].astype(BF16)
        own_time[0].wait()
        yield

    def rest():
        local.extend(
            [
                keep(square.at[3], w3.at[c], local_sem.at[3]),
                keep(key_part(r), wk.at[c, r], local_sem.at[4]),
                keep(value_part(r), wv.at[c, r], local_sem.at[5]),
                keep(next_part(c), wn.at[r, c], local_sem.at[6]),
            ]
        )
        for p in rows:
            links.go(par, parg.at[r], (p, c))
        yield
        for p in rows:
            links.go(key_part(p), wk.at[c, r], (p, c))
        for p in cols:
            links.go(next_part(p), wn.at[r, c], (r, p))
        for p in rows:
            links.go(value_part(p), wv.at[c, r], (p, c))

    together(
        feed(),
        ring(
            links,
            "row",
            lambda chip, side: hx.at[2 * chip + side],
            own=hid_own,
            which=(h, 1 - h),
            ready=hid_ready,
        ),
        casts(),
        ring(links, "col", time_slot, ready=time_ready, seen=time_seen),
        rest(),
        ring(links, "col", out_slot, own=out_own),
    )
    links.finish()
    for copy in local:
        copy.wait()


def dot(a, b, dims=((1,), (0,))):
    return lax.dot_general(a, b, (dims, ((), ())), preferred_element_type=F32)


def split(x):
    high = x.astype(BF16)
    return high, (x - high.astype(F32)).astype(BF16)


def dot3(a, b, dims=((1,), (0,))):
    a_high, a_low = a
    b_high, b_low = b
    return dot(a_high, b_high, dims) + (dot(a_high, b_low, dims) + dot(a_low, b_high, dims))


def norm(source, gain, bias):
    center = jnp.sum(source, axis=-1, keepdims=True) / WIDTH
    second = jnp.sum(source * source, axis=-1, keepdims=True) / WIDTH
    scaled = (source - center) * lax.rsqrt(second - center * center + 1e-05)
    return (scaled * gain + bias).astype(BF16).astype(F32)


def row_of(par, i):
    return jnp.concatenate([par[j, i : i + 1, :] for j in range(N_ROW)], axis=1)


def step_back(z):
    position = lax.rem(lax.broadcasted_iota(jnp.int32, z.shape, 0), LMAX)
    return jnp.where(position == 0, 0.0, pltpu.roll(z, 1, 0)) - z


def one_prompt(prompt, lens, rkv, low, coef, up, att, final):
    r, c, h, q, _ = place()
    length = lens[c * 8 + h * 4 + prompt]
    tokens = aligned(prompt, LMAX)
    wide = SLICE
    channels = aligned(q, SLICE)
    heads = wide // HEAD
    live = (lax.broadcasted_iota(jnp.int32, (LMAX, wide), 0) < length).astype(F32)
    lane = lax.broadcasted_iota(jnp.int32, (LMAX, wide), 1) // HEAD
    t = lax.broadcasted_iota(jnp.int32, (LMAX, LMAX), 0)
    u = lax.broadcasted_iota(jnp.int32, (LMAX, LMAX), 1)
    seg = (
        lax.broadcasted_iota(jnp.int32, (wide, wide), 0) // HEAD
        == lax.broadcasted_iota(jnp.int32, (wide, wide), 1) // HEAD
    ).astype(F32).astype(BF16)
    lower = (t >= u).astype(F32).astype(BF16)

    def head_sum(x):
        high, low_part = split(x)
        return dot(high, seg) + dot(low_part, seg)

    def only(x, k):
        return jnp.where(lane == k, x, jnp.zeros_like(x))

    receptance, key, value = rkv[0], rkv[1], rkv[2]
    decay = (
        -0.606531
        * jax.nn.sigmoid(coef[0:1, channels] + dot(jnp.tanh(low[0]).astype(BF16), up[0, :, channels]))
        * live
    )
    rate = jax.nn.sigmoid(coef[1:2, channels] + dot(low[1].astype(BF16), up[1, :, channels]))
    kappa = key * coef[2:3, channels]
    kappa = kappa * lax.rsqrt(head_sum(kappa * kappa) + 1e-05)
    remove = -kappa * live
    write = kappa * rate * live
    key = key * live
    value = value * live
    d_high, d_rest = split(decay)
    d_mid, d_low = split(decay - d_high.astype(F32))
    total = dot(lower, d_high) + (dot(lower, d_mid) + dot(lower, d_low))
    middle = total[LMAX // 2 - 1 : LMAX // 2, :]
    last = total[LMAX - 1 : LMAX, :]
    back = jnp.exp(middle - total)
    pull = split(remove * jnp.exp(total - decay - middle))
    read = split(receptance * jnp.exp(total - middle))
    write_back = split(write * back)
    key_back = split(key * back)
    value_parts = split(value)

    left = tuple(
        jnp.concatenate([x for k in range(heads) for x in (only(pull[i], k), only(read[i], k))])
        for i in range(2)
    )
    right = tuple(jnp.concatenate([write_back[i], key_back[i]]) for i in range(2))
    pairs = dot3(left, right, ((1,), (1,)))
    strict = t > u
    t2 = lax.broadcasted_iota(jnp.int32, (LMAX, 2 * LMAX), 0)
    u2 = lax.rem(lax.broadcasted_iota(jnp.int32, (LMAX, 2 * LMAX), 1), LMAX)
    upto = t2 >= u2
    solves, pull_key, reads = [], [], []
    for k in range(heads):
        base = k * 2 * LMAX
        system = jnp.where(strict, pairs[base : base + LMAX, :LMAX], 0.0)
        pull_key.append(split(jnp.where(strict, pairs[base : base + LMAX, LMAX:], 0.0)))
        reads.append(split(jnp.where(upto, pairs[base + LMAX : base + 2 * LMAX], 0.0)))
        solves.append(system)
    inverse = []
    for k in range(heads):
        near = (t // 2 == u // 2)
        inverse.append(
            jnp.where(near, solves[k], 0.0) + (t == u).astype(F32)
        )
    size = 2
    while size < LMAX:
        inside = (t // (2 * size) == u // (2 * size)) & (t // size != u // size)
        grown = []
        for k in range(heads):
            known = split(inverse[k])
            cross = split(jnp.where(inside, solves[k], 0.0))
            product = split(dot3(known, cross))
            grown.append(inverse[k] + dot3(product, known))
        inverse = grown
        size *= 2

    def across(mats, parts):
        wide_left = tuple(jnp.concatenate([mat[i] for mat in mats], axis=1) for i in range(2))
        tall = tuple(
            jnp.concatenate([only(part[i], k) for k in range(heads) for part in parts])
            for i in range(2)
        )
        return dot3(wide_left, tall)

    start = across(pull_key, [value_parts])
    pulled = split(across([split(x) for x in inverse], [split(start)]))
    output = across(reads, [pulled, value_parts])
    tail = jnp.exp(last - total)
    write_tail = split(write * tail)
    key_tail = split(key * tail)
    tall = tuple(jnp.concatenate([pulled[i], value_parts[i]]) for i in range(2))
    tails = tuple(jnp.concatenate([write_tail[i], key_tail[i]]) for i in range(2))
    state = dot3(tall, tails, ((0,), (0,)))
    even = lax.broadcasted_iota(jnp.int32, (HEAD, FEAT), 1) < HEAD
    for k in range(heads // 2):
        lanes = slice(k * FEAT, (k + 1) * FEAT)
        final[prompt, k] = jnp.where(
            even,
            state[k * FEAT : k * FEAT + HEAD, lanes],
            state[k * FEAT + HEAD : (k + 1) * FEAT, lanes],
        ).astype(BF16)
    bonus = head_sum(receptance * key * coef[3:4, channels])
    out = (output + bonus * value) * live
    center = head_sum(out) * (1.0 / HEAD)
    out = out - center
    spread = head_sum(out * out) * (1.0 / HEAD)
    out = (out * lax.rsqrt(spread + 0.00064) * coef[4:5, channels] + coef[5:6, channels]).astype(BF16)
    for side in range(2):
        att[side, tokens] = out[:, side * FEAT : (side + 1) * FEAT]


PROMPTS = MINE // LMAX
HOPS = 9


class PromptRing:
    def __init__(self, send_sem, recv_sem, base, axis, own, got):
        self.send_sem = send_sem
        self.recv_sem = recv_sem
        self.base = base
        self.here, self.chips, self.to = ring_at(axis)
        self.own = own
        self.got = got

    def hop(self, m, slot, chip, side, half=None):
        def block():
            at = self.chips.get(chip, self.here)
            if half is None:
                return self.got.at[pl.ds(2 * at, 2), aligned(m, LMAX)]
            return self.got.at[2 * at + half, aligned(m, LMAX)]

        def source():
            if chip == "own" and self.own is not None:
                return self.own.at[:, aligned(m, LMAX)]
            return block()

        return Copy(
            source,
            block,
            self.send_sem,
            self.recv_sem,
            self.base + m * HOPS + slot,
            self.to[side],
        )

    def hops(self, m):
        return [
            self.hop(m, 0, "own", "p"),
            self.hop(m, 1, "own", "m"),
            self.hop(m, 2, "own", "z"),
            self.hop(m, 3, "m", "p", 0),
            self.hop(m, 4, "p", "m", 1),
            self.hop(m, 5, "z", "p"),
            self.hop(m, 6, "z", "m"),
            self.hop(m, 7, "o", "z", 0),
            self.hop(m, 8, "o", "z", 1),
        ]

    def begin(self, m):
        copies = self.hops(m)
        for k in (2, 0, 1):
            copies[k].start()

    def forward(self, m):
        copies = self.hops(m)
        copies[0].wait_recv()
        copies[3].start()
        copies[1].wait_recv()
        copies[4].start()
        copies[2].wait_recv()
        copies[5].start()
        copies[6].start()

    def close(self, m):
        copies = self.hops(m)
        copies[3].wait_recv()
        copies[7].start()
        copies[4].wait_recv()
        copies[8].start()

    def last(self, m):
        for k in (5, 6, 7, 8):
            self.hops(m)[k].wait_recv()

    def sent(self, m):
        for copy in self.hops(m):
            copy.wait_send()


N_SUM = PROMPTS * (N_ROW - 1)
N_TURN = N_SUM + 2 * PROMPTS
N_STATE = N_TURN + 1
N_WEIGHT = N_STATE + 3 * PROMPTS * HOPS
N_ALL = N_WEIGHT + 1 + 2 * (1 + 14 + RING) + 1 + 14 + RING


def body_kernel(
    lens,
    hx,
    par,
    shift,
    wt,
    down,
    coef,
    up,
    w3,
    wk,
    wv,
    wn,
    out,
    next_rkv,
    final,
    send_sem,
    recv_sem,
    local_sem,
    rkv,
    low,
    state,
    att,
    attg,
    w3x,
    mid,
    midg,
    held,
    theirs,
    act_scr,
    part,
    got,
    nx,
    wng,
):
    r, c, h, q, sibling = place()
    rows = [lax.rem(r + d, N_ROW) for d in range(1, N_ROW)]

    def local():
        return [
            pltpu.make_async_copy(wk.at[c], held.at[0, :, c], local_sem.at[0]),
            pltpu.make_async_copy(wv.at[c], held.at[1, :, c], local_sem.at[1]),
            pltpu.make_async_copy(wn.at[r], wng.at[r], local_sem.at[2]),
        ]

    for copy in local():
        copy.start()

    def target(i):
        return (2 * c + lax.rem(h + i, 2), q)

    barrier = pltpu.get_barrier_semaphore()
    peers = [(p, c) for p in rows] + ring_peers("col")

    @pl.when(q != c)
    def _():
        for i in range(2):
            pl.semaphore_signal(barrier, inc=1, device_id=target(i), device_id_type=MESH)

    for device in peers:
        pl.semaphore_signal(barrier, inc=1, device_id=device, device_id_type=MESH)
    pl.semaphore_wait(barrier, len(peers) + 2 * (q != c).astype(jnp.int32))

    links = Links(send_sem, recv_sem, N_WEIGHT)
    links.go(w3, w3x, (sibling, c))

    col_place = ring_at("col")

    def mlp_ring(which, source):
        def slot(chip, half):
            return held.at[which, pl.ds(8 * half, 8), chip]

        def over(chip, half):
            return theirs.at[which, pl.ds(8 * half, 8), chip]

        def seen(chip, half):
            links.go(lambda: slot(chip, half), lambda: over(chip, half), (sibling, c))

        def begin():
            links.go(lambda: source.at[c], lambda: theirs.at[which, :, c], (sibling, c))
            yield from ring(
                links,
                "col",
                slot,
                own=lambda k: source.at[c, pl.ds(8 * k, 8)],
                seen=seen,
                at=col_place,
            )

        return begin()

    def weight_slot(chip, half):
        return wng.at[2 * chip + h, pl.ds(4 * half, 4)]

    far_links = Links(send_sem, recv_sem, N_ALL - 1 - 14 - RING)

    def weight_seen(chip, half):
        far_links.go(
            lambda: weight_slot(chip, half), lambda: weight_slot(chip, half), (sibling, c)
        )

    def weight_ring():
        far_links.go(lambda: wn.at[r], lambda: wng.at[r], (sibling, c))
        yield from ring(
            far_links,
            "row",
            weight_slot,
            own=lambda k: wn.at[r, pl.ds(4 * k, 4)],
            seen=weight_seen,
        )

    keys = mlp_ring(0, wk)
    values = mlp_ring(1, wv)
    weights = weight_ring()
    next(weights)
    next(keys)

    att_ring = PromptRing(send_sem, recv_sem, N_STATE, "row", att, attg)
    mid_ring = PromptRing(send_sem, recv_sem, N_STATE + PROMPTS * HOPS, "row", mid, midg)
    out_ring = PromptRing(send_sem, recv_sem, N_STATE + 2 * PROMPTS * HOPS, "col", None, nx)
    move_state = Copy(state, final, send_sem, recv_sem, N_TURN, target(0))

    def wide(ref, m):
        return jnp.concatenate([ref[j, aligned(m, LMAX), :] for j in range(N_ROW)], axis=1)

    def normed(ref, m, k):
        return norm(wide(ref, m).astype(F32), row_of(par, k), row_of(par, k + 1))

    def blends(m):
        z = normed(hx, m, 0)
        dz = step_back(z)
        for j in range(5):
            blend = (z + dz * shift[j : j + 1, :]).astype(BF16)
            if j < 3:
                weight = jnp.concatenate(
                    [wt[side, j].reshape(WIDTH, FEAT) for side in range(2)], axis=1
                )
                rkv[j] = dot(blend, weight)
            else:
                low[j - 3] = dot(blend, down[j - 3], ((1,), (1,)))

    def core(m):
        one_prompt(m, lens, rkv, low, coef, up, att, state)
        att_ring.begin(m)
        for side in range(2):
            attg[2 * q + side, aligned(m, LMAX)] = att[side, aligned(m, LMAX)]

    def project(m):
        att_ring.last(m)
        tokens = aligned(m, LMAX)
        weight = jnp.concatenate([w[...].reshape(FEAT, WIDTH) for w in (w3, w3x)])
        total = dot(wide(attg, m), weight, ((1,), (1,)))
        for k, side in enumerate((h, 1 - h)):
            block = (
                hx[r - h + side, tokens, :].astype(F32) + total[:, k * FEAT : (k + 1) * FEAT]
            ).astype(BF16)
            mid[side, tokens, :] = block
            midg[r - h + side, tokens, :] = block
        mid_ring.begin(m)

    def sums(m):
        def copy_of(i, p):
            return Copy(
                lambda: part.at[p, aligned(m, LMAX)],
                lambda: got.at[r, aligned(m, LMAX)],
                send_sem,
                recv_sem,
                m * (N_ROW - 1) + i,
                (p, c),
            )

        return [copy_of(i, p) for i, p in enumerate(rows)]

    def channel(m):
        mid_ring.last(m)
        tokens = aligned(m, LMAX)
        z = normed(midg, m, 2)
        blend = (z + step_back(z) * shift[5:6, :]).astype(BF16)
        for side, weight in enumerate((held, theirs)):
            act = jnp.square(jnp.maximum(dot(blend, weight[0].reshape(WIDTH, MINE)), 0.0))
            act_scr[side] = act.astype(BF16)

        @pl.loop(0, N_CHIP)
        def _(n):
            total = None
            for side, weight in enumerate((held, theirs)):
                rows_n = weight[1, pl.ds(2 * n, 2)].reshape(SLICE, MINE)
                term = dot(act_scr[side], rows_n, ((1,), (1,)))
                total = term if total is None else total + term
            for side in range(2):
                added = jnp.where(n == q, mid[side, tokens, :].astype(F32), 0.0)
                part[2 * n + side, tokens, :] = (
                    total[:, side * FEAT : (side + 1) * FEAT] + added
                ).astype(BF16)

        for copy in sums(m):
            copy.start()
        got[r, tokens, :] = part[r, tokens, :]

    def source_rows(m, i):
        return pl.ds(pl.multiple_of(lax.rem(h + i, 2) * MINE + m * LMAX, LMAX), LMAX)

    def turn(m, i):
        return pltpu.make_async_remote_copy(
            src_ref=out.at[source_rows(m, i)],
            dst_ref=nx.at[2 * q + h, aligned(m, LMAX)],
            send_sem=send_sem.at[N_SUM + 2 * m + i],
            recv_sem=recv_sem.at[N_SUM + 2 * m + h],
            device_id=target(i),
            device_id_type=MESH,
        )

    def add_up(m):
        for copy in sums(m):
            copy.wait_recv()
        tokens = aligned(m, LMAX)
        for side in range(2):
            total = got[side, tokens, :].astype(F32)
            for k in range(1, N_CHIP):
                total += got[2 * k + side, tokens, :].astype(F32)
            rows_m = pl.ds(pl.multiple_of(side * MINE + m * LMAX, LMAX), LMAX)
            out[rows_m, :] = total.astype(BF16)

        @pl.when(q == c)
        def _():
            keep(
                out.at[source_rows(m, 0)],
                nx.at[r, aligned(m, LMAX)],
                recv_sem.at[N_SUM + 2 * m + h],
            )

        @pl.when(q != c)
        def _():
            turn(m, 0).start()

        turn(m, 1).start()

    def spread(m):
        for k in range(2):
            block = nx.at[2 * c + k, aligned(m, LMAX)]
            pltpu.make_async_copy(block, block, recv_sem.at[N_SUM + 2 * m + k]).wait()
        out_ring.begin(m)

    def project_next(m):
        out_ring.last(m)
        z = normed(nx, m, 4)
        dz = step_back(z)
        for j in range(3):
            blend = (z + dz * shift[6 + j : 7 + j, :]).astype(BF16)
            next_rkv[j, aligned(m, LMAX), :] = dot(
                blend, wng[:, :, j].reshape(WIDTH, SLICE)
            ).astype(BF16)

    stages = (
        blends,
        core,
        att_ring.forward,
        att_ring.close,
        project,
        mid_ring.forward,
        mid_ring.close,
        channel,
        add_up,
        spread,
        out_ring.forward,
        out_ring.close,
        project_next,
    )
    end = object()

    def wait_mlp():
        for copy in local():
            copy.wait()
        for copy in links.open:
            copy.wait_recv()
        links.open = []

    def send_state():
        @pl.when(q == c)
        def _():
            keep(state, final, recv_sem.at[N_TURN])

        @pl.when(q != c)
        def _():
            move_state.start()

    def wait_far():
        for copy in far_links.open:
            copy.wait_recv()
        far_links.open = []

    beside = {
        1: [weights, keys],
        2: [keys, values],
        3: [weights, keys, values, lambda: links.arrive(links.copies[0])],
        4: [keys, values],
        5: [weights, values],
        6: [values],
        7: [send_state, wait_mlp],
        8: [weights],
        12: [wait_far],
    }
    middle = stages.index(channel)

    def run(t, first, end_at):
        for lag in range(first, end_at):
            since = t - lag

            @pl.when((since >= 0) & (since < 2 * PROMPTS) & (lax.rem(t + lag, 2) == 0))
            def _():
                stages[lag](lax.div(since, 2))

    @pl.loop(0, 2 * PROMPTS + len(stages) - 2)
    def _(t):
        run(t, 0, middle)
        for at, works in beside.items():

            @pl.when(t == at)
            def _():
                for work in works:
                    if callable(work):
                        work()
                    else:
                        next(work, end)

        run(t, middle, len(stages))

    @pl.loop(0, PROMPTS)
    def _(m):
        for copy in sums(m):
            copy.wait_send()
        for prompt_ring in (att_ring, mid_ring, out_ring):
            prompt_ring.sent(m)

        @pl.when(q != c)
        def _():
            turn(m, 0).wait_send()

        turn(m, 1).wait_send()

    pltpu.make_async_copy(state, final, recv_sem.at[N_TURN]).wait()

    @pl.when(q != c)
    def _():
        move_state.wait_send()

    for copy in links.copies + far_links.copies:
        copy.wait_send()


def per_device(
    hidden,
    lengths,
    square_matrix_shards,
    channel_mix_shards,
    lowrank_down,
    lowrank_up,
    token_shift_weights,
    attention_coefficients,
    norm_parameters,
):
    hx, wt, w3, wk, wv, wn, parg = exchange(
        start_kernel,
        [
            ((N_ROW, MINE, FEAT), BF16),
            ((2, 3, N_ROW, N_COL, 16, FEAT), BF16),
            ((N_COL, 16, WIDTH), BF16),
            ((N_COL, N_ROW, 16, MINE), BF16),
            ((N_COL, N_ROW, 16, MINE), BF16),
            ((N_ROW, N_COL, 3, 16, SLICE), BF16),
            ((N_ROW, 6, FEAT), F32),
        ],
        15 + 1 + 3 * RING + 1 + 14 + 15 + 15 + 7 + 15,
        9,
        1,
        square_matrix_shards,
        channel_mix_shards,
        norm_parameters,
        hidden,
        scratch=[
            pltpu.VMEM(square_matrix_shards.shape, F32),
            pltpu.VMEM(channel_mix_shards.shape, F32),
            pltpu.VMEM(square_matrix_shards.shape, BF16),
            pltpu.VMEM(channel_mix_shards.shape, BF16),
        ],
    )
    lowrank = lowrank_down.shape[2]
    out_hidden, next_rkv, final = exchange(
        body_kernel,
        [
            ((2 * MINE, FEAT), BF16),
            ((3, MINE, SLICE), BF16),
            ((PROMPTS, 2, HEAD, FEAT), BF16),
        ],
        N_ALL,
        3,
        2,
        lengths,
        hx,
        parg,
        token_shift_weights,
        wt,
        lowrank_down.transpose(0, 2, 1),
        attention_coefficients,
        lowrank_up,
        w3,
        wk,
        wv,
        wn,
        scratch=[
            pltpu.VMEM((3, LMAX, SLICE), F32),
            pltpu.VMEM((2, LMAX, lowrank), F32),
            pltpu.VMEM((PROMPTS, 2, HEAD, FEAT), BF16),
            pltpu.VMEM((2, MINE, FEAT), BF16),
            pltpu.VMEM((N_ROW, MINE, FEAT), BF16),
            pltpu.VMEM((N_COL, 16, WIDTH), BF16),
            pltpu.VMEM((2, MINE, FEAT), BF16),
            pltpu.VMEM((N_ROW, MINE, FEAT), BF16),
            pltpu.VMEM((2, N_ROW, N_COL, 16, MINE), BF16),
            pltpu.VMEM((2, N_ROW, N_COL, 16, MINE), BF16),
            pltpu.VMEM((2, LMAX, MINE), BF16),
            pltpu.VMEM((N_ROW, MINE, FEAT), BF16),
            pltpu.VMEM((N_ROW, MINE, FEAT), BF16),
            pltpu.VMEM((N_ROW, MINE, FEAT), BF16),
            pltpu.VMEM((N_ROW, N_COL, 3, 16, SLICE), BF16),
        ],
        in_specs=[pl.BlockSpec(memory_space=pltpu.SMEM)] + [VMEM] * 8 + [ANY] * 3,
        out_specs=[VMEM, VMEM, ANY],
    )
    final = final.reshape(4, 2, HEAD, 2, HEAD).transpose(0, 1, 3, 2, 4).astype(F32)
    final_state = final.reshape(4, 4, HEAD * HEAD)
    return (out_hidden, next_rkv, final_state)


def solution(mesh):
    return jax.shard_map(
        per_device,
        mesh=mesh,
        in_specs=(
            P("col", "row"),
            P(),
            P(None, ("row", "col"), None),
            P(None, ("row", "col"), None),
            P(),
            P(),
            P(),
            P(),
            P(None, "row"),
        ),
        out_specs=(P("col", "row"), P(None, "row", "col"), P("row", "col", None)),
        check_vma=False,
    )
```

```python
import functools

import jax
import jax.numpy as jnp
from jax import lax
from jax.experimental import pallas as pl
from jax.experimental.pallas import tpu as pltpu
from jax.sharding import PartitionSpec as P

WIDTH = 2048
HEAD = 64
LMAX = 128
F32 = jnp.float32
BF16 = jnp.bfloat16
MESH = pl.DeviceIdType.MESH
ANY = pl.BlockSpec(memory_space=pl.ANY)
VMEM = pl.BlockSpec(memory_space=pltpu.VMEM)
N_ROW = 16
N_COL = 8
N_CHIP = 8
MINE = 512
FEAT = 128
SLICE = 256


def greet(devices):
    barrier = pltpu.get_barrier_semaphore()
    for device in devices:
        pl.semaphore_signal(barrier, inc=1, device_id=device, device_id_type=MESH)
    pl.semaphore_wait(barrier, len(devices))


class Copy:
    def __init__(self, source, target, send_sem, recv_sem, slot, device):
        self.made = lambda: pltpu.make_async_remote_copy(
            src_ref=source() if callable(source) else source,
            dst_ref=target() if callable(target) else target,
            send_sem=send_sem.at[slot],
            recv_sem=recv_sem.at[slot],
            device_id=device,
            device_id_type=MESH,
        )

    def start(self):
        self.made().start()

    def wait_recv(self):
        self.made().wait_recv()

    def wait_send(self):
        self.made().wait_send()


def keep(source, target, sem):
    copy = pltpu.make_async_copy(source, target, sem)
    copy.start()
    return copy


def exchange(
    kernel,
    outs,
    n_remote,
    n_local,
    collective_id,
    *operands,
    scratch=(),
    in_specs=None,
    out_specs=None,
):
    return pl.pallas_call(
        kernel,
        out_shape=[jax.ShapeDtypeStruct(*out) for out in outs],
        in_specs=in_specs or [ANY] * len(operands),
        out_specs=out_specs or [ANY] * len(outs),
        scratch_shapes=[
            pltpu.SemaphoreType.DMA((n_remote,)),
            pltpu.SemaphoreType.DMA((n_remote,)),
            pltpu.SemaphoreType.DMA((n_local,)),
            *scratch,
        ],
        compiler_params=pltpu.CompilerParams(
            collective_id=collective_id, has_side_effects=True, vmem_limit_bytes=56 * 2**20
        ),
        cost_estimate=pl.CostEstimate(flops=0, bytes_accessed=48 * 2**20, transcendentals=0),
    )(*operands)


def place():
    r = lax.axis_index("row")
    c = lax.axis_index("col")
    h = lax.rem(r, 2)
    return r, c, h, lax.div(r, 2), r + 1 - 2 * h


class Links:
    def __init__(self, send_sem, recv_sem, first=0):
        self.send_sem = send_sem
        self.recv_sem = recv_sem
        self.slot = first
        self.copies = []
        self.open = []

    def go(self, source, target, device):
        copy = Copy(source, target, self.send_sem, self.recv_sem, self.slot, device)
        copy.start()
        self.slot += 1
        self.copies.append(copy)
        self.open.append(copy)
        return copy

    def arrive(self, copy):
        copy.wait_recv()
        self.open = [other for other in self.open if other is not copy]

    def finish(self):
        for copy in self.open:
            copy.wait_recv()
        for copy in self.copies:
            copy.wait_send()


RING = 14


def ring_at(axis):
    r, c, h, q, _ = place()
    here = q if axis == "row" else c
    step_z = 1 - 2 * lax.rem(here, 2)
    chips = {
        "p": lax.rem(here + 2, 8),
        "m": lax.rem(here + 6, 8),
        "z": here + step_z,
        "o": lax.rem(here + 4, 8),
        "pz": lax.rem(here + 2, 8) + step_z,
        "mz": lax.rem(here + 6, 8) + step_z,
        "oz": lax.rem(here + 4, 8) + step_z,
    }
    devices = {
        side: (2 * chips[side] + h, c) if axis == "row" else (r, chips[side]) for side in "pmz"
    }
    return here, chips, devices


def ring_peers(axis):
    return list(ring_at(axis)[2].values())


def ring(links, axis, slot, own=None, which=(0, 1), ready=None, seen=None, heavy=None, at=None):
    here, chips, to = at or ring_at(axis)
    heavy = axis == "row" if heavy is None else heavy
    seen = seen or (lambda chip, half: None)

    def take(copy, chip, half):
        links.arrive(copy)
        seen(chip, half)

    def forward(chip, half, side):
        return links.go(lambda: slot(chip, half), lambda: slot(chip, half), to[side])

    first = {}
    for k in range(2):
        if ready is not None:
            ready(k)
        target = functools.partial(slot, here, which[k])
        source = functools.partial(own, k) if own is not None else target
        for side in "zpm":
            first[side, k] = links.go(source, target, to[side])
    yield
    for k in range(2):
        take(first["p", k], chips["m"], which[k])
    low = forward(chips["m"], 0, "p")
    for k in range(2):
        take(first["m", k], chips["p"], which[k])
    high = forward(chips["p"], 1, "m")
    yield
    beside = {}
    for k in range(2):
        take(first["z", k], chips["z"], which[k])
        for side in "pm":
            beside[side, k] = forward(chips["z"], which[k], side)
    yield
    if heavy:
        take(low, chips["o"], 0)
        low = forward(chips["o"], 0, "z")
        take(high, chips["o"], 1)
        high = forward(chips["o"], 1, "z")
        yield
        for k in range(2):
            take(beside["p", k], chips["mz"], which[k])
            take(beside["m", k], chips["pz"], which[k])
    else:
        take(low, chips["o"], 0)
        take(high, chips["o"], 1)
        for k in range(2):
            take(beside["p", k], chips["mz"], which[k])
        low = forward(chips["mz"], 0, "p")
        for k in range(2):
            take(beside["m", k], chips["pz"], which[k])
        high = forward(chips["pz"], 1, "m")
        yield
    take(low, chips["oz"], 0)
    take(high, chips["oz"], 1)


def together(*steps):
    active = list(steps)
    while active:
        for step in list(active):
            if next(step, StopIteration) is StopIteration:
                active.remove(step)


def aligned(index, size):
    return pl.ds(pl.multiple_of(index * size, size), size)


def start_kernel(
    square_in,
    mlp_in,
    par,
    hid,
    hx,
    wt,
    w3,
    wk,
    wv,
    wn,
    parg,
    send_sem,
    recv_sem,
    local_sem,
    square_wide,
    mlp_wide,
    square,
    mlp,
):
    r, c, h, q, sibling = place()
    rows = [lax.rem(r + d, N_ROW) for d in range(1, N_ROW)]
    cols = [lax.rem(c + d, N_COL) for d in range(1, N_COL)]

    def time_part(p):
        return square.at[pl.ds(0, 3), :, aligned(p, FEAT)]

    def key_part(p):
        return mlp.at[0, :, aligned(p, MINE)]

    def value_part(p):
        return mlp.at[1, :, aligned(p, MINE)]

    def next_part(p):
        return square.at[pl.ds(4, 3), :, aligned(p, SLICE)]

    mine = hid.at[aligned(h, MINE)]
    square_load = keep(square_in, square_wide, local_sem.at[7])
    mlp_load = keep(mlp_in, mlp_wide, local_sem.at[8])
    local = [
        keep(par, parg.at[r], local_sem.at[1]),
        keep(mine, hx.at[r], local_sem.at[2]),
    ]
    greet([(p, c) for p in rows] + [(r, p) for p in cols])
    links = Links(send_sem, recv_sem)
    times = []
    own_time = []
    other = links.go(hid.at[aligned(1 - h, MINE)], hx.at[r], (sibling, c))

    def hid_own(k):
        return (mine, hx.at[sibling])[k]

    def hid_ready(k):
        if k == 1:
            links.arrive(other)

    def time_ready(k):
        if k == 0:
            for copy in times:
                links.arrive(copy)
            links.go(wt.at[h, :, :, c], wt.at[h, :, :, c], (sibling, c))

    def time_slot(chip, half):
        return wt.at[h, :, pl.ds(8 * half, 8), chip]

    def time_seen(chip, half):
        links.go(time_slot(chip, half), time_slot(chip, half), (sibling, c))

    def out_slot(chip, half):
        return w3.at[chip, :, pl.ds(1024 * half, 1024)]

    def out_own(k):
        return square.at[3, :, pl.ds(1024 * k, 1024)]

    def feed():
        square_load.wait()
        for j in range(3):
            square[j] = square_wide[j].astype(BF16)
        for p in rows:
            times.append(links.go(time_part(p), wt.at[lax.rem(p, 2), :, r, c], (p, c)))
        own_time.append(keep(time_part(r), wt.at[h, :, r, c], local_sem.at[0]))
        yield

    def casts():
        for j in range(3, 7):
            square[j] = square_wide[j].astype(BF16)
        mlp_load.wait()
        mlp[...] = mlp_wide[...].astype(BF16)
        own_time[0].wait()
        yield

    nexts = []

    def next_slot(chip, half):
        return wn.at[2 * chip + h, pl.ds(4 * half, 4)]

    def next_seen(chip, half):
        links.go(lambda: next_slot(chip, half), lambda: next_slot(chip, half), (sibling, c))

    def next_ready(k):
        if k == 0:
            for copy in nexts:
                links.arrive(copy)
            own_next[0].wait()
            links.go(wn.at[r], wn.at[r], (sibling, c))

    own_next = []

    def rest():
        local.extend(
            [
                keep(square.at[3], w3.at[c], local_sem.at[3]),
                keep(key_part(r), wk.at[c, r], local_sem.at[4]),
                keep(value_part(r), wv.at[c, r], local_sem.at[5]),
            ]
        )
        own_next.append(keep(next_part(c), wn.at[r, c], local_sem.at[6]))
        for p in cols:
            nexts.append(links.go(next_part(p), wn.at[r, c], (r, p)))
        for p in rows:
            links.go(par, parg.at[r], (p, c))
        yield
        for p in rows:
            links.go(key_part(p), wk.at[c, r], (p, c))
        for p in rows:
            links.go(value_part(p), wv.at[c, r], (p, c))

    together(
        feed(),
        ring(
            links,
            "row",
            lambda chip, side: hx.at[2 * chip + side],
            own=hid_own,
            which=(h, 1 - h),
            ready=hid_ready,
        ),
        casts(),
        ring(links, "col", time_slot, ready=time_ready, seen=time_seen),
        rest(),
        ring(links, "col", out_slot, own=out_own),
        ring(links, "row", next_slot, ready=next_ready, seen=next_seen),
    )
    links.finish()
    for copy in local:
        copy.wait()


def dot(a, b, dims=((1,), (0,))):
    return lax.dot_general(a, b, (dims, ((), ())), preferred_element_type=F32)


def split(x):
    high = x.astype(BF16)
    return high, (x - high.astype(F32)).astype(BF16)


def dot3(a, b, dims=((1,), (0,))):
    a_high, a_low = a
    b_high, b_low = b
    return dot(a_high, b_high, dims) + (dot(a_high, b_low, dims) + dot(a_low, b_high, dims))


def norm(source, gain, bias):
    center = jnp.sum(source, axis=-1, keepdims=True) / WIDTH
    second = jnp.sum(source * source, axis=-1, keepdims=True) / WIDTH
    scaled = (source - center) * lax.rsqrt(second - center * center + 1e-05)
    return (scaled * gain + bias).astype(BF16).astype(F32)


def row_of(par, i):
    return jnp.concatenate([par[j, i : i + 1, :] for j in range(N_ROW)], axis=1)


def step_back(z):
    position = lax.rem(lax.broadcasted_iota(jnp.int32, z.shape, 0), LMAX)
    return jnp.where(position == 0, 0.0, pltpu.roll(z, 1, 0)) - z


def one_prompt(prompt, lens, rkv, low, coef, up, att, final):
    r, c, h, q, _ = place()
    length = lens[c * 8 + h * 4 + prompt]
    tokens = aligned(prompt, LMAX)
    wide = SLICE
    channels = aligned(q, SLICE)
    heads = wide // HEAD
    live = (lax.broadcasted_iota(jnp.int32, (LMAX, wide), 0) < length).astype(F32)
    lane = lax.broadcasted_iota(jnp.int32, (LMAX, wide), 1) // HEAD
    t = lax.broadcasted_iota(jnp.int32, (LMAX, LMAX), 0)
    u = lax.broadcasted_iota(jnp.int32, (LMAX, LMAX), 1)
    seg = (
        lax.broadcasted_iota(jnp.int32, (wide, wide), 0) // HEAD
        == lax.broadcasted_iota(jnp.int32, (wide, wide), 1) // HEAD
    ).astype(F32).astype(BF16)
    lower = (t >= u).astype(F32).astype(BF16)

    def head_sum(x):
        high, low_part = split(x)
        return dot(high, seg) + dot(low_part, seg)

    def only(x, k):
        return jnp.where(lane == k, x, jnp.zeros_like(x))

    receptance, key, value = rkv[0], rkv[1], rkv[2]
    decay = (
        -0.606531
        * jax.nn.sigmoid(coef[0:1, channels] + dot(jnp.tanh(low[0]).astype(BF16), up[0, :, channels]))
        * live
    )
    rate = jax.nn.sigmoid(coef[1:2, channels] + dot(low[1].astype(BF16), up[1, :, channels]))
    kappa = key * coef[2:3, channels]
    kappa = kappa * lax.rsqrt(head_sum(kappa * kappa) + 1e-05)
    remove = -kappa * live
    write = kappa * rate * live
    key = key * live
    value = value * live
    d_high, d_rest = split(decay)
    d_mid, d_low = split(decay - d_high.astype(F32))
    total = dot(lower, d_high) + (dot(lower, d_mid) + dot(lower, d_low))
    middle = total[LMAX // 2 - 1 : LMAX // 2, :]
    last = total[LMAX - 1 : LMAX, :]
    back = jnp.exp(middle - total)
    pull = split(remove * jnp.exp(total - decay - middle))
    read = split(receptance * jnp.exp(total - middle))
    write_back = split(write * back)
    key_back = split(key * back)
    value_parts = split(value)

    left = tuple(
        jnp.concatenate([x for k in range(heads) for x in (only(pull[i], k), only(read[i], k))])
        for i in range(2)
    )
    right = tuple(jnp.concatenate([write_back[i], key_back[i]]) for i in range(2))
    pairs = dot3(left, right, ((1,), (1,)))
    strict = t > u
    t2 = lax.broadcasted_iota(jnp.int32, (LMAX, 2 * LMAX), 0)
    u2 = lax.rem(lax.broadcasted_iota(jnp.int32, (LMAX, 2 * LMAX), 1), LMAX)
    upto = t2 >= u2
    solves, pull_key, reads = [], [], []
    for k in range(heads):
        base = k * 2 * LMAX
        system = jnp.where(strict, pairs[base : base + LMAX, :LMAX], 0.0)
        pull_key.append(split(jnp.where(strict, pairs[base : base + LMAX, LMAX:], 0.0)))
        reads.append(split(jnp.where(upto, pairs[base + LMAX : base + 2 * LMAX], 0.0)))
        solves.append(system)
    inverse = []
    for k in range(heads):
        near = (t // 2 == u // 2)
        inverse.append(
            jnp.where(near, solves[k], 0.0) + (t == u).astype(F32)
        )
    size = 2
    while size < LMAX:
        inside = (t // (2 * size) == u // (2 * size)) & (t // size != u // size)
        grown = []
        for k in range(heads):
            known = split(inverse[k])
            cross = split(jnp.where(inside, solves[k], 0.0))
            product = split(dot3(known, cross))
            grown.append(inverse[k] + dot3(product, known))
        inverse = grown
        size *= 2

    def across(mats, parts):
        wide_left = tuple(jnp.concatenate([mat[i] for mat in mats], axis=1) for i in range(2))
        tall = tuple(
            jnp.concatenate([only(part[i], k) for k in range(heads) for part in parts])
            for i in range(2)
        )
        return dot3(wide_left, tall)

    start = across(pull_key, [value_parts])
    pulled = split(across([split(x) for x in inverse], [split(start)]))
    output = across(reads, [pulled, value_parts])
    tail = jnp.exp(last - total)
    write_tail = split(write * tail)
    key_tail = split(key * tail)
    tall = tuple(jnp.concatenate([pulled[i], value_parts[i]]) for i in range(2))
    tails = tuple(jnp.concatenate([write_tail[i], key_tail[i]]) for i in range(2))
    state = dot3(tall, tails, ((0,), (0,)))
    even = lax.broadcasted_iota(jnp.int32, (HEAD, FEAT), 1) < HEAD
    for k in range(heads // 2):
        lanes = slice(k * FEAT, (k + 1) * FEAT)
        final[prompt, k] = jnp.where(
            even,
            state[k * FEAT : k * FEAT + HEAD, lanes],
            state[k * FEAT + HEAD : (k + 1) * FEAT, lanes],
        ).astype(BF16)
    bonus = head_sum(receptance * key * coef[3:4, channels])
    out = (output + bonus * value) * live
    center = head_sum(out) * (1.0 / HEAD)
    out = out - center
    spread = head_sum(out * out) * (1.0 / HEAD)
    out = (out * lax.rsqrt(spread + 0.00064) * coef[4:5, channels] + coef[5:6, channels]).astype(BF16)
    for side in range(2):
        att[side, tokens] = out[:, side * FEAT : (side + 1) * FEAT]


PROMPTS = MINE // LMAX
HOPS = 9


class PromptRing:
    def __init__(self, send_sem, recv_sem, base, axis, own, got):
        self.send_sem = send_sem
        self.recv_sem = recv_sem
        self.base = base
        self.here, self.chips, self.to = ring_at(axis)
        self.own = own
        self.got = got
        self.heavy = axis == "row"

    def hop(self, m, slot, chip, side, half=None):
        def block():
            at = self.chips.get(chip, self.here)
            if half is None:
                return self.got.at[pl.ds(2 * at, 2), aligned(m, LMAX)]
            return self.got.at[2 * at + half, aligned(m, LMAX)]

        def source():
            if chip == "own" and self.own is not None:
                return self.own.at[:, aligned(m, LMAX)]
            return block()

        return Copy(
            source,
            block,
            self.send_sem,
            self.recv_sem,
            self.base + m * HOPS + slot,
            self.to[side],
        )

    def hops(self, m):
        return [
            self.hop(m, 0, "own", "p"),
            self.hop(m, 1, "own", "m"),
            self.hop(m, 2, "own", "z"),
            self.hop(m, 3, "m", "p", 0),
            self.hop(m, 4, "p", "m", 1),
            self.hop(m, 5, "z", "p"),
            self.hop(m, 6, "z", "m"),
            self.hop(m, 7, "o", "z", 0) if self.heavy else self.hop(m, 7, "mz", "p", 0),
            self.hop(m, 8, "o", "z", 1) if self.heavy else self.hop(m, 8, "pz", "m", 1),
        ]

    def begin(self, m):
        copies = self.hops(m)
        for k in (2, 0, 1):
            copies[k].start()

    def forward(self, m):
        copies = self.hops(m)
        copies[0].wait_recv()
        copies[3].start()
        copies[1].wait_recv()
        copies[4].start()
        copies[2].wait_recv()
        copies[5].start()
        copies[6].start()

    def close(self, m):
        copies = self.hops(m)
        for early, late in ((3, 7), (4, 8)) if self.heavy else ((6, 8), (5, 7)):
            copies[early].wait_recv()
            copies[late].start()

    def last(self, m):
        for k in (5, 6, 7, 8) if self.heavy else (3, 4, 7, 8):
            self.hops(m)[k].wait_recv()

    def sent(self, m):
        for copy in self.hops(m):
            copy.wait_send()


N_SUM = PROMPTS * 6
N_TURN = N_SUM + 2 * PROMPTS
N_STATE = N_TURN + 1
N_WEIGHT = N_STATE + 3 * PROMPTS * HOPS
N_ALL = N_WEIGHT + 1 + 2 * (1 + 14 + RING)


def body_kernel(
    lens,
    hx,
    par,
    shift,
    wt,
    down,
    coef,
    up,
    w3,
    wk,
    wv,
    wn,
    out,
    next_rkv,
    final,
    send_sem,
    recv_sem,
    local_sem,
    rkv,
    low,
    state,
    att,
    attg,
    w3x,
    mid,
    midg,
    held,
    theirs,
    act_scr,
    part,
    got,
    summed,
    fin,
    nx,
    wng,
):
    r, c, h, q, sibling = place()
    x_here = lax.div(r, 4)
    z_row = 4 * x_here + 2 * (1 - lax.rem(q, 2))

    def local():
        return [
            pltpu.make_async_copy(wk.at[c], held.at[0, :, c], local_sem.at[0]),
            pltpu.make_async_copy(wv.at[c], held.at[1, :, c], local_sem.at[1]),
            pltpu.make_async_copy(wn, wng, local_sem.at[2]),
        ]

    for copy in local():
        copy.start()

    def target(i):
        return (2 * c + lax.rem(h + i, 2), q)

    barrier = pltpu.get_barrier_semaphore()
    peers = [(lax.rem(r + 4 * d, N_ROW), c) for d in range(1, 4)] + ring_peers("col")
    peers += [(sibling, c), (z_row, c), (z_row + 1, c)]

    @pl.when(q != c)
    def _():
        for i in range(2):
            pl.semaphore_signal(barrier, inc=1, device_id=target(i), device_id_type=MESH)

    for device in peers:
        pl.semaphore_signal(barrier, inc=1, device_id=device, device_id_type=MESH)
    pl.semaphore_wait(barrier, len(peers) + 2 * (q != c).astype(jnp.int32))

    links = Links(send_sem, recv_sem, N_WEIGHT)
    links.go(w3, w3x, (sibling, c))

    col_place = ring_at("col")

    def mlp_ring(which, source):
        def slot(chip, half):
            return held.at[which, pl.ds(8 * half, 8), chip]

        def over(chip, half):
            return theirs.at[which, pl.ds(8 * half, 8), chip]

        def seen(chip, half):
            links.go(lambda: slot(chip, half), lambda: over(chip, half), (sibling, c))

        def begin():
            links.go(lambda: source.at[c], lambda: theirs.at[which, :, c], (sibling, c))
            yield from ring(
                links,
                "col",
                slot,
                own=lambda k: source.at[c, pl.ds(8 * k, 8)],
                seen=seen,
                at=col_place,
            )

        return begin()

    keys = mlp_ring(0, wk)
    values = mlp_ring(1, wv)
    next(keys)

    att_ring = PromptRing(send_sem, recv_sem, N_STATE, "row", att, attg)
    mid_ring = PromptRing(send_sem, recv_sem, N_STATE + PROMPTS * HOPS, "row", mid, midg)
    out_ring = PromptRing(send_sem, recv_sem, N_STATE + 2 * PROMPTS * HOPS, "col", None, nx)
    move_state = Copy(state, final, send_sem, recv_sem, N_TURN, target(0))

    def wide(ref, m):
        return jnp.concatenate([ref[j, aligned(m, LMAX), :] for j in range(N_ROW)], axis=1)

    def normed(ref, m, k):
        return norm(wide(ref, m).astype(F32), row_of(par, k), row_of(par, k + 1))

    def blends(m):
        z = normed(hx, m, 0)
        dz = step_back(z)
        for j in range(5):
            blend = (z + dz * shift[j : j + 1, :]).astype(BF16)
            if j < 3:
                weight = jnp.concatenate(
                    [wt[side, j].reshape(WIDTH, FEAT) for side in range(2)], axis=1
                )
                rkv[j] = dot(blend, weight)
            else:
                low[j - 3] = dot(blend, down[j - 3], ((1,), (1,)))

    def core(m):
        one_prompt(m, lens, rkv, low, coef, up, att, state)
        att_ring.begin(m)
        for side in range(2):
            attg[2 * q + side, aligned(m, LMAX)] = att[side, aligned(m, LMAX)]

    def project(m):
        att_ring.last(m)
        tokens = aligned(m, LMAX)
        weight = jnp.concatenate([w[...].reshape(FEAT, WIDTH) for w in (w3, w3x)])
        total = dot(wide(attg, m), weight, ((1,), (1,)))
        for k, side in enumerate((h, 1 - h)):
            block = (
                hx[r - h + side, tokens, :].astype(F32) + total[:, k * FEAT : (k + 1) * FEAT]
            ).astype(BF16)
            mid[side, tokens, :] = block
            midg[r - h + side, tokens, :] = block
        mid_ring.begin(m)

    def first_sums(m):
        def copy_of(d):
            x_there = lax.rem(x_here + d, 4)
            return Copy(
                lambda: part.at[pl.ds(4 * x_there, 4), aligned(m, LMAX)],
                lambda: got.at[pl.ds(4 * x_here, 4), aligned(m, LMAX)],
                send_sem,
                recv_sem,
                6 * m + d - 1,
                (lax.rem(r + 4 * d, N_ROW), c),
            )

        return [copy_of(d) for d in range(1, 4)]

    def plane_move(m, k):
        there = sibling if k == 0 else z_row + k - 1
        own_k = 0 if k == 0 else 1 + h
        return pltpu.make_async_remote_copy(
            src_ref=summed.at[there - 4 * x_here, aligned(m, LMAX)],
            dst_ref=fin.at[(0 if k == 0 else 2) + h, aligned(m, LMAX)],
            send_sem=send_sem.at[6 * m + 3 + k],
            recv_sem=recv_sem.at[6 * m + 3 + own_k],
            device_id=(there, c),
            device_id_type=MESH,
        )

    def channel(m):
        mid_ring.last(m)
        tokens = aligned(m, LMAX)
        z = normed(midg, m, 2)
        blend = (z + step_back(z) * shift[5:6, :]).astype(BF16)
        for side, weight in enumerate((held, theirs)):
            act = jnp.square(jnp.maximum(dot(blend, weight[0].reshape(WIDTH, MINE)), 0.0))
            act_scr[side] = act.astype(BF16)

        @pl.loop(0, N_CHIP)
        def _(n):
            total = None
            for side, weight in enumerate((held, theirs)):
                rows_n = weight[1, pl.ds(2 * n, 2)].reshape(SLICE, MINE)
                term = dot(act_scr[side], rows_n, ((1,), (1,)))
                total = term if total is None else total + term
            for side in range(2):
                added = jnp.where(n == q, mid[side, tokens, :].astype(F32), 0.0)
                part[2 * n + side, tokens, :] = (
                    total[:, side * FEAT : (side + 1) * FEAT] + added
                ).astype(BF16)

        for copy in first_sums(m):
            copy.start()
        for k in range(4):
            got[4 * x_here + k, tokens, :] = part[4 * x_here + k, tokens, :]

    def plane_sum(m):
        for copy in first_sums(m):
            copy.wait_recv()
        tokens = aligned(m, LMAX)
        for k in range(4):
            total = got[k, tokens, :].astype(F32)
            for x in range(1, 4):
                total += got[4 * x + k, tokens, :].astype(F32)
            summed[k, tokens, :] = total.astype(BF16)
        for k in (1, 2, 0):
            plane_move(m, k).start()
        fin[h, tokens, :] = summed[r - 4 * x_here, tokens, :]

    def source_rows(m, i):
        return pl.ds(pl.multiple_of(lax.rem(h + i, 2) * MINE + m * LMAX, LMAX), LMAX)

    def turn(m, i):
        return pltpu.make_async_remote_copy(
            src_ref=out.at[source_rows(m, i)],
            dst_ref=nx.at[2 * q + h, aligned(m, LMAX)],
            send_sem=send_sem.at[N_SUM + 2 * m + i],
            recv_sem=recv_sem.at[N_SUM + 2 * m + h],
            device_id=target(i),
            device_id_type=MESH,
        )

    def add_up(m):
        tokens = aligned(m, LMAX)
        for k in range(3):
            block = fin.at[0, tokens]
            pltpu.make_async_copy(block, block, recv_sem.at[6 * m + 3 + k]).wait()
        for side in range(2):
            total = fin[side, tokens, :].astype(F32) + fin[2 + side, tokens, :].astype(F32)
            rows_m = pl.ds(pl.multiple_of(side * MINE + m * LMAX, LMAX), LMAX)
            out[rows_m, :] = total.astype(BF16)

        @pl.when(q == c)
        def _():
            keep(
                out.at[source_rows(m, 0)],
                nx.at[r, aligned(m, LMAX)],
                recv_sem.at[N_SUM + 2 * m + h],
            )

        @pl.when(q != c)
        def _():
            turn(m, 0).start()

        turn(m, 1).start()

    def spread(m):
        for k in range(2):
            block = nx.at[2 * c + k, aligned(m, LMAX)]
            pltpu.make_async_copy(block, block, recv_sem.at[N_SUM + 2 * m + k]).wait()
        out_ring.begin(m)

    def project_next(m):
        out_ring.last(m)
        z = normed(nx, m, 4)
        dz = step_back(z)
        for j in range(3):
            blend = (z + dz * shift[6 + j : 7 + j, :]).astype(BF16)
            next_rkv[j, aligned(m, LMAX), :] = dot(
                blend, wng[:, :, j].reshape(WIDTH, SLICE)
            ).astype(BF16)

    stages = (
        blends,
        core,
        att_ring.forward,
        att_ring.close,
        project,
        mid_ring.forward,
        mid_ring.close,
        channel,
        plane_sum,
        add_up,
        spread,
        out_ring.forward,
        out_ring.close,
        project_next,
    )
    end = object()

    def wait_mlp():
        for copy in local()[:2]:
            copy.wait()
        for copy in links.open:
            copy.wait_recv()
        links.open = []

    def send_state():
        @pl.when(q == c)
        def _():
            keep(state, final, recv_sem.at[N_TURN])

        @pl.when(q != c)
        def _():
            move_state.start()

    def wait_far():
        local()[2].wait()

    beside = {
        1: [keys],
        2: [keys, values],
        3: [keys, values, lambda: links.arrive(links.copies[0])],
        4: [keys, values],
        5: [values],
        6: [values],
        7: [send_state, wait_mlp],
        13: [wait_far],
    }
    middle = stages.index(channel)

    def run(t, first, end_at):
        for lag in range(first, end_at):
            since = t - lag

            @pl.when((since >= 0) & (since < 2 * PROMPTS) & (lax.rem(t + lag, 2) == 0))
            def _():
                stages[lag](lax.div(since, 2))

    @pl.loop(0, 2 * PROMPTS + len(stages) - 2)
    def _(t):
        run(t, 0, middle)
        for at, works in beside.items():

            @pl.when(t == at)
            def _():
                for work in works:
                    if callable(work):
                        work()
                    else:
                        next(work, end)

        run(t, middle, len(stages))

    @pl.loop(0, PROMPTS)
    def _(m):
        for copy in first_sums(m):
            copy.wait_send()
        for k in range(3):
            plane_move(m, k).wait_send()
        for prompt_ring in (att_ring, mid_ring, out_ring):
            prompt_ring.sent(m)

        @pl.when(q != c)
        def _():
            turn(m, 0).wait_send()

        turn(m, 1).wait_send()

    pltpu.make_async_copy(state, final, recv_sem.at[N_TURN]).wait()

    @pl.when(q != c)
    def _():
        move_state.wait_send()

    for copy in links.copies:
        copy.wait_send()


def per_device(
    hidden,
    lengths,
    square_matrix_shards,
    channel_mix_shards,
    lowrank_down,
    lowrank_up,
    token_shift_weights,
    attention_coefficients,
    norm_parameters,
):
    hx, wt, w3, wk, wv, wn, parg = exchange(
        start_kernel,
        [
            ((N_ROW, MINE, FEAT), BF16),
            ((2, 3, N_ROW, N_COL, 16, FEAT), BF16),
            ((N_COL, 16, WIDTH), BF16),
            ((N_COL, N_ROW, 16, MINE), BF16),
            ((N_COL, N_ROW, 16, MINE), BF16),
            ((N_ROW, N_COL, 3, 16, SLICE), BF16),
            ((N_ROW, 6, FEAT), F32),
        ],
        15 + 1 + 4 * RING + 2 * (1 + 14) + 15 + 15 + 7 + 15,
        9,
        1,
        square_matrix_shards,
        channel_mix_shards,
        norm_parameters,
        hidden,
        scratch=[
            pltpu.VMEM(square_matrix_shards.shape, F32),
            pltpu.VMEM(channel_mix_shards.shape, F32),
            pltpu.VMEM(square_matrix_shards.shape, BF16),
            pltpu.VMEM(channel_mix_shards.shape, BF16),
        ],
    )
    lowrank = lowrank_down.shape[2]
    out_hidden, next_rkv, final = exchange(
        body_kernel,
        [
            ((2 * MINE, FEAT), BF16),
            ((3, MINE, SLICE), BF16),
            ((PROMPTS, 2, HEAD, FEAT), BF16),
        ],
        N_ALL,
        3,
        2,
        lengths,
        hx,
        parg,
        token_shift_weights,
        wt,
        lowrank_down.transpose(0, 2, 1),
        attention_coefficients,
        lowrank_up,
        w3,
        wk,
        wv,
        wn,
        scratch=[
            pltpu.VMEM((3, LMAX, SLICE), F32),
            pltpu.VMEM((2, LMAX, lowrank), F32),
            pltpu.VMEM((PROMPTS, 2, HEAD, FEAT), BF16),
            pltpu.VMEM((2, MINE, FEAT), BF16),
            pltpu.VMEM((N_ROW, MINE, FEAT), BF16),
            pltpu.VMEM((N_COL, 16, WIDTH), BF16),
            pltpu.VMEM((2, MINE, FEAT), BF16),
            pltpu.VMEM((N_ROW, MINE, FEAT), BF16),
            pltpu.VMEM((2, N_ROW, N_COL, 16, MINE), BF16),
            pltpu.VMEM((2, N_ROW, N_COL, 16, MINE), BF16),
            pltpu.VMEM((2, LMAX, MINE), BF16),
            pltpu.VMEM((N_ROW, MINE, FEAT), BF16),
            pltpu.VMEM((N_ROW, MINE, FEAT), BF16),
            pltpu.VMEM((4, MINE, FEAT), BF16),
            pltpu.VMEM((4, MINE, FEAT), BF16),
            pltpu.VMEM((N_ROW, MINE, FEAT), BF16),
            pltpu.VMEM((N_ROW, N_COL, 3, 16, SLICE), BF16),
        ],
        in_specs=[pl.BlockSpec(memory_space=pltpu.SMEM)] + [VMEM] * 8 + [ANY] * 3,
        out_specs=[VMEM, VMEM, ANY],
    )
    final = final.reshape(4, 2, HEAD, 2, HEAD).transpose(0, 1, 3, 2, 4).astype(F32)
    final_state = final.reshape(4, 4, HEAD * HEAD)
    return (out_hidden, next_rkv, final_state)


def solution(mesh):
    return jax.shard_map(
        per_device,
        mesh=mesh,
        in_specs=(
            P("col", "row"),
            P(),
            P(None, ("row", "col"), None),
            P(None, ("row", "col"), None),
            P(),
            P(),
            P(),
            P(),
            P(None, "row"),
        ),
        out_specs=(P("col", "row"), P(None, "row", "col"), P("row", "col", None)),
        check_vma=False,
    )
```

```python
import functools

import jax
import jax.numpy as jnp
from jax import lax
from jax.experimental import pallas as pl
from jax.experimental.pallas import tpu as pltpu
from jax.sharding import PartitionSpec as P

WIDTH = 2048
HEAD = 64
LMAX = 128
F32 = jnp.float32
BF16 = jnp.bfloat16
MESH = pl.DeviceIdType.MESH
ANY = pl.BlockSpec(memory_space=pl.ANY)
VMEM = pl.BlockSpec(memory_space=pltpu.VMEM)
N_ROW = 16
N_COL = 8
N_CHIP = 8
MINE = 512
FEAT = 128
SLICE = 256


def greet(devices):
    barrier = pltpu.get_barrier_semaphore()
    for device in devices:
        pl.semaphore_signal(barrier, inc=1, device_id=device, device_id_type=MESH)
    pl.semaphore_wait(barrier, len(devices))


class Copy:
    def __init__(self, source, target, send_sem, recv_sem, slot, device):
        self.made = lambda: pltpu.make_async_remote_copy(
            src_ref=source() if callable(source) else source,
            dst_ref=target() if callable(target) else target,
            send_sem=send_sem.at[slot],
            recv_sem=recv_sem.at[slot],
            device_id=device,
            device_id_type=MESH,
        )

    def start(self):
        self.made().start()

    def wait_recv(self):
        self.made().wait_recv()

    def wait_send(self):
        self.made().wait_send()


def keep(source, target, sem):
    copy = pltpu.make_async_copy(source, target, sem)
    copy.start()
    return copy


def exchange(
    kernel,
    outs,
    n_remote,
    n_local,
    collective_id,
    *operands,
    scratch=(),
    in_specs=None,
    out_specs=None,
):
    return pl.pallas_call(
        kernel,
        out_shape=[jax.ShapeDtypeStruct(*out) for out in outs],
        in_specs=in_specs or [ANY] * len(operands),
        out_specs=out_specs or [ANY] * len(outs),
        scratch_shapes=[
            pltpu.SemaphoreType.DMA((n_remote,)),
            pltpu.SemaphoreType.DMA((n_remote,)),
            pltpu.SemaphoreType.DMA((n_local,)),
            *scratch,
        ],
        compiler_params=pltpu.CompilerParams(
            collective_id=collective_id, has_side_effects=True, vmem_limit_bytes=56 * 2**20
        ),
        cost_estimate=pl.CostEstimate(flops=0, bytes_accessed=48 * 2**20, transcendentals=0),
    )(*operands)


def place():
    r = lax.axis_index("row")
    c = lax.axis_index("col")
    h = lax.rem(r, 2)
    return r, c, h, lax.div(r, 2), r + 1 - 2 * h


class Links:
    def __init__(self, send_sem, recv_sem, first=0):
        self.send_sem = send_sem
        self.recv_sem = recv_sem
        self.slot = first
        self.copies = []
        self.open = []

    def go(self, source, target, device):
        copy = Copy(source, target, self.send_sem, self.recv_sem, self.slot, device)
        copy.start()
        self.slot += 1
        self.copies.append(copy)
        self.open.append(copy)
        return copy

    def arrive(self, copy):
        copy.wait_recv()
        self.open = [other for other in self.open if other is not copy]

    def finish(self):
        for copy in self.open:
            copy.wait_recv()
        for copy in self.copies:
            copy.wait_send()


RING = 14


def ring_at(axis):
    r, c, h, q, _ = place()
    here = q if axis == "row" else c
    step_z = 1 - 2 * lax.rem(here, 2)
    chips = {
        "p": lax.rem(here + 2, 8),
        "m": lax.rem(here + 6, 8),
        "z": here + step_z,
        "o": lax.rem(here + 4, 8),
        "pz": lax.rem(here + 2, 8) + step_z,
        "mz": lax.rem(here + 6, 8) + step_z,
        "oz": lax.rem(here + 4, 8) + step_z,
    }
    devices = {
        side: (2 * chips[side] + h, c) if axis == "row" else (r, chips[side]) for side in "pmz"
    }
    return here, chips, devices


def ring_peers(axis):
    return list(ring_at(axis)[2].values())


def ring(links, axis, slot, own=None, which=(0, 1), ready=None, seen=None, heavy=None, at=None):
    here, chips, to = at or ring_at(axis)
    heavy = axis == "row" if heavy is None else heavy
    seen = seen or (lambda chip, half: None)

    def take(copy, chip, half):
        links.arrive(copy)
        seen(chip, half)

    def forward(chip, half, side):
        return links.go(lambda: slot(chip, half), lambda: slot(chip, half), to[side])

    first = {}
    for k in range(2):
        if ready is not None:
            ready(k)
        target = functools.partial(slot, here, which[k])
        source = functools.partial(own, k) if own is not None else target
        for side in "zpm":
            first[side, k] = links.go(source, target, to[side])
    yield
    for k in range(2):
        take(first["p", k], chips["m"], which[k])
    low = forward(chips["m"], 0, "p")
    for k in range(2):
        take(first["m", k], chips["p"], which[k])
    high = forward(chips["p"], 1, "m")
    yield
    beside = {}
    for k in range(2):
        take(first["z", k], chips["z"], which[k])
        for side in "pm":
            beside[side, k] = forward(chips["z"], which[k], side)
    yield
    if heavy:
        take(low, chips["o"], 0)
        low = forward(chips["o"], 0, "z")
        take(high, chips["o"], 1)
        high = forward(chips["o"], 1, "z")
        yield
        for k in range(2):
            take(beside["p", k], chips["mz"], which[k])
            take(beside["m", k], chips["pz"], which[k])
    else:
        take(low, chips["o"], 0)
        take(high, chips["o"], 1)
        for k in range(2):
            take(beside["p", k], chips["mz"], which[k])
        low = forward(chips["mz"], 0, "p")
        for k in range(2):
            take(beside["m", k], chips["pz"], which[k])
        high = forward(chips["pz"], 1, "m")
        yield
    take(low, chips["oz"], 0)
    take(high, chips["oz"], 1)


def together(*steps):
    active = list(steps)
    while active:
        for step in list(active):
            if next(step, StopIteration) is StopIteration:
                active.remove(step)


def aligned(index, size):
    return pl.ds(pl.multiple_of(index * size, size), size)


def start_kernel(
    square_in,
    mlp_in,
    par,
    hid,
    hx,
    wt,
    w3,
    wk,
    wv,
    wn,
    parg,
    send_sem,
    recv_sem,
    local_sem,
    square_wide,
    mlp_wide,
    square,
    mlp,
):
    r, c, h, q, sibling = place()
    rows = [lax.rem(r + d, N_ROW) for d in range(1, N_ROW)]
    cols = [lax.rem(c + d, N_COL) for d in range(1, N_COL)]

    def time_part(p):
        return square.at[pl.ds(0, 3), :, aligned(p, FEAT)]

    def key_part(p):
        return mlp.at[0, :, aligned(p, MINE)]

    def value_part(p):
        return mlp.at[1, :, aligned(p, MINE)]

    def next_part(p):
        return square.at[pl.ds(4, 3), :, aligned(p, SLICE)]

    mine = hid.at[aligned(h, MINE)]
    square_load = keep(square_in, square_wide, local_sem.at[7])
    mlp_load = keep(mlp_in, mlp_wide, local_sem.at[8])
    local = [
        keep(par, parg.at[r], local_sem.at[1]),
        keep(mine, hx.at[r], local_sem.at[2]),
    ]
    greet([(p, c) for p in rows] + [(r, p) for p in cols])
    links = Links(send_sem, recv_sem)
    times = []
    own_time = []
    other = links.go(hid.at[aligned(1 - h, MINE)], hx.at[r], (sibling, c))

    def hid_own(k):
        return (mine, hx.at[sibling])[k]

    def hid_ready(k):
        if k == 1:
            links.arrive(other)

    def time_ready(k):
        if k == 0:
            for copy in times:
                links.arrive(copy)
            links.go(wt.at[h, :, :, c], wt.at[h, :, :, c], (sibling, c))

    def time_slot(chip, half):
        return wt.at[h, :, pl.ds(8 * half, 8), chip]

    def time_seen(chip, half):
        links.go(time_slot(chip, half), time_slot(chip, half), (sibling, c))

    def out_slot(chip, half):
        return w3.at[chip, :, pl.ds(1024 * half, 1024)]

    def out_own(k):
        return square.at[3, :, pl.ds(1024 * k, 1024)]

    def feed():
        square_load.wait()
        for j in range(3):
            square[j] = square_wide[j].astype(BF16)
        for p in rows:
            times.append(links.go(time_part(p), wt.at[lax.rem(p, 2), :, r, c], (p, c)))
        own_time.append(keep(time_part(r), wt.at[h, :, r, c], local_sem.at[0]))
        yield

    def casts():
        for j in range(3, 7):
            square[j] = square_wide[j].astype(BF16)
        mlp_load.wait()
        mlp[...] = mlp_wide[...].astype(BF16)
        own_time[0].wait()
        yield

    def rest():
        local.extend(
            [
                keep(square.at[3], w3.at[c], local_sem.at[3]),
                keep(key_part(r), wk.at[c, r], local_sem.at[4]),
                keep(value_part(r), wv.at[c, r], local_sem.at[5]),
                keep(next_part(c), wn.at[r, c], local_sem.at[6]),
            ]
        )
        for p in rows:
            links.go(par, parg.at[r], (p, c))
        yield
        for p in rows:
            links.go(key_part(p), wk.at[c, r], (p, c))
        for p in cols:
            links.go(next_part(p), wn.at[r, c], (r, p))
        for p in rows:
            links.go(value_part(p), wv.at[c, r], (p, c))

    together(
        feed(),
        ring(
            links,
            "row",
            lambda chip, side: hx.at[2 * chip + side],
            own=hid_own,
            which=(h, 1 - h),
            ready=hid_ready,
        ),
        casts(),
        ring(links, "col", time_slot, ready=time_ready, seen=time_seen),
        rest(),
        ring(links, "col", out_slot, own=out_own),
    )
    links.finish()
    for copy in local:
        copy.wait()


def dot(a, b, dims=((1,), (0,))):
    return lax.dot_general(a, b, (dims, ((), ())), preferred_element_type=F32)


def split(x):
    high = x.astype(BF16)
    return high, (x - high.astype(F32)).astype(BF16)


def dot3(a, b, dims=((1,), (0,))):
    a_high, a_low = a
    b_high, b_low = b
    return dot(a_high, b_high, dims) + (dot(a_high, b_low, dims) + dot(a_low, b_high, dims))


def norm(source, gain, bias):
    center = jnp.sum(source, axis=-1, keepdims=True) / WIDTH
    second = jnp.sum(source * source, axis=-1, keepdims=True) / WIDTH
    scaled = (source - center) * lax.rsqrt(second - center * center + 1e-05)
    return (scaled * gain + bias).astype(BF16).astype(F32)


def row_of(par, i):
    return jnp.concatenate([par[j, i : i + 1, :] for j in range(N_ROW)], axis=1)


def step_back(z):
    position = lax.rem(lax.broadcasted_iota(jnp.int32, z.shape, 0), LMAX)
    return jnp.where(position == 0, 0.0, pltpu.roll(z, 1, 0)) - z


def one_prompt(prompt, lens, rkv, low, coef, up, att, final):
    r, c, h, q, _ = place()
    length = lens[c * 8 + h * 4 + prompt]
    tokens = aligned(prompt, LMAX)
    wide = SLICE
    channels = aligned(q, SLICE)
    heads = wide // HEAD
    live = (lax.broadcasted_iota(jnp.int32, (LMAX, wide), 0) < length).astype(F32)
    lane = lax.broadcasted_iota(jnp.int32, (LMAX, wide), 1) // HEAD
    t = lax.broadcasted_iota(jnp.int32, (LMAX, LMAX), 0)
    u = lax.broadcasted_iota(jnp.int32, (LMAX, LMAX), 1)
    seg = (
        lax.broadcasted_iota(jnp.int32, (wide, wide), 0) // HEAD
        == lax.broadcasted_iota(jnp.int32, (wide, wide), 1) // HEAD
    ).astype(F32).astype(BF16)
    lower = (t >= u).astype(F32).astype(BF16)

    def head_sum(x):
        high, low_part = split(x)
        return dot(high, seg) + dot(low_part, seg)

    def only(x, k):
        return jnp.where(lane == k, x, jnp.zeros_like(x))

    receptance, key, value = rkv[0], rkv[1], rkv[2]
    decay = (
        -0.606531
        * jax.nn.sigmoid(coef[0:1, channels] + dot(jnp.tanh(low[0]).astype(BF16), up[0, :, channels]))
        * live
    )
    rate = jax.nn.sigmoid(coef[1:2, channels] + dot(low[1].astype(BF16), up[1, :, channels]))
    kappa = key * coef[2:3, channels]
    kappa = kappa * lax.rsqrt(head_sum(kappa * kappa) + 1e-05)
    remove = -kappa * live
    write = kappa * rate * live
    key = key * live
    value = value * live
    d_high, d_rest = split(decay)
    d_mid, d_low = split(decay - d_high.astype(F32))
    total = dot(lower, d_high) + (dot(lower, d_mid) + dot(lower, d_low))
    middle = total[LMAX // 2 - 1 : LMAX // 2, :]
    last = total[LMAX - 1 : LMAX, :]
    back = jnp.exp(middle - total)
    pull = split(remove * jnp.exp(total - decay - middle))
    read = split(receptance * jnp.exp(total - middle))
    write_back = split(write * back)
    key_back = split(key * back)
    value_parts = split(value)

    left = tuple(
        jnp.concatenate([x for k in range(heads) for x in (only(pull[i], k), only(read[i], k))])
        for i in range(2)
    )
    right = tuple(jnp.concatenate([write_back[i], key_back[i]]) for i in range(2))
    pairs = dot3(left, right, ((1,), (1,)))
    strict = t > u
    t2 = lax.broadcasted_iota(jnp.int32, (LMAX, 2 * LMAX), 0)
    u2 = lax.rem(lax.broadcasted_iota(jnp.int32, (LMAX, 2 * LMAX), 1), LMAX)
    upto = t2 >= u2
    solves, pull_key, reads = [], [], []
    for k in range(heads):
        base = k * 2 * LMAX
        system = jnp.where(strict, pairs[base : base + LMAX, :LMAX], 0.0)
        pull_key.append(split(jnp.where(strict, pairs[base : base + LMAX, LMAX:], 0.0)))
        reads.append(split(jnp.where(upto, pairs[base + LMAX : base + 2 * LMAX], 0.0)))
        solves.append(system)
    inverse = []
    for k in range(heads):
        near = (t // 2 == u // 2)
        inverse.append(
            jnp.where(near, solves[k], 0.0) + (t == u).astype(F32)
        )
    size = 2
    while size < LMAX:
        inside = (t // (2 * size) == u // (2 * size)) & (t // size != u // size)
        grown = []
        for k in range(heads):
            known = split(inverse[k])
            cross = split(jnp.where(inside, solves[k], 0.0))
            product = split(dot3(known, cross))
            grown.append(inverse[k] + dot3(product, known))
        inverse = grown
        size *= 2

    def across(mats, parts):
        wide_left = tuple(jnp.concatenate([mat[i] for mat in mats], axis=1) for i in range(2))
        tall = tuple(
            jnp.concatenate([only(part[i], k) for k in range(heads) for part in parts])
            for i in range(2)
        )
        return dot3(wide_left, tall)

    start = across(pull_key, [value_parts])
    pulled = split(across([split(x) for x in inverse], [split(start)]))
    output = across(reads, [pulled, value_parts])
    tail = jnp.exp(last - total)
    write_tail = split(write * tail)
    key_tail = split(key * tail)
    tall = tuple(jnp.concatenate([pulled[i], value_parts[i]]) for i in range(2))
    tails = tuple(jnp.concatenate([write_tail[i], key_tail[i]]) for i in range(2))
    state = dot3(tall, tails, ((0,), (0,)))
    even = lax.broadcasted_iota(jnp.int32, (HEAD, FEAT), 1) < HEAD
    for k in range(heads // 2):
        lanes = slice(k * FEAT, (k + 1) * FEAT)
        final[prompt, k] = jnp.where(
            even,
            state[k * FEAT : k * FEAT + HEAD, lanes],
            state[k * FEAT + HEAD : (k + 1) * FEAT, lanes],
        ).astype(BF16)
    bonus = head_sum(receptance * key * coef[3:4, channels])
    out = (output + bonus * value) * live
    center = head_sum(out) * (1.0 / HEAD)
    out = out - center
    spread = head_sum(out * out) * (1.0 / HEAD)
    out = (out * lax.rsqrt(spread + 0.00064) * coef[4:5, channels] + coef[5:6, channels]).astype(BF16)
    for side in range(2):
        att[side, tokens] = out[:, side * FEAT : (side + 1) * FEAT]


PROMPTS = MINE // LMAX
HOPS = 9


class PromptRing:
    def __init__(self, send_sem, recv_sem, base, axis, own, got):
        self.send_sem = send_sem
        self.recv_sem = recv_sem
        self.base = base
        self.here, self.chips, self.to = ring_at(axis)
        self.own = own
        self.got = got

    def hop(self, m, slot, chip, side, half=None):
        def block():
            at = self.chips.get(chip, self.here)
            if half is None:
                return self.got.at[pl.ds(2 * at, 2), aligned(m, LMAX)]
            return self.got.at[2 * at + half, aligned(m, LMAX)]

        def source():
            if chip == "own" and self.own is not None:
                return self.own.at[:, aligned(m, LMAX)]
            return block()

        return Copy(
            source,
            block,
            self.send_sem,
            self.recv_sem,
            self.base + m * HOPS + slot,
            self.to[side],
        )

    def hops(self, m):
        return [
            self.hop(m, 0, "own", "p"),
            self.hop(m, 1, "own", "m"),
            self.hop(m, 2, "own", "z"),
            self.hop(m, 3, "m", "p", 0),
            self.hop(m, 4, "p", "m", 1),
            self.hop(m, 5, "z", "p"),
            self.hop(m, 6, "z", "m"),
            self.hop(m, 7, "o", "z", 0),
            self.hop(m, 8, "o", "z", 1),
        ]

    def begin(self, m):
        copies = self.hops(m)
        for k in (2, 0, 1):
            copies[k].start()

    def forward(self, m):
        copies = self.hops(m)
        copies[0].wait_recv()
        copies[3].start()
        copies[1].wait_recv()
        copies[4].start()
        copies[2].wait_recv()
        copies[5].start()
        copies[6].start()

    def close(self, m):
        copies = self.hops(m)
        copies[3].wait_recv()
        copies[7].start()
        copies[4].wait_recv()
        copies[8].start()

    def last(self, m):
        for k in (5, 6, 7, 8):
            self.hops(m)[k].wait_recv()

    def sent(self, m):
        for copy in self.hops(m):
            copy.wait_send()


N_SUM = PROMPTS * (N_ROW - 1)
N_TURN = N_SUM + 2 * PROMPTS
N_STATE = N_TURN + 1
N_WEIGHT = N_STATE + 3 * PROMPTS * HOPS
N_ALL = N_WEIGHT + 1 + 2 * (1 + 14 + RING) + 1 + 14 + RING


def body_kernel(
    lens,
    hx,
    par,
    shift,
    wt,
    down,
    coef,
    up,
    w3,
    wk,
    wv,
    wn,
    out,
    next_rkv,
    final,
    send_sem,
    recv_sem,
    local_sem,
    rkv,
    low,
    state,
    att,
    attg,
    w3x,
    mid,
    midg,
    held,
    theirs,
    act_scr,
    part,
    got,
    nx,
    wng,
):
    r, c, h, q, sibling = place()
    rows = [lax.rem(r + d, N_ROW) for d in range(1, N_ROW)]

    def local():
        return [
            pltpu.make_async_copy(wk.at[c], held.at[0, :, c], local_sem.at[0]),
            pltpu.make_async_copy(wv.at[c], held.at[1, :, c], local_sem.at[1]),
            pltpu.make_async_copy(wn.at[r], wng.at[r], local_sem.at[2]),
        ]

    for copy in local():
        copy.start()

    def target(i):
        return (2 * c + lax.rem(h + i, 2), q)

    barrier = pltpu.get_barrier_semaphore()
    peers = [(p, c) for p in rows] + [(r, lax.rem(c + d, N_COL)) for d in range(1, N_COL)]

    @pl.when(q != c)
    def _():
        for i in range(2):
            pl.semaphore_signal(barrier, inc=1, device_id=target(i), device_id_type=MESH)

    for device in peers:
        pl.semaphore_signal(barrier, inc=1, device_id=device, device_id_type=MESH)
    pl.semaphore_wait(barrier, len(peers) + 2 * (q != c).astype(jnp.int32))

    links = Links(send_sem, recv_sem, N_WEIGHT)
    links.go(w3, w3x, (sibling, c))

    col_place = ring_at("col")

    def mlp_ring(which, source):
        def slot(chip, half):
            return held.at[which, pl.ds(8 * half, 8), chip]

        def over(chip, half):
            return theirs.at[which, pl.ds(8 * half, 8), chip]

        def seen(chip, half):
            links.go(lambda: slot(chip, half), lambda: over(chip, half), (sibling, c))

        def begin():
            links.go(lambda: source.at[c], lambda: theirs.at[which, :, c], (sibling, c))
            yield from ring(
                links,
                "col",
                slot,
                own=lambda k: source.at[c, pl.ds(8 * k, 8)],
                seen=seen,
                at=col_place,
            )

        return begin()

    def weight_slot(chip, half):
        return wng.at[2 * chip + h, pl.ds(4 * half, 4)]

    far_links = Links(send_sem, recv_sem, N_ALL - 1 - 14 - RING)

    def weight_seen(chip, half):
        far_links.go(
            lambda: weight_slot(chip, half), lambda: weight_slot(chip, half), (sibling, c)
        )

    def weight_ring():
        far_links.go(lambda: wn.at[r], lambda: wng.at[r], (sibling, c))
        yield from ring(
            far_links,
            "row",
            weight_slot,
            own=lambda k: wn.at[r, pl.ds(4 * k, 4)],
            seen=weight_seen,
        )

    keys = mlp_ring(0, wk)
    values = mlp_ring(1, wv)
    weights = weight_ring()
    for steps in (weights, keys, values):
        next(steps)

    att_ring = PromptRing(send_sem, recv_sem, N_STATE, "row", att, attg)
    mid_ring = PromptRing(send_sem, recv_sem, N_STATE + PROMPTS * HOPS, "row", mid, midg)
    cols = [lax.rem(c + d, N_COL) for d in range(1, N_COL)]

    def out_sends(m):
        def copy_of(k, p):
            def block():
                return nx.at[pl.ds(2 * c, 2), aligned(m, LMAX)]

            at = N_STATE + (2 * PROMPTS + m) * HOPS + k
            return Copy(block, block, send_sem, recv_sem, at, (r, p))

        return [copy_of(k, p) for k, p in enumerate(cols)]

    move_state = Copy(state, final, send_sem, recv_sem, N_TURN, target(0))

    def wide(ref, m):
        return jnp.concatenate([ref[j, aligned(m, LMAX), :] for j in range(N_ROW)], axis=1)

    def normed(ref, m, k):
        return norm(wide(ref, m).astype(F32), row_of(par, k), row_of(par, k + 1))

    def blends(m):
        z = normed(hx, m, 0)
        dz = step_back(z)
        for j in range(5):
            blend = (z + dz * shift[j : j + 1, :]).astype(BF16)
            if j < 3:
                weight = jnp.concatenate(
                    [wt[side, j].reshape(WIDTH, FEAT) for side in range(2)], axis=1
                )
                rkv[j] = dot(blend, weight)
            else:
                low[j - 3] = dot(blend, down[j - 3], ((1,), (1,)))

    def core(m):
        blends(m)
        one_prompt(m, lens, rkv, low, coef, up, att, state)
        att_ring.begin(m)
        for side in range(2):
            attg[2 * q + side, aligned(m, LMAX)] = att[side, aligned(m, LMAX)]

    def project(m):
        att_ring.last(m)
        tokens = aligned(m, LMAX)
        weight = jnp.concatenate([w[...].reshape(FEAT, WIDTH) for w in (w3, w3x)])
        total = dot(wide(attg, m), weight, ((1,), (1,)))
        for k, side in enumerate((h, 1 - h)):
            block = (
                hx[r - h + side, tokens, :].astype(F32) + total[:, k * FEAT : (k + 1) * FEAT]
            ).astype(BF16)
            mid[side, tokens, :] = block
            midg[r - h + side, tokens, :] = block
        mid_ring.begin(m)

    def sums(m):
        def copy_of(i, p):
            return Copy(
                lambda: part.at[p, aligned(m, LMAX)],
                lambda: got.at[r, aligned(m, LMAX)],
                send_sem,
                recv_sem,
                m * (N_ROW - 1) + i,
                (p, c),
            )

        return [copy_of(i, p) for i, p in enumerate(rows)]

    def channel(m):
        mid_ring.last(m)
        tokens = aligned(m, LMAX)
        z = normed(midg, m, 2)
        blend = (z + step_back(z) * shift[5:6, :]).astype(BF16)
        for side, weight in enumerate((held, theirs)):
            act = jnp.square(jnp.maximum(dot(blend, weight[0].reshape(WIDTH, MINE)), 0.0))
            act_scr[side] = act.astype(BF16)

        @pl.loop(0, N_CHIP)
        def _(n):
            total = None
            for side, weight in enumerate((held, theirs)):
                rows_n = weight[1, pl.ds(2 * n, 2)].reshape(SLICE, MINE)
                term = dot(act_scr[side], rows_n, ((1,), (1,)))
                total = term if total is None else total + term
            for side in range(2):
                added = jnp.where(n == q, mid[side, tokens, :].astype(F32), 0.0)
                part[2 * n + side, tokens, :] = (
                    total[:, side * FEAT : (side + 1) * FEAT] + added
                ).astype(BF16)

        for copy in sums(m):
            copy.start()
        got[r, tokens, :] = part[r, tokens, :]

    def source_rows(m, i):
        return pl.ds(pl.multiple_of(lax.rem(h + i, 2) * MINE + m * LMAX, LMAX), LMAX)

    def turn(m, i):
        return pltpu.make_async_remote_copy(
            src_ref=out.at[source_rows(m, i)],
            dst_ref=nx.at[2 * q + h, aligned(m, LMAX)],
            send_sem=send_sem.at[N_SUM + 2 * m + i],
            recv_sem=recv_sem.at[N_SUM + 2 * m + h],
            device_id=target(i),
            device_id_type=MESH,
        )

    def add_up(m):
        for copy in sums(m):
            copy.wait_recv()
        tokens = aligned(m, LMAX)
        for side in range(2):
            total = got[side, tokens, :].astype(F32)
            for k in range(1, N_CHIP):
                total += got[2 * k + side, tokens, :].astype(F32)
            rows_m = pl.ds(pl.multiple_of(side * MINE + m * LMAX, LMAX), LMAX)
            out[rows_m, :] = total.astype(BF16)

        @pl.when(q == c)
        def _():
            keep(
                out.at[source_rows(m, 0)],
                nx.at[r, aligned(m, LMAX)],
                recv_sem.at[N_SUM + 2 * m + h],
            )

        @pl.when(q != c)
        def _():
            turn(m, 0).start()

        turn(m, 1).start()

    def spread(m):
        for k in range(2):
            block = nx.at[2 * c + k, aligned(m, LMAX)]
            pltpu.make_async_copy(block, block, recv_sem.at[N_SUM + 2 * m + k]).wait()
        for copy in out_sends(m):
            copy.start()

    def project_next(m):
        for copy in out_sends(m):
            copy.wait_recv()
        z = normed(nx, m, 4)
        dz = step_back(z)
        for j in range(3):
            blend = (z + dz * shift[6 + j : 7 + j, :]).astype(BF16)
            next_rkv[j, aligned(m, LMAX), :] = dot(
                blend, wng[:, :, j].reshape(WIDTH, SLICE)
            ).astype(BF16)

    stages = (
        core,
        att_ring.forward,
        att_ring.close,
        project,
        mid_ring.forward,
        mid_ring.close,
        channel,
        add_up,
        spread,
        project_next,
    )
    end = object()

    def wait_mlp():
        for copy in local():
            copy.wait()
        for copy in links.open:
            copy.wait_recv()
        links.open = []

    def send_state():
        @pl.when(q == c)
        def _():
            keep(state, final, recv_sem.at[N_TURN])

        @pl.when(q != c)
        def _():
            move_state.start()

    def wait_far():
        for copy in far_links.open:
            copy.wait_recv()
        far_links.open = []

    beside = {
        0: [weights, keys, values, weights, keys, values],
        2: [weights, keys, values, lambda: links.arrive(links.copies[0])],
        3: [send_state],
        4: [weights, keys, values],
        5: [wait_mlp],
        8: [wait_far],
    }

    @pl.loop(0, PROMPTS + len(stages) - 1)
    def _(t):
        for lag, stage in enumerate(stages):

            @pl.when((t >= lag) & (t < PROMPTS + lag))
            def _():
                stage(t - lag)

        for at, works in beside.items():

            @pl.when(t == at)
            def _():
                for work in works:
                    if callable(work):
                        work()
                    else:
                        next(work, end)

    @pl.loop(0, PROMPTS)
    def _(m):
        for copy in sums(m) + out_sends(m):
            copy.wait_send()
        for prompt_ring in (att_ring, mid_ring):
            prompt_ring.sent(m)

        @pl.when(q != c)
        def _():
            turn(m, 0).wait_send()

        turn(m, 1).wait_send()

    pltpu.make_async_copy(state, final, recv_sem.at[N_TURN]).wait()

    @pl.when(q != c)
    def _():
        move_state.wait_send()

    for copy in links.copies + far_links.copies:
        copy.wait_send()


def per_device(
    hidden,
    lengths,
    square_matrix_shards,
    channel_mix_shards,
    lowrank_down,
    lowrank_up,
    token_shift_weights,
    attention_coefficients,
    norm_parameters,
):
    hx, wt, w3, wk, wv, wn, parg = exchange(
        start_kernel,
        [
            ((N_ROW, MINE, FEAT), BF16),
            ((2, 3, N_ROW, N_COL, 16, FEAT), BF16),
            ((N_COL, 16, WIDTH), BF16),
            ((N_COL, N_ROW, 16, MINE), BF16),
            ((N_COL, N_ROW, 16, MINE), BF16),
            ((N_ROW, N_COL, 3, 16, SLICE), BF16),
            ((N_ROW, 6, FEAT), F32),
        ],
        15 + 1 + 3 * RING + 1 + 14 + 15 + 15 + 7 + 15,
        9,
        1,
        square_matrix_shards,
        channel_mix_shards,
        norm_parameters,
        hidden,
        scratch=[
            pltpu.VMEM(square_matrix_shards.shape, F32),
            pltpu.VMEM(channel_mix_shards.shape, F32),
            pltpu.VMEM(square_matrix_shards.shape, BF16),
            pltpu.VMEM(channel_mix_shards.shape, BF16),
        ],
    )
    lowrank = lowrank_down.shape[2]
    out_hidden, next_rkv, final = exchange(
        body_kernel,
        [
            ((2 * MINE, FEAT), BF16),
            ((3, MINE, SLICE), BF16),
            ((PROMPTS, 2, HEAD, FEAT), BF16),
        ],
        N_ALL,
        3,
        2,
        lengths,
        hx,
        parg,
        token_shift_weights,
        wt,
        lowrank_down.transpose(0, 2, 1),
        attention_coefficients,
        lowrank_up,
        w3,
        wk,
        wv,
        wn,
        scratch=[
            pltpu.VMEM((3, LMAX, SLICE), F32),
            pltpu.VMEM((2, LMAX, lowrank), F32),
            pltpu.VMEM((PROMPTS, 2, HEAD, FEAT), BF16),
            pltpu.VMEM((2, MINE, FEAT), BF16),
            pltpu.VMEM((N_ROW, MINE, FEAT), BF16),
            pltpu.VMEM((N_COL, 16, WIDTH), BF16),
            pltpu.VMEM((2, MINE, FEAT), BF16),
            pltpu.VMEM((N_ROW, MINE, FEAT), BF16),
            pltpu.VMEM((2, N_ROW, N_COL, 16, MINE), BF16),
            pltpu.VMEM((2, N_ROW, N_COL, 16, MINE), BF16),
            pltpu.VMEM((2, LMAX, MINE), BF16),
            pltpu.VMEM((N_ROW, MINE, FEAT), BF16),
            pltpu.VMEM((N_ROW, MINE, FEAT), BF16),
            pltpu.VMEM((N_ROW, MINE, FEAT), BF16),
            pltpu.VMEM((N_ROW, N_COL, 3, 16, SLICE), BF16),
        ],
        in_specs=[pl.BlockSpec(memory_space=pltpu.SMEM)] + [VMEM] * 8 + [ANY] * 3,
        out_specs=[VMEM, VMEM, ANY],
    )
    final = final.reshape(4, 2, HEAD, 2, HEAD).transpose(0, 1, 3, 2, 4).astype(F32)
    final_state = final.reshape(4, 4, HEAD * HEAD)
    return (out_hidden, next_rkv, final_state)


def solution(mesh):
    return jax.shard_map(
        per_device,
        mesh=mesh,
        in_specs=(
            P("col", "row"),
            P(),
            P(None, ("row", "col"), None),
            P(None, ("row", "col"), None),
            P(),
            P(),
            P(),
            P(),
            P(None, "row"),
        ),
        out_specs=(P("col", "row"), P(None, "row", "col"), P("row", "col", None)),
        check_vma=False,
    )
```

```python
import functools

import jax
import jax.numpy as jnp
from jax import lax
from jax.experimental import pallas as pl
from jax.experimental.pallas import tpu as pltpu
from jax.sharding import PartitionSpec as P

WIDTH = 2048
HEAD = 64
LMAX = 128
F32 = jnp.float32
BF16 = jnp.bfloat16
MESH = pl.DeviceIdType.MESH
ANY = pl.BlockSpec(memory_space=pl.ANY)
VMEM = pl.BlockSpec(memory_space=pltpu.VMEM)
N_ROW = 16
N_COL = 8
N_CHIP = 8
MINE = 512
FEAT = 128
SLICE = 256


def greet(devices):
    barrier = pltpu.get_barrier_semaphore()
    for device in devices:
        pl.semaphore_signal(barrier, inc=1, device_id=device, device_id_type=MESH)
    pl.semaphore_wait(barrier, len(devices))


class Copy:
    def __init__(self, source, target, send_sem, recv_sem, slot, device):
        self.made = lambda: pltpu.make_async_remote_copy(
            src_ref=source() if callable(source) else source,
            dst_ref=target() if callable(target) else target,
            send_sem=send_sem.at[slot],
            recv_sem=recv_sem.at[slot],
            device_id=device,
            device_id_type=MESH,
        )

    def start(self):
        self.made().start()

    def wait_recv(self):
        self.made().wait_recv()

    def wait_send(self):
        self.made().wait_send()


def keep(source, target, sem):
    copy = pltpu.make_async_copy(source, target, sem)
    copy.start()
    return copy


def exchange(
    kernel,
    outs,
    n_remote,
    n_local,
    collective_id,
    *operands,
    scratch=(),
    in_specs=None,
    out_specs=None,
):
    return pl.pallas_call(
        kernel,
        out_shape=[jax.ShapeDtypeStruct(*out) for out in outs],
        in_specs=in_specs or [ANY] * len(operands),
        out_specs=out_specs or [ANY] * len(outs),
        scratch_shapes=[
            pltpu.SemaphoreType.DMA((n_remote,)),
            pltpu.SemaphoreType.DMA((n_remote,)),
            pltpu.SemaphoreType.DMA((n_local,)),
            *scratch,
        ],
        compiler_params=pltpu.CompilerParams(
            collective_id=collective_id, has_side_effects=True, vmem_limit_bytes=56 * 2**20
        ),
        cost_estimate=pl.CostEstimate(flops=0, bytes_accessed=48 * 2**20, transcendentals=0),
    )(*operands)


def place():
    r = lax.axis_index("row")
    c = lax.axis_index("col")
    h = lax.rem(r, 2)
    return r, c, h, lax.div(r, 2), r + 1 - 2 * h


class Links:
    def __init__(self, send_sem, recv_sem, first=0):
        self.send_sem = send_sem
        self.recv_sem = recv_sem
        self.slot = first
        self.copies = []
        self.open = []

    def go(self, source, target, device):
        copy = Copy(source, target, self.send_sem, self.recv_sem, self.slot, device)
        copy.start()
        self.slot += 1
        self.copies.append(copy)
        self.open.append(copy)
        return copy

    def arrive(self, copy):
        copy.wait_recv()
        self.open = [other for other in self.open if other is not copy]

    def finish(self):
        for copy in self.open:
            copy.wait_recv()
        for copy in self.copies:
            copy.wait_send()


RING = 14


def ring_at(axis):
    r, c, h, q, _ = place()
    here = q if axis == "row" else c
    step_z = 1 - 2 * lax.rem(here, 2)
    chips = {
        "p": lax.rem(here + 2, 8),
        "m": lax.rem(here + 6, 8),
        "z": here + step_z,
        "o": lax.rem(here + 4, 8),
        "pz": lax.rem(here + 2, 8) + step_z,
        "mz": lax.rem(here + 6, 8) + step_z,
        "oz": lax.rem(here + 4, 8) + step_z,
    }
    devices = {
        side: (2 * chips[side] + h, c) if axis == "row" else (r, chips[side]) for side in "pmz"
    }
    return here, chips, devices


def ring_peers(axis):
    return list(ring_at(axis)[2].values())


def ring(links, axis, slot, own=None, which=(0, 1), ready=None, seen=None, heavy=None, at=None):
    here, chips, to = at or ring_at(axis)
    heavy = axis == "row" if heavy is None else heavy
    seen = seen or (lambda chip, half: None)

    def take(copy, chip, half):
        links.arrive(copy)
        seen(chip, half)

    def forward(chip, half, side):
        return links.go(lambda: slot(chip, half), lambda: slot(chip, half), to[side])

    first = {}
    for k in range(2):
        if ready is not None:
            ready(k)
        target = functools.partial(slot, here, which[k])
        source = functools.partial(own, k) if own is not None else target
        for side in "zpm":
            first[side, k] = links.go(source, target, to[side])
    yield
    for k in range(2):
        take(first["p", k], chips["m"], which[k])
    low = forward(chips["m"], 0, "p")
    for k in range(2):
        take(first["m", k], chips["p"], which[k])
    high = forward(chips["p"], 1, "m")
    yield
    beside = {}
    for k in range(2):
        take(first["z", k], chips["z"], which[k])
        for side in "pm":
            beside[side, k] = forward(chips["z"], which[k], side)
    yield
    if heavy:
        take(low, chips["o"], 0)
        low = forward(chips["o"], 0, "z")
        take(high, chips["o"], 1)
        high = forward(chips["o"], 1, "z")
        yield
        for k in range(2):
            take(beside["p", k], chips["mz"], which[k])
            take(beside["m", k], chips["pz"], which[k])
    else:
        take(low, chips["o"], 0)
        take(high, chips["o"], 1)
        for k in range(2):
            take(beside["p", k], chips["mz"], which[k])
        low = forward(chips["mz"], 0, "p")
        for k in range(2):
            take(beside["m", k], chips["pz"], which[k])
        high = forward(chips["pz"], 1, "m")
        yield
    take(low, chips["oz"], 0)
    take(high, chips["oz"], 1)


def together(*steps):
    active = list(steps)
    while active:
        for step in list(active):
            if next(step, StopIteration) is StopIteration:
                active.remove(step)


def aligned(index, size):
    return pl.ds(pl.multiple_of(index * size, size), size)


def start_kernel(
    square_in,
    mlp_in,
    par,
    hid,
    hx,
    wt,
    w3,
    wk,
    wv,
    wn,
    parg,
    send_sem,
    recv_sem,
    local_sem,
    square_wide,
    mlp_wide,
    square,
    mlp,
):
    r, c, h, q, sibling = place()
    rows = [lax.rem(r + d, N_ROW) for d in range(1, N_ROW)]
    cols = [lax.rem(c + d, N_COL) for d in range(1, N_COL)]

    def time_part(p):
        return square.at[pl.ds(0, 3), :, aligned(p, FEAT)]

    def key_part(p):
        return mlp.at[0, :, aligned(p, MINE)]

    def value_part(p):
        return mlp.at[1, :, aligned(p, MINE)]

    def next_part(p):
        return square.at[pl.ds(4, 3), :, aligned(p, SLICE)]

    mine = hid.at[aligned(h, MINE)]
    square_load = keep(square_in, square_wide, local_sem.at[7])
    mlp_load = keep(mlp_in, mlp_wide, local_sem.at[8])
    local = [
        keep(par, parg.at[r], local_sem.at[1]),
        keep(mine, hx.at[r], local_sem.at[2]),
    ]
    greet([(p, c) for p in rows] + [(r, p) for p in cols])
    links = Links(send_sem, recv_sem)
    times = []
    own_time = []
    other = links.go(hid.at[aligned(1 - h, MINE)], hx.at[r], (sibling, c))

    def hid_own(k):
        return (mine, hx.at[sibling])[k]

    def hid_ready(k):
        if k == 1:
            links.arrive(other)

    def time_ready(k):
        if k == 0:
            for copy in times:
                links.arrive(copy)
            links.go(wt.at[h, :, :, c], wt.at[h, :, :, c], (sibling, c))

    def time_slot(chip, half):
        return wt.at[h, :, pl.ds(8 * half, 8), chip]

    def time_seen(chip, half):
        links.go(time_slot(chip, half), time_slot(chip, half), (sibling, c))

    def out_slot(chip, half):
        return w3.at[chip, :, pl.ds(1024 * half, 1024)]

    def out_own(k):
        return square.at[3, :, pl.ds(1024 * k, 1024)]

    def feed():
        square_load.wait()
        for j in range(3):
            square[j] = square_wide[j].astype(BF16)
        for p in rows:
            times.append(links.go(time_part(p), wt.at[lax.rem(p, 2), :, r, c], (p, c)))
        own_time.append(keep(time_part(r), wt.at[h, :, r, c], local_sem.at[0]))
        yield

    def casts():
        for j in range(3, 7):
            square[j] = square_wide[j].astype(BF16)
        mlp_load.wait()
        mlp[...] = mlp_wide[...].astype(BF16)
        own_time[0].wait()
        yield

    def rest():
        local.extend(
            [
                keep(square.at[3], w3.at[c], local_sem.at[3]),
                keep(key_part(r), wk.at[c, r], local_sem.at[4]),
                keep(value_part(r), wv.at[c, r], local_sem.at[5]),
                keep(next_part(c), wn.at[r, c], local_sem.at[6]),
            ]
        )
        for p in rows:
            links.go(par, parg.at[r], (p, c))
        yield
        for p in rows:
            links.go(key_part(p), wk.at[c, r], (p, c))
        for p in cols:
            links.go(next_part(p), wn.at[r, c], (r, p))
        for p in rows:
            links.go(value_part(p), wv.at[c, r], (p, c))

    together(
        feed(),
        ring(
            links,
            "row",
            lambda chip, side: hx.at[2 * chip + side],
            own=hid_own,
            which=(h, 1 - h),
            ready=hid_ready,
        ),
        casts(),
        ring(links, "col", time_slot, ready=time_ready, seen=time_seen),
        rest(),
        ring(links, "col", out_slot, own=out_own),
    )
    links.finish()
    for copy in local:
        copy.wait()


def dot(a, b, dims=((1,), (0,))):
    return lax.dot_general(a, b, (dims, ((), ())), preferred_element_type=F32)


def split(x):
    high = x.astype(BF16)
    return high, (x - high.astype(F32)).astype(BF16)


def dot3(a, b, dims=((1,), (0,))):
    a_high, a_low = a
    b_high, b_low = b
    return dot(a_high, b_high, dims) + (dot(a_high, b_low, dims) + dot(a_low, b_high, dims))


def norm(source, gain, bias):
    center = jnp.sum(source, axis=-1, keepdims=True) / WIDTH
    second = jnp.sum(source * source, axis=-1, keepdims=True) / WIDTH
    scaled = (source - center) * lax.rsqrt(second - center * center + 1e-05)
    return (scaled * gain + bias).astype(BF16).astype(F32)


def row_of(par, i):
    return jnp.concatenate([par[j, i : i + 1, :] for j in range(N_ROW)], axis=1)


def step_back(z):
    position = lax.rem(lax.broadcasted_iota(jnp.int32, z.shape, 0), LMAX)
    return jnp.where(position == 0, 0.0, pltpu.roll(z, 1, 0)) - z


def one_prompt(prompt, lens, rkv, low, coef, up, att, final):
    r, c, h, q, _ = place()
    length = lens[c * 8 + h * 4 + prompt]
    tokens = aligned(prompt, LMAX)
    wide = SLICE
    channels = aligned(q, SLICE)
    heads = wide // HEAD
    live = (lax.broadcasted_iota(jnp.int32, (LMAX, wide), 0) < length).astype(F32)
    lane = lax.broadcasted_iota(jnp.int32, (LMAX, wide), 1) // HEAD
    t = lax.broadcasted_iota(jnp.int32, (LMAX, LMAX), 0)
    u = lax.broadcasted_iota(jnp.int32, (LMAX, LMAX), 1)
    seg = (
        lax.broadcasted_iota(jnp.int32, (wide, wide), 0) // HEAD
        == lax.broadcasted_iota(jnp.int32, (wide, wide), 1) // HEAD
    ).astype(F32).astype(BF16)
    lower = (t >= u).astype(F32).astype(BF16)

    def head_sum(x):
        high, low_part = split(x)
        return dot(high, seg) + dot(low_part, seg)

    def only(x, k):
        return jnp.where(lane == k, x, jnp.zeros_like(x))

    receptance, key, value = rkv[0], rkv[1], rkv[2]
    decay = (
        -0.606531
        * jax.nn.sigmoid(coef[0:1, channels] + dot(jnp.tanh(low[0]).astype(BF16), up[0, :, channels]))
        * live
    )
    rate = jax.nn.sigmoid(coef[1:2, channels] + dot(low[1].astype(BF16), up[1, :, channels]))
    kappa = key * coef[2:3, channels]
    kappa = kappa * lax.rsqrt(head_sum(kappa * kappa) + 1e-05)
    remove = -kappa * live
    write = kappa * rate * live
    key = key * live
    value = value * live
    d_high, d_rest = split(decay)
    d_mid, d_low = split(decay - d_high.astype(F32))
    total = dot(lower, d_high) + (dot(lower, d_mid) + dot(lower, d_low))
    middle = total[LMAX // 2 - 1 : LMAX // 2, :]
    last = total[LMAX - 1 : LMAX, :]
    back = jnp.exp(middle - total)
    pull = split(remove * jnp.exp(total - decay - middle))
    read = split(receptance * jnp.exp(total - middle))
    write_back = split(write * back)
    key_back = split(key * back)
    value_parts = split(value)

    left = tuple(
        jnp.concatenate([x for k in range(heads) for x in (only(pull[i], k), only(read[i], k))])
        for i in range(2)
    )
    right = tuple(jnp.concatenate([write_back[i], key_back[i]]) for i in range(2))
    pairs = dot3(left, right, ((1,), (1,)))
    strict = t > u
    t2 = lax.broadcasted_iota(jnp.int32, (LMAX, 2 * LMAX), 0)
    u2 = lax.rem(lax.broadcasted_iota(jnp.int32, (LMAX, 2 * LMAX), 1), LMAX)
    upto = t2 >= u2
    solves, pull_key, reads = [], [], []
    for k in range(heads):
        base = k * 2 * LMAX
        system = jnp.where(strict, pairs[base : base + LMAX, :LMAX], 0.0)
        pull_key.append(split(jnp.where(strict, pairs[base : base + LMAX, LMAX:], 0.0)))
        reads.append(split(jnp.where(upto, pairs[base + LMAX : base + 2 * LMAX], 0.0)))
        solves.append(system)
    inverse = []
    for k in range(heads):
        near = (t // 2 == u // 2)
        inverse.append(
            jnp.where(near, solves[k], 0.0) + (t == u).astype(F32)
        )
    size = 2
    while size < LMAX:
        inside = (t // (2 * size) == u // (2 * size)) & (t // size != u // size)
        grown = []
        for k in range(heads):
            known = split(inverse[k])
            cross = split(jnp.where(inside, solves[k], 0.0))
            product = split(dot3(known, cross))
            grown.append(inverse[k] + dot3(product, known))
        inverse = grown
        size *= 2

    def across(mats, parts):
        wide_left = tuple(jnp.concatenate([mat[i] for mat in mats], axis=1) for i in range(2))
        tall = tuple(
            jnp.concatenate([only(part[i], k) for k in range(heads) for part in parts])
            for i in range(2)
        )
        return dot3(wide_left, tall)

    start = across(pull_key, [value_parts])
    pulled = split(across([split(x) for x in inverse], [split(start)]))
    output = across(reads, [pulled, value_parts])
    tail = jnp.exp(last - total)
    write_tail = split(write * tail)
    key_tail = split(key * tail)
    tall = tuple(jnp.concatenate([pulled[i], value_parts[i]]) for i in range(2))
    tails = tuple(jnp.concatenate([write_tail[i], key_tail[i]]) for i in range(2))
    state = dot3(tall, tails, ((0,), (0,)))
    even = lax.broadcasted_iota(jnp.int32, (HEAD, FEAT), 1) < HEAD
    for k in range(heads // 2):
        lanes = slice(k * FEAT, (k + 1) * FEAT)
        final[prompt, k] = jnp.where(
            even,
            state[k * FEAT : k * FEAT + HEAD, lanes],
            state[k * FEAT + HEAD : (k + 1) * FEAT, lanes],
        ).astype(BF16)
    bonus = head_sum(receptance * key * coef[3:4, channels])
    out = (output + bonus * value) * live
    center = head_sum(out) * (1.0 / HEAD)
    out = out - center
    spread = head_sum(out * out) * (1.0 / HEAD)
    out = (out * lax.rsqrt(spread + 0.00064) * coef[4:5, channels] + coef[5:6, channels]).astype(BF16)
    for side in range(2):
        att[side, tokens] = out[:, side * FEAT : (side + 1) * FEAT]


PROMPTS = MINE // LMAX
HOPS = 9


class PromptRing:
    def __init__(self, send_sem, recv_sem, base, axis, own, got):
        self.send_sem = send_sem
        self.recv_sem = recv_sem
        self.base = base
        self.here, self.chips, self.to = ring_at(axis)
        self.own = own
        self.got = got
        self.heavy = axis == "row"

    def hop(self, m, slot, chip, side, half=None):
        def block():
            at = self.chips.get(chip, self.here)
            if half is None:
                return self.got.at[pl.ds(2 * at, 2), aligned(m, LMAX)]
            return self.got.at[2 * at + half, aligned(m, LMAX)]

        def source():
            if chip == "own" and self.own is not None:
                return self.own.at[:, aligned(m, LMAX)]
            return block()

        return Copy(
            source,
            block,
            self.send_sem,
            self.recv_sem,
            self.base + m * HOPS + slot,
            self.to[side],
        )

    def hops(self, m):
        return [
            self.hop(m, 0, "own", "p"),
            self.hop(m, 1, "own", "m"),
            self.hop(m, 2, "own", "z"),
            self.hop(m, 3, "m", "p", 0),
            self.hop(m, 4, "p", "m", 1),
            self.hop(m, 5, "z", "p"),
            self.hop(m, 6, "z", "m"),
            self.hop(m, 7, "o", "z", 0) if self.heavy else self.hop(m, 7, "mz", "p", 0),
            self.hop(m, 8, "o", "z", 1) if self.heavy else self.hop(m, 8, "pz", "m", 1),
        ]

    def begin(self, m):
        copies = self.hops(m)
        for k in (2, 0, 1):
            copies[k].start()

    def forward(self, m):
        copies = self.hops(m)
        copies[0].wait_recv()
        copies[3].start()
        copies[1].wait_recv()
        copies[4].start()
        copies[2].wait_recv()
        copies[5].start()
        copies[6].start()

    def close(self, m):
        copies = self.hops(m)
        for early, late in ((3, 7), (4, 8)) if self.heavy else ((6, 8), (5, 7)):
            copies[early].wait_recv()
            copies[late].start()

    def last(self, m):
        for k in (5, 6, 7, 8) if self.heavy else (3, 4, 7, 8):
            self.hops(m)[k].wait_recv()

    def sent(self, m):
        for copy in self.hops(m):
            copy.wait_send()


N_SUM = PROMPTS * 9
N_TURN = N_SUM + 2 * PROMPTS
N_STATE = N_TURN + 1
N_WEIGHT = N_STATE + 3 * PROMPTS * HOPS
N_ALL = N_WEIGHT + 1 + 2 * (1 + 14 + RING) + 1 + 14 + RING


def body_kernel(
    lens,
    hx,
    par,
    shift,
    wt,
    down,
    coef,
    up,
    w3,
    wk,
    wv,
    wn,
    out,
    next_rkv,
    final,
    send_sem,
    recv_sem,
    local_sem,
    rkv,
    low,
    state,
    att,
    attg,
    w3x,
    mid,
    midg,
    held,
    theirs,
    act_scr,
    part,
    got,
    summed,
    fin,
    nx,
    wng,
):
    r, c, h, q, sibling = place()
    x_here = lax.div(r, 4)
    x_plus, x_over, x_minus = (lax.rem(x_here + d, 4) for d in range(1, 4))
    z_row = 4 * x_here + 2 * (1 - lax.rem(q, 2))

    def local():
        return [
            pltpu.make_async_copy(wk.at[c], held.at[0, :, c], local_sem.at[0]),
            pltpu.make_async_copy(wv.at[c], held.at[1, :, c], local_sem.at[1]),
            pltpu.make_async_copy(wn.at[r], wng.at[r], local_sem.at[2]),
        ]

    for copy in local():
        copy.start()

    def target(i):
        return (2 * c + lax.rem(h + i, 2), q)

    barrier = pltpu.get_barrier_semaphore()
    peers = [(lax.rem(r + 4, N_ROW), c), (lax.rem(r + 12, N_ROW), c)] + ring_peers("col")
    peers += [(sibling, c), (z_row, c), (z_row + 1, c)]

    @pl.when(q != c)
    def _():
        for i in range(2):
            pl.semaphore_signal(barrier, inc=1, device_id=target(i), device_id_type=MESH)

    for device in peers:
        pl.semaphore_signal(barrier, inc=1, device_id=device, device_id_type=MESH)
    pl.semaphore_wait(barrier, len(peers) + 2 * (q != c).astype(jnp.int32))

    links = Links(send_sem, recv_sem, N_WEIGHT)
    links.go(w3, w3x, (sibling, c))

    col_place = ring_at("col")

    def mlp_ring(which, source):
        def slot(chip, half):
            return held.at[which, pl.ds(8 * half, 8), chip]

        def over(chip, half):
            return theirs.at[which, pl.ds(8 * half, 8), chip]

        def seen(chip, half):
            links.go(lambda: slot(chip, half), lambda: over(chip, half), (sibling, c))

        def begin():
            links.go(lambda: source.at[c], lambda: theirs.at[which, :, c], (sibling, c))
            yield from ring(
                links,
                "col",
                slot,
                own=lambda k: source.at[c, pl.ds(8 * k, 8)],
                seen=seen,
                at=col_place,
            )

        return begin()

    def weight_slot(chip, half):
        return wng.at[2 * chip + h, pl.ds(4 * half, 4)]

    far_links = Links(send_sem, recv_sem, N_ALL - 1 - 14 - RING)

    def weight_seen(chip, half):
        far_links.go(
            lambda: weight_slot(chip, half), lambda: weight_slot(chip, half), (sibling, c)
        )

    def weight_ring():
        far_links.go(lambda: wn.at[r], lambda: wng.at[r], (sibling, c))
        yield from ring(
            far_links,
            "row",
            weight_slot,
            own=lambda k: wn.at[r, pl.ds(4 * k, 4)],
            seen=weight_seen,
            heavy=False,
        )

    keys = mlp_ring(0, wk)
    values = mlp_ring(1, wv)
    weights = weight_ring()
    for steps in (weights, keys, values):
        next(steps)

    att_ring = PromptRing(send_sem, recv_sem, N_STATE, "row", att, attg)
    mid_ring = PromptRing(send_sem, recv_sem, N_STATE + PROMPTS * HOPS, "row", mid, midg)
    out_ring = PromptRing(send_sem, recv_sem, N_STATE + 2 * PROMPTS * HOPS, "col", None, nx)
    move_state = Copy(state, final, send_sem, recv_sem, N_TURN, target(0))

    def wide(ref, m):
        return jnp.concatenate([ref[j, aligned(m, LMAX), :] for j in range(N_ROW)], axis=1)

    def normed(ref, m, k):
        return norm(wide(ref, m).astype(F32), row_of(par, k), row_of(par, k + 1))

    def blends(m):
        z = normed(hx, m, 0)
        dz = step_back(z)
        for j in range(5):
            blend = (z + dz * shift[j : j + 1, :]).astype(BF16)
            if j < 3:
                weight = jnp.concatenate(
                    [wt[side, j].reshape(WIDTH, FEAT) for side in range(2)], axis=1
                )
                rkv[j] = dot(blend, weight)
            else:
                low[j - 3] = dot(blend, down[j - 3], ((1,), (1,)))

    def core(m):
        blends(m)
        one_prompt(m, lens, rkv, low, coef, up, att, state)
        att_ring.begin(m)
        for side in range(2):
            attg[2 * q + side, aligned(m, LMAX)] = att[side, aligned(m, LMAX)]

    def project(m):
        att_ring.last(m)
        tokens = aligned(m, LMAX)
        weight = jnp.concatenate([w[...].reshape(FEAT, WIDTH) for w in (w3, w3x)])
        total = dot(wide(attg, m), weight, ((1,), (1,)))
        for k, side in enumerate((h, 1 - h)):
            block = (
                hx[r - h + side, tokens, :].astype(F32) + total[:, k * FEAT : (k + 1) * FEAT]
            ).astype(BF16)
            mid[side, tokens, :] = block
            midg[r - h + side, tokens, :] = block
        mid_ring.begin(m)

    def x_move(m, k):
        tokens = aligned(m, LMAX)
        source, first, target_at, step = (
            (part, 4 * x_over, 0, 4),
            (part, 4 * x_over + 2, 2, 12),
            (part, 4 * x_plus + 2, 6, 4),
            (part, 4 * x_minus, 8, 12),
            (got, 12, 4, 4),
            (got, 14, 10, 12),
        )[k]
        return pltpu.make_async_remote_copy(
            src_ref=source.at[pl.ds(first, 2), tokens],
            dst_ref=got.at[pl.ds(target_at, 2), tokens],
            send_sem=send_sem.at[9 * m + k],
            recv_sem=recv_sem.at[9 * m + k],
            device_id=(lax.rem(r + step, N_ROW), c),
            device_id_type=MESH,
        )

    def plane_move(m, k):
        there = sibling if k == 0 else z_row + k - 1
        own_k = 0 if k == 0 else 1 + h
        return pltpu.make_async_remote_copy(
            src_ref=summed.at[there - 4 * x_here, aligned(m, LMAX)],
            dst_ref=fin.at[(0 if k == 0 else 2) + h, aligned(m, LMAX)],
            send_sem=send_sem.at[9 * m + 6 + k],
            recv_sem=recv_sem.at[9 * m + 6 + own_k],
            device_id=(there, c),
            device_id_type=MESH,
        )

    def channel(m):
        mid_ring.last(m)
        tokens = aligned(m, LMAX)
        z = normed(midg, m, 2)
        blend = (z + step_back(z) * shift[5:6, :]).astype(BF16)
        for side, weight in enumerate((held, theirs)):
            act = jnp.square(jnp.maximum(dot(blend, weight[0].reshape(WIDTH, MINE)), 0.0))
            act_scr[side] = act.astype(BF16)

        @pl.loop(0, N_CHIP)
        def _(n):
            total = None
            for side, weight in enumerate((held, theirs)):
                rows_n = weight[1, pl.ds(2 * n, 2)].reshape(SLICE, MINE)
                term = dot(act_scr[side], rows_n, ((1,), (1,)))
                total = term if total is None else total + term
            for side in range(2):
                added = jnp.where(n == q, mid[side, tokens, :].astype(F32), 0.0)
                part[2 * n + side, tokens, :] = (
                    total[:, side * FEAT : (side + 1) * FEAT] + added
                ).astype(BF16)

        for k in range(4):
            x_move(m, k).start()

    def relay(m):
        tokens = aligned(m, LMAX)
        for k, other in enumerate((x_plus, x_minus)):
            x_move(m, k).wait_recv()
            for j in range(2):
                added = part[4 * other + 2 * k + j, tokens, :].astype(F32)
                got[12 + 2 * k + j, tokens, :] = (
                    got[2 * k + j, tokens, :].astype(F32) + added
                ).astype(BF16)
            x_move(m, 4 + k).start()

    def plane_sum(m):
        tokens = aligned(m, LMAX)
        for k in range(2, 6):
            x_move(m, k).wait_recv()
        for k, places in enumerate(((4, 8), (5, 9), (10, 6), (11, 7))):
            total = part[4 * x_here + k, tokens, :].astype(F32)
            for j in places:
                total += got[j, tokens, :].astype(F32)
            summed[k, tokens, :] = total.astype(BF16)
        for k in (1, 2, 0):
            plane_move(m, k).start()
        fin[h, tokens, :] = summed[r - 4 * x_here, tokens, :]

    def source_rows(m, i):
        return pl.ds(pl.multiple_of(lax.rem(h + i, 2) * MINE + m * LMAX, LMAX), LMAX)

    def turn(m, i):
        return pltpu.make_async_remote_copy(
            src_ref=out.at[source_rows(m, i)],
            dst_ref=nx.at[2 * q + h, aligned(m, LMAX)],
            send_sem=send_sem.at[N_SUM + 2 * m + i],
            recv_sem=recv_sem.at[N_SUM + 2 * m + h],
            device_id=target(i),
            device_id_type=MESH,
        )

    def add_up(m):
        tokens = aligned(m, LMAX)
        for k in range(3):
            block = fin.at[0, tokens]
            pltpu.make_async_copy(block, block, recv_sem.at[9 * m + 6 + k]).wait()
        for side in range(2):
            total = fin[side, tokens, :].astype(F32) + fin[2 + side, tokens, :].astype(F32)
            rows_m = pl.ds(pl.multiple_of(side * MINE + m * LMAX, LMAX), LMAX)
            out[rows_m, :] = total.astype(BF16)

        @pl.when(q == c)
        def _():
            keep(
                out.at[source_rows(m, 0)],
                nx.at[r, aligned(m, LMAX)],
                recv_sem.at[N_SUM + 2 * m + h],
            )

        @pl.when(q != c)
        def _():
            turn(m, 0).start()

        turn(m, 1).start()

    def spread(m):
        for k in range(2):
            block = nx.at[2 * c + k, aligned(m, LMAX)]
            pltpu.make_async_copy(block, block, recv_sem.at[N_SUM + 2 * m + k]).wait()
        out_ring.begin(m)

    def project_next(m):
        out_ring.last(m)
        z = normed(nx, m, 4)
        dz = step_back(z)
        for j in range(3):
            blend = (z + dz * shift[6 + j : 7 + j, :]).astype(BF16)
            next_rkv[j, aligned(m, LMAX), :] = dot(
                blend, wng[:, :, j].reshape(WIDTH, SLICE)
            ).astype(BF16)

    stages = (
        core,
        att_ring.forward,
        att_ring.close,
        project,
        mid_ring.forward,
        mid_ring.close,
        channel,
        relay,
        plane_sum,
        add_up,
        spread,
        out_ring.forward,
        out_ring.close,
        project_next,
    )
    end = object()

    def wait_mlp():
        for copy in local():
            copy.wait()
        for copy in links.open:
            copy.wait_recv()
        links.open = []

    def send_state():
        @pl.when(q == c)
        def _():
            keep(state, final, recv_sem.at[N_TURN])

        @pl.when(q != c)
        def _():
            move_state.start()

    def wait_far():
        for copy in far_links.open:
            copy.wait_recv()
        far_links.open = []

    beside = {
        0: [weights, keys, values, weights, keys, values],
        2: [weights, keys, values, lambda: links.arrive(links.copies[0])],
        3: [send_state],
        4: [weights, keys, values],
        5: [wait_mlp],
        12: [wait_far],
    }

    @pl.loop(0, PROMPTS + len(stages) - 1)
    def _(t):
        for lag, stage in enumerate(stages):

            @pl.when((t >= lag) & (t < PROMPTS + lag))
            def _():
                stage(t - lag)

        for at, works in beside.items():

            @pl.when(t == at)
            def _():
                for work in works:
                    if callable(work):
                        work()
                    else:
                        next(work, end)

    @pl.loop(0, PROMPTS)
    def _(m):
        for k in range(6):
            x_move(m, k).wait_send()
        for k in range(3):
            plane_move(m, k).wait_send()
        for prompt_ring in (att_ring, mid_ring, out_ring):
            prompt_ring.sent(m)

        @pl.when(q != c)
        def _():
            turn(m, 0).wait_send()

        turn(m, 1).wait_send()

    pltpu.make_async_copy(state, final, recv_sem.at[N_TURN]).wait()

    @pl.when(q != c)
    def _():
        move_state.wait_send()

    for copy in links.copies + far_links.copies:
        copy.wait_send()


def per_device(
    hidden,
    lengths,
    square_matrix_shards,
    channel_mix_shards,
    lowrank_down,
    lowrank_up,
    token_shift_weights,
    attention_coefficients,
    norm_parameters,
):
    hx, wt, w3, wk, wv, wn, parg = exchange(
        start_kernel,
        [
            ((N_ROW, MINE, FEAT), BF16),
            ((2, 3, N_ROW, N_COL, 16, FEAT), BF16),
            ((N_COL, 16, WIDTH), BF16),
            ((N_COL, N_ROW, 16, MINE), BF16),
            ((N_COL, N_ROW, 16, MINE), BF16),
            ((N_ROW, N_COL, 3, 16, SLICE), BF16),
            ((N_ROW, 6, FEAT), F32),
        ],
        15 + 1 + 3 * RING + 1 + 14 + 15 + 15 + 7 + 15,
        9,
        1,
        square_matrix_shards,
        channel_mix_shards,
        norm_parameters,
        hidden,
        scratch=[
            pltpu.VMEM(square_matrix_shards.shape, F32),
            pltpu.VMEM(channel_mix_shards.shape, F32),
            pltpu.VMEM(square_matrix_shards.shape, BF16),
            pltpu.VMEM(channel_mix_shards.shape, BF16),
        ],
    )
    lowrank = lowrank_down.shape[2]
    out_hidden, next_rkv, final = exchange(
        body_kernel,
        [
            ((2 * MINE, FEAT), BF16),
            ((3, MINE, SLICE), BF16),
            ((PROMPTS, 2, HEAD, FEAT), BF16),
        ],
        N_ALL,
        3,
        2,
        lengths,
        hx,
        parg,
        token_shift_weights,
        wt,
        lowrank_down.transpose(0, 2, 1),
        attention_coefficients,
        lowrank_up,
        w3,
        wk,
        wv,
        wn,
        scratch=[
            pltpu.VMEM((3, LMAX, SLICE), F32),
            pltpu.VMEM((2, LMAX, lowrank), F32),
            pltpu.VMEM((PROMPTS, 2, HEAD, FEAT), BF16),
            pltpu.VMEM((2, MINE, FEAT), BF16),
            pltpu.VMEM((N_ROW, MINE, FEAT), BF16),
            pltpu.VMEM((N_COL, 16, WIDTH), BF16),
            pltpu.VMEM((2, MINE, FEAT), BF16),
            pltpu.VMEM((N_ROW, MINE, FEAT), BF16),
            pltpu.VMEM((2, N_ROW, N_COL, 16, MINE), BF16),
            pltpu.VMEM((2, N_ROW, N_COL, 16, MINE), BF16),
            pltpu.VMEM((2, LMAX, MINE), BF16),
            pltpu.VMEM((N_ROW, MINE, FEAT), BF16),
            pltpu.VMEM((N_ROW, MINE, FEAT), BF16),
            pltpu.VMEM((4, MINE, FEAT), BF16),
            pltpu.VMEM((4, MINE, FEAT), BF16),
            pltpu.VMEM((N_ROW, MINE, FEAT), BF16),
            pltpu.VMEM((N_ROW, N_COL, 3, 16, SLICE), BF16),
        ],
        in_specs=[pl.BlockSpec(memory_space=pltpu.SMEM)] + [VMEM] * 8 + [ANY] * 3,
        out_specs=[VMEM, VMEM, ANY],
    )
    final = final.reshape(4, 2, HEAD, 2, HEAD).transpose(0, 1, 3, 2, 4).astype(F32)
    final_state = final.reshape(4, 4, HEAD * HEAD)
    return (out_hidden, next_rkv, final_state)


def solution(mesh):
    return jax.shard_map(
        per_device,
        mesh=mesh,
        in_specs=(
            P("col", "row"),
            P(),
            P(None, ("row", "col"), None),
            P(None, ("row", "col"), None),
            P(),
            P(),
            P(),
            P(),
            P(None, "row"),
        ),
        out_specs=(P("col", "row"), P(None, "row", "col"), P("row", "col", None)),
        check_vma=False,
    )
```

```python
import functools

import jax
import jax.numpy as jnp
from jax import lax
from jax.experimental import pallas as pl
from jax.experimental.pallas import tpu as pltpu
from jax.sharding import PartitionSpec as P

WIDTH = 2048
HEAD = 64
LMAX = 128
F32 = jnp.float32
BF16 = jnp.bfloat16
MESH = pl.DeviceIdType.MESH
ANY = pl.BlockSpec(memory_space=pl.ANY)
VMEM = pl.BlockSpec(memory_space=pltpu.VMEM)
N_ROW = 16
N_COL = 8
N_CHIP = 8
MINE = 512
FEAT = 128
SLICE = 256


def greet(devices):
    barrier = pltpu.get_barrier_semaphore()
    for device in devices:
        pl.semaphore_signal(barrier, inc=1, device_id=device, device_id_type=MESH)
    pl.semaphore_wait(barrier, len(devices))


class Copy:
    def __init__(self, source, target, send_sem, recv_sem, slot, device):
        self.made = lambda: pltpu.make_async_remote_copy(
            src_ref=source() if callable(source) else source,
            dst_ref=target() if callable(target) else target,
            send_sem=send_sem.at[slot],
            recv_sem=recv_sem.at[slot],
            device_id=device,
            device_id_type=MESH,
        )

    def start(self):
        self.made().start()

    def wait_recv(self):
        self.made().wait_recv()

    def wait_send(self):
        self.made().wait_send()


def keep(source, target, sem):
    copy = pltpu.make_async_copy(source, target, sem)
    copy.start()
    return copy


def exchange(
    kernel,
    outs,
    n_remote,
    n_local,
    collective_id,
    *operands,
    scratch=(),
    in_specs=None,
    out_specs=None,
):
    return pl.pallas_call(
        kernel,
        out_shape=[jax.ShapeDtypeStruct(*out) for out in outs],
        in_specs=in_specs or [ANY] * len(operands),
        out_specs=out_specs or [ANY] * len(outs),
        scratch_shapes=[
            pltpu.SemaphoreType.DMA((n_remote,)),
            pltpu.SemaphoreType.DMA((n_remote,)),
            pltpu.SemaphoreType.DMA((n_local,)),
            *scratch,
        ],
        compiler_params=pltpu.CompilerParams(
            collective_id=collective_id, has_side_effects=True, vmem_limit_bytes=56 * 2**20
        ),
        cost_estimate=pl.CostEstimate(flops=0, bytes_accessed=48 * 2**20, transcendentals=0),
    )(*operands)


def place():
    r = lax.axis_index("row")
    c = lax.axis_index("col")
    h = lax.rem(r, 2)
    return r, c, h, lax.div(r, 2), r + 1 - 2 * h


class Links:
    def __init__(self, send_sem, recv_sem, first=0):
        self.send_sem = send_sem
        self.recv_sem = recv_sem
        self.slot = first
        self.copies = []
        self.open = []

    def go(self, source, target, device):
        copy = Copy(source, target, self.send_sem, self.recv_sem, self.slot, device)
        copy.start()
        self.slot += 1
        self.copies.append(copy)
        self.open.append(copy)
        return copy

    def arrive(self, copy):
        copy.wait_recv()
        self.open = [other for other in self.open if other is not copy]

    def finish(self):
        for copy in self.open:
            copy.wait_recv()
        for copy in self.copies:
            copy.wait_send()


RING = 14


def ring_at(axis):
    r, c, h, q, _ = place()
    here = q if axis == "row" else c
    step_z = 1 - 2 * lax.rem(here, 2)
    chips = {
        "p": lax.rem(here + 2, 8),
        "m": lax.rem(here + 6, 8),
        "z": here + step_z,
        "o": lax.rem(here + 4, 8),
        "pz": lax.rem(here + 2, 8) + step_z,
        "mz": lax.rem(here + 6, 8) + step_z,
        "oz": lax.rem(here + 4, 8) + step_z,
    }
    devices = {
        side: (2 * chips[side] + h, c) if axis == "row" else (r, chips[side]) for side in "pmz"
    }
    return here, chips, devices


def ring_peers(axis):
    return list(ring_at(axis)[2].values())


def ring(links, axis, slot, own=None, which=(0, 1), ready=None, seen=None, heavy=None, at=None):
    here, chips, to = at or ring_at(axis)
    heavy = axis == "row" if heavy is None else heavy
    seen = seen or (lambda chip, half: None)

    def take(copy, chip, half):
        links.arrive(copy)
        seen(chip, half)

    def forward(chip, half, side):
        return links.go(lambda: slot(chip, half), lambda: slot(chip, half), to[side])

    first = {}
    for k in range(2):
        if ready is not None:
            ready(k)
        target = functools.partial(slot, here, which[k])
        source = functools.partial(own, k) if own is not None else target
        for side in "zpm":
            first[side, k] = links.go(source, target, to[side])
    yield
    for k in range(2):
        take(first["p", k], chips["m"], which[k])
    low = forward(chips["m"], 0, "p")
    for k in range(2):
        take(first["m", k], chips["p"], which[k])
    high = forward(chips["p"], 1, "m")
    yield
    beside = {}
    for k in range(2):
        take(first["z", k], chips["z"], which[k])
        for side in "pm":
            beside[side, k] = forward(chips["z"], which[k], side)
    yield
    if heavy:
        take(low, chips["o"], 0)
        low = forward(chips["o"], 0, "z")
        take(high, chips["o"], 1)
        high = forward(chips["o"], 1, "z")
        yield
        for k in range(2):
            take(beside["p", k], chips["mz"], which[k])
            take(beside["m", k], chips["pz"], which[k])
    else:
        take(low, chips["o"], 0)
        take(high, chips["o"], 1)
        for k in range(2):
            take(beside["p", k], chips["mz"], which[k])
        low = forward(chips["mz"], 0, "p")
        for k in range(2):
            take(beside["m", k], chips["pz"], which[k])
        high = forward(chips["pz"], 1, "m")
        yield
    take(low, chips["oz"], 0)
    take(high, chips["oz"], 1)


def together(*steps):
    active = list(steps)
    while active:
        for step in list(active):
            if next(step, StopIteration) is StopIteration:
                active.remove(step)


def aligned(index, size):
    return pl.ds(pl.multiple_of(index * size, size), size)


def start_kernel(
    square_in,
    mlp_in,
    par,
    hid,
    hx,
    wt,
    w3,
    wk,
    wv,
    wn,
    parg,
    send_sem,
    recv_sem,
    local_sem,
    square_wide,
    mlp_wide,
    square,
    mlp,
):
    r, c, h, q, sibling = place()
    rows = [lax.rem(r + d, N_ROW) for d in range(1, N_ROW)]
    cols = [lax.rem(c + d, N_COL) for d in range(1, N_COL)]

    def time_part(p):
        return square.at[pl.ds(0, 3), :, aligned(p, FEAT)]

    def key_part(p):
        return mlp.at[0, :, aligned(p, MINE)]

    def value_part(p):
        return mlp.at[1, :, aligned(p, MINE)]

    def next_part(p):
        return square.at[pl.ds(4, 3), :, aligned(p, SLICE)]

    mine = hid.at[aligned(h, MINE)]
    square_load = keep(square_in, square_wide, local_sem.at[7])
    mlp_load = keep(mlp_in, mlp_wide, local_sem.at[8])
    local = [
        keep(par, parg.at[r], local_sem.at[1]),
        keep(mine, hx.at[r], local_sem.at[2]),
    ]
    greet([(p, c) for p in rows] + [(r, p) for p in cols])
    links = Links(send_sem, recv_sem)
    times = []
    own_time = []
    other = links.go(hid.at[aligned(1 - h, MINE)], hx.at[r], (sibling, c))

    def hid_own(k):
        return (mine, hx.at[sibling])[k]

    def hid_ready(k):
        if k == 1:
            links.arrive(other)

    def time_ready(k):
        if k == 0:
            for copy in times:
                links.arrive(copy)
            links.go(wt.at[h, :, :, c], wt.at[h, :, :, c], (sibling, c))

    def time_slot(chip, half):
        return wt.at[h, :, pl.ds(8 * half, 8), chip]

    def time_seen(chip, half):
        links.go(time_slot(chip, half), time_slot(chip, half), (sibling, c))

    def out_slot(chip, half):
        return w3.at[chip, :, pl.ds(1024 * half, 1024)]

    def out_own(k):
        return square.at[3, :, pl.ds(1024 * k, 1024)]

    def feed():
        square_load.wait()
        for j in range(3):
            square[j] = square_wide[j].astype(BF16)
        for p in rows:
            times.append(links.go(time_part(p), wt.at[lax.rem(p, 2), :, r, c], (p, c)))
        own_time.append(keep(time_part(r), wt.at[h, :, r, c], local_sem.at[0]))
        yield

    def casts():
        for j in range(3, 7):
            square[j] = square_wide[j].astype(BF16)
        mlp_load.wait()
        mlp[...] = mlp_wide[...].astype(BF16)
        own_time[0].wait()
        yield

    def rest():
        local.extend(
            [
                keep(square.at[3], w3.at[c], local_sem.at[3]),
                keep(key_part(r), wk.at[c, r], local_sem.at[4]),
                keep(value_part(r), wv.at[c, r], local_sem.at[5]),
                keep(next_part(c), wn.at[r, c], local_sem.at[6]),
            ]
        )
        for p in rows:
            links.go(par, parg.at[r], (p, c))
        yield
        for p in rows:
            links.go(key_part(p), wk.at[c, r], (p, c))
        for p in cols:
            links.go(next_part(p), wn.at[r, c], (r, p))
        for p in rows:
            links.go(value_part(p), wv.at[c, r], (p, c))

    together(
        feed(),
        ring(
            links,
            "row",
            lambda chip, side: hx.at[2 * chip + side],
            own=hid_own,
            which=(h, 1 - h),
            ready=hid_ready,
        ),
        casts(),
        ring(links, "col", time_slot, ready=time_ready, seen=time_seen),
        rest(),
        ring(links, "col", out_slot, own=out_own),
    )
    links.finish()
    for copy in local:
        copy.wait()


def dot(a, b, dims=((1,), (0,))):
    return lax.dot_general(a, b, (dims, ((), ())), preferred_element_type=F32)


def split(x):
    high = x.astype(BF16)
    return high, (x - high.astype(F32)).astype(BF16)


def dot3(a, b, dims=((1,), (0,))):
    a_high, a_low = a
    b_high, b_low = b
    left = jnp.concatenate([a_high, a_high, a_low], axis=dims[0][0])
    right = jnp.concatenate([b_high, b_low, b_high], axis=dims[1][0])
    return dot(left, right, dims)


def norm(source, gain, bias):
    center = jnp.sum(source, axis=-1, keepdims=True) / WIDTH
    second = jnp.sum(source * source, axis=-1, keepdims=True) / WIDTH
    scaled = (source - center) * lax.rsqrt(second - center * center + 1e-05)
    return (scaled * gain + bias).astype(BF16).astype(F32)


def row_of(par, i):
    return jnp.concatenate([par[j, i : i + 1, :] for j in range(N_ROW)], axis=1)


def step_back(z):
    position = lax.rem(lax.broadcasted_iota(jnp.int32, z.shape, 0), LMAX)
    return jnp.where(position == 0, 0.0, pltpu.roll(z, 1, 0)) - z


def one_prompt(prompt, lens, rkv, low, coef, up, att, final):
    r, c, h, q, _ = place()
    length = lens[c * 8 + h * 4 + prompt]
    tokens = aligned(prompt, LMAX)
    wide = SLICE
    channels = aligned(q, SLICE)
    heads = wide // HEAD
    live = (lax.broadcasted_iota(jnp.int32, (LMAX, wide), 0) < length).astype(F32)
    lane = lax.broadcasted_iota(jnp.int32, (LMAX, wide), 1) // HEAD
    t = lax.broadcasted_iota(jnp.int32, (LMAX, LMAX), 0)
    u = lax.broadcasted_iota(jnp.int32, (LMAX, LMAX), 1)
    seg = (
        lax.broadcasted_iota(jnp.int32, (wide, wide), 0) // HEAD
        == lax.broadcasted_iota(jnp.int32, (wide, wide), 1) // HEAD
    ).astype(F32).astype(BF16)
    lower = (t >= u).astype(F32).astype(BF16)

    def head_sum(x):
        high, low_part = split(x)
        return dot(high, seg) + dot(low_part, seg)

    def only(x, k):
        return jnp.where(lane == k, x, jnp.zeros_like(x))

    receptance, key, value = rkv[0], rkv[1], rkv[2]
    decay = (
        -0.606531
        * jax.nn.sigmoid(coef[0:1, channels] + dot(jnp.tanh(low[0]).astype(BF16), up[0, :, channels]))
        * live
    )
    rate = jax.nn.sigmoid(coef[1:2, channels] + dot(low[1].astype(BF16), up[1, :, channels]))
    kappa = key * coef[2:3, channels]
    kappa = kappa * lax.rsqrt(head_sum(kappa * kappa) + 1e-05)
    remove = -kappa * live
    write = kappa * rate * live
    key = key * live
    value = value * live
    d_high, d_rest = split(decay)
    d_mid, d_low = split(decay - d_high.astype(F32))
    total = dot(lower, d_high) + (dot(lower, d_mid) + dot(lower, d_low))
    middle = total[LMAX // 2 - 1 : LMAX // 2, :]
    last = total[LMAX - 1 : LMAX, :]
    back = jnp.exp(middle - total)
    pull = split(remove * jnp.exp(total - decay - middle))
    read = split(receptance * jnp.exp(total - middle))
    write_back = split(write * back)
    key_back = split(key * back)
    value_parts = split(value)

    left = tuple(
        jnp.concatenate([x for k in range(heads) for x in (only(pull[i], k), only(read[i], k))])
        for i in range(2)
    )
    right = tuple(jnp.concatenate([write_back[i], key_back[i]]) for i in range(2))
    pairs = dot3(left, right, ((1,), (1,)))
    strict = t > u
    t2 = lax.broadcasted_iota(jnp.int32, (LMAX, 2 * LMAX), 0)
    u2 = lax.rem(lax.broadcasted_iota(jnp.int32, (LMAX, 2 * LMAX), 1), LMAX)
    upto = t2 >= u2
    solves, pull_key, reads = [], [], []
    for k in range(heads):
        base = k * 2 * LMAX
        system = jnp.where(strict, pairs[base : base + LMAX, :LMAX], 0.0)
        pull_key.append(split(jnp.where(strict, pairs[base : base + LMAX, LMAX:], 0.0)))
        reads.append(split(jnp.where(upto, pairs[base + LMAX : base + 2 * LMAX], 0.0)))
        solves.append(system)
    inverse = []
    for k in range(heads):
        near = (t // 2 == u // 2)
        inverse.append(
            jnp.where(near, solves[k], 0.0) + (t == u).astype(F32)
        )
    size = 2
    while size < LMAX:
        inside = (t // (2 * size) == u // (2 * size)) & (t // size != u // size)
        grown = []
        for k in range(heads):
            known = split(inverse[k])
            cross = split(jnp.where(inside, solves[k], 0.0))
            product = split(dot3(known, cross))
            grown.append(inverse[k] + dot3(product, known))
        inverse = grown
        size *= 2

    def across(mats, parts):
        wide_left = tuple(jnp.concatenate([mat[i] for mat in mats], axis=1) for i in range(2))
        tall = tuple(
            jnp.concatenate([only(part[i], k) for k in range(heads) for part in parts])
            for i in range(2)
        )
        return dot3(wide_left, tall)

    start = across(pull_key, [value_parts])
    pulled = split(across([split(x) for x in inverse], [split(start)]))
    output = across(reads, [pulled, value_parts])
    tail = jnp.exp(last - total)
    write_tail = split(write * tail)
    key_tail = split(key * tail)
    tall = tuple(jnp.concatenate([pulled[i], value_parts[i]]) for i in range(2))
    tails = tuple(jnp.concatenate([write_tail[i], key_tail[i]]) for i in range(2))
    state = dot3(tall, tails, ((0,), (0,)))
    even = lax.broadcasted_iota(jnp.int32, (HEAD, FEAT), 1) < HEAD
    for k in range(heads // 2):
        lanes = slice(k * FEAT, (k + 1) * FEAT)
        final[prompt, k] = jnp.where(
            even,
            state[k * FEAT : k * FEAT + HEAD, lanes],
            state[k * FEAT + HEAD : (k + 1) * FEAT, lanes],
        ).astype(BF16)
    bonus = head_sum(receptance * key * coef[3:4, channels])
    out = (output + bonus * value) * live
    center = head_sum(out) * (1.0 / HEAD)
    out = out - center
    spread = head_sum(out * out) * (1.0 / HEAD)
    out = (out * lax.rsqrt(spread + 0.00064) * coef[4:5, channels] + coef[5:6, channels]).astype(BF16)
    for side in range(2):
        att[side, tokens] = out[:, side * FEAT : (side + 1) * FEAT]


PROMPTS = MINE // LMAX
HOPS = 9


class PromptRing:
    def __init__(self, send_sem, recv_sem, base, axis, own, got):
        self.send_sem = send_sem
        self.recv_sem = recv_sem
        self.base = base
        self.here, self.chips, self.to = ring_at(axis)
        self.own = own
        self.got = got
        self.heavy = axis == "row"

    def hop(self, m, slot, chip, side, half=None):
        def block():
            at = self.chips.get(chip, self.here)
            if half is None:
                return self.got.at[pl.ds(2 * at, 2), aligned(m, LMAX)]
            return self.got.at[2 * at + half, aligned(m, LMAX)]

        def source():
            if chip == "own" and self.own is not None:
                return self.own.at[:, aligned(m, LMAX)]
            return block()

        return Copy(
            source,
            block,
            self.send_sem,
            self.recv_sem,
            self.base + m * HOPS + slot,
            self.to[side],
        )

    def hops(self, m):
        return [
            self.hop(m, 0, "own", "p"),
            self.hop(m, 1, "own", "m"),
            self.hop(m, 2, "own", "z"),
            self.hop(m, 3, "m", "p", 0),
            self.hop(m, 4, "p", "m", 1),
            self.hop(m, 5, "z", "p"),
            self.hop(m, 6, "z", "m"),
            self.hop(m, 7, "o", "z", 0) if self.heavy else self.hop(m, 7, "mz", "p", 0),
            self.hop(m, 8, "o", "z", 1) if self.heavy else self.hop(m, 8, "pz", "m", 1),
        ]

    def begin(self, m):
        copies = self.hops(m)
        for k in (2, 0, 1):
            copies[k].start()

    def forward(self, m):
        copies = self.hops(m)
        copies[0].wait_recv()
        copies[3].start()
        copies[1].wait_recv()
        copies[4].start()
        copies[2].wait_recv()
        copies[5].start()
        copies[6].start()

    def close(self, m):
        copies = self.hops(m)
        for early, late in ((3, 7), (4, 8)) if self.heavy else ((6, 8), (5, 7)):
            copies[early].wait_recv()
            copies[late].start()

    def last(self, m):
        for k in (5, 6, 7, 8) if self.heavy else (3, 4, 7, 8):
            self.hops(m)[k].wait_recv()

    def sent(self, m):
        for copy in self.hops(m):
            copy.wait_send()


N_SUM = PROMPTS * 9
N_TURN = N_SUM + 2 * PROMPTS
N_STATE = N_TURN + 1
N_WEIGHT = N_STATE + 3 * PROMPTS * HOPS
N_ALL = N_WEIGHT + 1 + 2 * (1 + 14 + RING) + 1 + 14 + RING


def body_kernel(
    lens,
    hx,
    par,
    shift,
    wt,
    down,
    coef,
    up,
    w3,
    wk,
    wv,
    wn,
    out,
    next_rkv,
    final,
    send_sem,
    recv_sem,
    local_sem,
    rkv,
    low,
    state,
    att,
    attg,
    w3x,
    mid,
    midg,
    held,
    theirs,
    act_scr,
    part,
    got,
    summed,
    fin,
    nx,
    wng,
):
    r, c, h, q, sibling = place()
    x_here = lax.div(r, 4)
    x_plus, x_over, x_minus = (lax.rem(x_here + d, 4) for d in range(1, 4))
    z_row = 4 * x_here + 2 * (1 - lax.rem(q, 2))

    def local():
        return [
            pltpu.make_async_copy(wk.at[c], held.at[0, :, c], local_sem.at[0]),
            pltpu.make_async_copy(wv.at[c], held.at[1, :, c], local_sem.at[1]),
            pltpu.make_async_copy(wn.at[r], wng.at[r], local_sem.at[2]),
        ]

    for copy in local():
        copy.start()

    def target(i):
        return (2 * c + lax.rem(h + i, 2), q)

    barrier = pltpu.get_barrier_semaphore()
    peers = [(lax.rem(r + 4, N_ROW), c), (lax.rem(r + 12, N_ROW), c)] + ring_peers("col")
    peers += [(sibling, c), (z_row, c), (z_row + 1, c)]

    @pl.when(q != c)
    def _():
        for i in range(2):
            pl.semaphore_signal(barrier, inc=1, device_id=target(i), device_id_type=MESH)

    for device in peers:
        pl.semaphore_signal(barrier, inc=1, device_id=device, device_id_type=MESH)
    pl.semaphore_wait(barrier, len(peers) + 2 * (q != c).astype(jnp.int32))

    links = Links(send_sem, recv_sem, N_WEIGHT)
    links.go(w3, w3x, (sibling, c))

    col_place = ring_at("col")

    def mlp_ring(which, source):
        def slot(chip, half):
            return held.at[which, pl.ds(8 * half, 8), chip]

        def over(chip, half):
            return theirs.at[which, pl.ds(8 * half, 8), chip]

        def seen(chip, half):
            links.go(lambda: slot(chip, half), lambda: over(chip, half), (sibling, c))

        def begin():
            links.go(lambda: source.at[c], lambda: theirs.at[which, :, c], (sibling, c))
            yield from ring(
                links,
                "col",
                slot,
                own=lambda k: source.at[c, pl.ds(8 * k, 8)],
                seen=seen,
                at=col_place,
            )

        return begin()

    def weight_slot(chip, half):
        return wng.at[2 * chip + h, pl.ds(4 * half, 4)]

    far_links = Links(send_sem, recv_sem, N_ALL - 1 - 14 - RING)

    def weight_seen(chip, half):
        far_links.go(
            lambda: weight_slot(chip, half), lambda: weight_slot(chip, half), (sibling, c)
        )

    def weight_ring():
        far_links.go(lambda: wn.at[r], lambda: wng.at[r], (sibling, c))
        yield from ring(
            far_links,
            "row",
            weight_slot,
            own=lambda k: wn.at[r, pl.ds(4 * k, 4)],
            seen=weight_seen,
            heavy=False,
        )

    keys = mlp_ring(0, wk)
    values = mlp_ring(1, wv)
    weights = weight_ring()
    for steps in (weights, keys, values):
        next(steps)

    att_ring = PromptRing(send_sem, recv_sem, N_STATE, "row", att, attg)
    mid_ring = PromptRing(send_sem, recv_sem, N_STATE + PROMPTS * HOPS, "row", mid, midg)
    out_ring = PromptRing(send_sem, recv_sem, N_STATE + 2 * PROMPTS * HOPS, "col", None, nx)
    move_state = Copy(state, final, send_sem, recv_sem, N_TURN, target(0))

    def wide(ref, m):
        return jnp.concatenate([ref[j, aligned(m, LMAX), :] for j in range(N_ROW)], axis=1)

    def normed(ref, m, k):
        return norm(wide(ref, m).astype(F32), row_of(par, k), row_of(par, k + 1))

    def blends(m):
        z = normed(hx, m, 0)
        dz = step_back(z)
        for j in range(5):
            blend = (z + dz * shift[j : j + 1, :]).astype(BF16)
            if j < 3:
                weight = jnp.concatenate(
                    [wt[side, j].reshape(WIDTH, FEAT) for side in range(2)], axis=1
                )
                rkv[j] = dot(blend, weight)
            else:
                low[j - 3] = dot(blend, down[j - 3], ((1,), (1,)))

    def core(m):
        blends(m)
        one_prompt(m, lens, rkv, low, coef, up, att, state)
        att_ring.begin(m)
        for side in range(2):
            attg[2 * q + side, aligned(m, LMAX)] = att[side, aligned(m, LMAX)]

    def project(m):
        att_ring.last(m)
        tokens = aligned(m, LMAX)
        weight = jnp.concatenate([w[...].reshape(FEAT, WIDTH) for w in (w3, w3x)])
        total = dot(wide(attg, m), weight, ((1,), (1,)))
        for k, side in enumerate((h, 1 - h)):
            block = (
                hx[r - h + side, tokens, :].astype(F32) + total[:, k * FEAT : (k + 1) * FEAT]
            ).astype(BF16)
            mid[side, tokens, :] = block
            midg[r - h + side, tokens, :] = block
        mid_ring.begin(m)

    def x_move(m, k):
        tokens = aligned(m, LMAX)
        source, first, target_at, step = (
            (part, 4 * x_over, 0, 4),
            (part, 4 * x_over + 2, 2, 12),
            (part, 4 * x_plus + 2, 6, 4),
            (part, 4 * x_minus, 8, 12),
            (got, 12, 4, 4),
            (got, 14, 10, 12),
        )[k]
        return pltpu.make_async_remote_copy(
            src_ref=source.at[pl.ds(first, 2), tokens],
            dst_ref=got.at[pl.ds(target_at, 2), tokens],
            send_sem=send_sem.at[9 * m + k],
            recv_sem=recv_sem.at[9 * m + k],
            device_id=(lax.rem(r + step, N_ROW), c),
            device_id_type=MESH,
        )

    def plane_move(m, k):
        there = sibling if k == 0 else z_row + k - 1
        own_k = 0 if k == 0 else 1 + h
        return pltpu.make_async_remote_copy(
            src_ref=summed.at[there - 4 * x_here, aligned(m, LMAX)],
            dst_ref=fin.at[(0 if k == 0 else 2) + h, aligned(m, LMAX)],
            send_sem=send_sem.at[9 * m + 6 + k],
            recv_sem=recv_sem.at[9 * m + 6 + own_k],
            device_id=(there, c),
            device_id_type=MESH,
        )

    def channel(m):
        mid_ring.last(m)
        tokens = aligned(m, LMAX)
        z = normed(midg, m, 2)
        blend = (z + step_back(z) * shift[5:6, :]).astype(BF16)
        for side, weight in enumerate((held, theirs)):
            act = jnp.square(jnp.maximum(dot(blend, weight[0].reshape(WIDTH, MINE)), 0.0))
            act_scr[side] = act.astype(BF16)

        @pl.loop(0, N_CHIP)
        def _(n):
            total = None
            for side, weight in enumerate((held, theirs)):
                rows_n = weight[1, pl.ds(2 * n, 2)].reshape(SLICE, MINE)
                term = dot(act_scr[side], rows_n, ((1,), (1,)))
                total = term if total is None else total + term
            for side in range(2):
                added = jnp.where(n == q, mid[side, tokens, :].astype(F32), 0.0)
                part[2 * n + side, tokens, :] = (
                    total[:, side * FEAT : (side + 1) * FEAT] + added
                ).astype(BF16)

        for k in range(4):
            x_move(m, k).start()

    def relay(m):
        tokens = aligned(m, LMAX)
        for k, other in enumerate((x_plus, x_minus)):
            x_move(m, k).wait_recv()
            for j in range(2):
                added = part[4 * other + 2 * k + j, tokens, :].astype(F32)
                got[12 + 2 * k + j, tokens, :] = (
                    got[2 * k + j, tokens, :].astype(F32) + added
                ).astype(BF16)
            x_move(m, 4 + k).start()

    def plane_sum(m):
        tokens = aligned(m, LMAX)
        for k in range(2, 6):
            x_move(m, k).wait_recv()
        for k, places in enumerate(((4, 8), (5, 9), (10, 6), (11, 7))):
            total = part[4 * x_here + k, tokens, :].astype(F32)
            for j in places:
                total += got[j, tokens, :].astype(F32)
            summed[k, tokens, :] = total.astype(BF16)
        for k in (1, 2, 0):
            plane_move(m, k).start()
        fin[h, tokens, :] = summed[r - 4 * x_here, tokens, :]

    def source_rows(m, i):
        return pl.ds(pl.multiple_of(lax.rem(h + i, 2) * MINE + m * LMAX, LMAX), LMAX)

    def turn(m, i):
        return pltpu.make_async_remote_copy(
            src_ref=out.at[source_rows(m, i)],
            dst_ref=nx.at[2 * q + h, aligned(m, LMAX)],
            send_sem=send_sem.at[N_SUM + 2 * m + i],
            recv_sem=recv_sem.at[N_SUM + 2 * m + h],
            device_id=target(i),
            device_id_type=MESH,
        )

    def add_up(m):
        tokens = aligned(m, LMAX)
        for k in range(3):
            block = fin.at[0, tokens]
            pltpu.make_async_copy(block, block, recv_sem.at[9 * m + 6 + k]).wait()
        for side in range(2):
            total = fin[side, tokens, :].astype(F32) + fin[2 + side, tokens, :].astype(F32)
            rows_m = pl.ds(pl.multiple_of(side * MINE + m * LMAX, LMAX), LMAX)
            out[rows_m, :] = total.astype(BF16)

        @pl.when(q == c)
        def _():
            keep(
                out.at[source_rows(m, 0)],
                nx.at[r, aligned(m, LMAX)],
                recv_sem.at[N_SUM + 2 * m + h],
            )

        @pl.when(q != c)
        def _():
            turn(m, 0).start()

        turn(m, 1).start()

    def spread(m):
        for k in range(2):
            block = nx.at[2 * c + k, aligned(m, LMAX)]
            pltpu.make_async_copy(block, block, recv_sem.at[N_SUM + 2 * m + k]).wait()
        out_ring.begin(m)

    def project_next(m):
        out_ring.last(m)
        z = normed(nx, m, 4)
        dz = step_back(z)
        for j in range(3):
            blend = (z + dz * shift[6 + j : 7 + j, :]).astype(BF16)
            next_rkv[j, aligned(m, LMAX), :] = dot(
                blend, wng[:, :, j].reshape(WIDTH, SLICE)
            ).astype(BF16)

    stages = (
        core,
        att_ring.forward,
        att_ring.close,
        project,
        mid_ring.forward,
        mid_ring.close,
        channel,
        relay,
        plane_sum,
        add_up,
        spread,
        out_ring.forward,
        out_ring.close,
        project_next,
    )
    end = object()

    def wait_mlp():
        for copy in local():
            copy.wait()
        for copy in links.open:
            copy.wait_recv()
        links.open = []

    def send_state():
        @pl.when(q == c)
        def _():
            keep(state, final, recv_sem.at[N_TURN])

        @pl.when(q != c)
        def _():
            move_state.start()

    def wait_far():
        for copy in far_links.open:
            copy.wait_recv()
        far_links.open = []

    beside = {
        0: [keys, values],
        1: [keys, values, weights, weights],
        2: [lambda: links.arrive(links.copies[0])],
        3: [keys, values, send_state],
        4: [weights],
        5: [keys, values, wait_mlp],
        6: [weights],
        12: [wait_far],
    }

    @pl.loop(0, PROMPTS + len(stages) - 1)
    def _(t):
        for lag, stage in enumerate(stages):

            @pl.when((t >= lag) & (t < PROMPTS + lag))
            def _():
                stage(t - lag)

        for at, works in beside.items():

            @pl.when(t == at)
            def _():
                for work in works:
                    if callable(work):
                        work()
                    else:
                        next(work, end)

    @pl.loop(0, PROMPTS)
    def _(m):
        for k in range(6):
            x_move(m, k).wait_send()
        for k in range(3):
            plane_move(m, k).wait_send()
        for prompt_ring in (att_ring, mid_ring, out_ring):
            prompt_ring.sent(m)

        @pl.when(q != c)
        def _():
            turn(m, 0).wait_send()

        turn(m, 1).wait_send()

    pltpu.make_async_copy(state, final, recv_sem.at[N_TURN]).wait()

    @pl.when(q != c)
    def _():
        move_state.wait_send()

    for copy in links.copies + far_links.copies:
        copy.wait_send()


def per_device(
    hidden,
    lengths,
    square_matrix_shards,
    channel_mix_shards,
    lowrank_down,
    lowrank_up,
    token_shift_weights,
    attention_coefficients,
    norm_parameters,
):
    hx, wt, w3, wk, wv, wn, parg = exchange(
        start_kernel,
        [
            ((N_ROW, MINE, FEAT), BF16),
            ((2, 3, N_ROW, N_COL, 16, FEAT), BF16),
            ((N_COL, 16, WIDTH), BF16),
            ((N_COL, N_ROW, 16, MINE), BF16),
            ((N_COL, N_ROW, 16, MINE), BF16),
            ((N_ROW, N_COL, 3, 16, SLICE), BF16),
            ((N_ROW, 6, FEAT), F32),
        ],
        15 + 1 + 3 * RING + 1 + 14 + 15 + 15 + 7 + 15,
        9,
        1,
        square_matrix_shards,
        channel_mix_shards,
        norm_parameters,
        hidden,
        scratch=[
            pltpu.VMEM(square_matrix_shards.shape, F32),
            pltpu.VMEM(channel_mix_shards.shape, F32),
            pltpu.VMEM(square_matrix_shards.shape, BF16),
            pltpu.VMEM(channel_mix_shards.shape, BF16),
        ],
    )
    lowrank = lowrank_down.shape[2]
    out_hidden, next_rkv, final = exchange(
        body_kernel,
        [
            ((2 * MINE, FEAT), BF16),
            ((3, MINE, SLICE), BF16),
            ((PROMPTS, 2, HEAD, FEAT), BF16),
        ],
        N_ALL,
        3,
        2,
        lengths,
        hx,
        parg,
        token_shift_weights,
        wt,
        lowrank_down.transpose(0, 2, 1),
        attention_coefficients,
        lowrank_up,
        w3,
        wk,
        wv,
        wn,
        scratch=[
            pltpu.VMEM((3, LMAX, SLICE), F32),
            pltpu.VMEM((2, LMAX, lowrank), F32),
            pltpu.VMEM((PROMPTS, 2, HEAD, FEAT), BF16),
            pltpu.VMEM((2, MINE, FEAT), BF16),
            pltpu.VMEM((N_ROW, MINE, FEAT), BF16),
            pltpu.VMEM((N_COL, 16, WIDTH), BF16),
            pltpu.VMEM((2, MINE, FEAT), BF16),
            pltpu.VMEM((N_ROW, MINE, FEAT), BF16),
            pltpu.VMEM((2, N_ROW, N_COL, 16, MINE), BF16),
            pltpu.VMEM((2, N_ROW, N_COL, 16, MINE), BF16),
            pltpu.VMEM((2, LMAX, MINE), BF16),
            pltpu.VMEM((N_ROW, MINE, FEAT), BF16),
            pltpu.VMEM((N_ROW, MINE, FEAT), BF16),
            pltpu.VMEM((4, MINE, FEAT), BF16),
            pltpu.VMEM((4, MINE, FEAT), BF16),
            pltpu.VMEM((N_ROW, MINE, FEAT), BF16),
            pltpu.VMEM((N_ROW, N_COL, 3, 16, SLICE), BF16),
        ],
        in_specs=[pl.BlockSpec(memory_space=pltpu.SMEM)] + [VMEM] * 8 + [ANY] * 3,
        out_specs=[VMEM, VMEM, ANY],
    )
    final = final.reshape(4, 2, HEAD, 2, HEAD).transpose(0, 1, 3, 2, 4).astype(F32)
    final_state = final.reshape(4, 4, HEAD * HEAD)
    return (out_hidden, next_rkv, final_state)


def solution(mesh):
    return jax.shard_map(
        per_device,
        mesh=mesh,
        in_specs=(
            P("col", "row"),
            P(),
            P(None, ("row", "col"), None),
            P(None, ("row", "col"), None),
            P(),
            P(),
            P(),
            P(),
            P(None, "row"),
        ),
        out_specs=(P("col", "row"), P(None, "row", "col"), P("row", "col", None)),
        check_vma=False,
    )
```

```python
import functools

import jax
import jax.numpy as jnp
from jax import lax
from jax.experimental import pallas as pl
from jax.experimental.pallas import tpu as pltpu
from jax.sharding import PartitionSpec as P

WIDTH = 2048
HEAD = 64
LMAX = 128
F32 = jnp.float32
BF16 = jnp.bfloat16
MESH = pl.DeviceIdType.MESH
ANY = pl.BlockSpec(memory_space=pl.ANY)
VMEM = pl.BlockSpec(memory_space=pltpu.VMEM)
N_ROW = 16
N_COL = 8
N_CHIP = 8
MINE = 512
FEAT = 128
SLICE = 256


def greet(devices):
    barrier = pltpu.get_barrier_semaphore()
    for device in devices:
        pl.semaphore_signal(barrier, inc=1, device_id=device, device_id_type=MESH)
    pl.semaphore_wait(barrier, len(devices))


class Copy:
    def __init__(self, source, target, send_sem, recv_sem, slot, device):
        self.made = lambda: pltpu.make_async_remote_copy(
            src_ref=source() if callable(source) else source,
            dst_ref=target() if callable(target) else target,
            send_sem=send_sem.at[slot],
            recv_sem=recv_sem.at[slot],
            device_id=device,
            device_id_type=MESH,
        )

    def start(self):
        self.made().start()

    def wait_recv(self):
        self.made().wait_recv()

    def wait_send(self):
        self.made().wait_send()


def keep(source, target, sem):
    copy = pltpu.make_async_copy(source, target, sem)
    copy.start()
    return copy


def exchange(
    kernel,
    outs,
    n_remote,
    n_local,
    collective_id,
    *operands,
    scratch=(),
    in_specs=None,
    out_specs=None,
):
    return pl.pallas_call(
        kernel,
        out_shape=[jax.ShapeDtypeStruct(*out) for out in outs],
        in_specs=in_specs or [ANY] * len(operands),
        out_specs=out_specs or [ANY] * len(outs),
        scratch_shapes=[
            pltpu.SemaphoreType.DMA((n_remote,)),
            pltpu.SemaphoreType.DMA((n_remote,)),
            pltpu.SemaphoreType.DMA((n_local,)),
            *scratch,
        ],
        compiler_params=pltpu.CompilerParams(
            collective_id=collective_id, has_side_effects=True, vmem_limit_bytes=56 * 2**20
        ),
        cost_estimate=pl.CostEstimate(flops=0, bytes_accessed=48 * 2**20, transcendentals=0),
    )(*operands)


def place():
    r = lax.axis_index("row")
    c = lax.axis_index("col")
    h = lax.rem(r, 2)
    return r, c, h, lax.div(r, 2), r + 1 - 2 * h


class Links:
    def __init__(self, send_sem, recv_sem, first=0):
        self.send_sem = send_sem
        self.recv_sem = recv_sem
        self.slot = first
        self.copies = []
        self.open = []

    def go(self, source, target, device):
        copy = Copy(source, target, self.send_sem, self.recv_sem, self.slot, device)
        copy.start()
        self.slot += 1
        self.copies.append(copy)
        self.open.append(copy)
        return copy

    def arrive(self, copy):
        copy.wait_recv()
        self.open = [other for other in self.open if other is not copy]

    def finish(self):
        for copy in self.open:
            copy.wait_recv()
        for copy in self.copies:
            copy.wait_send()


RING = 14


def ring_at(axis):
    r, c, h, q, _ = place()
    here = q if axis == "row" else c
    step_z = 1 - 2 * lax.rem(here, 2)
    chips = {
        "p": lax.rem(here + 2, 8),
        "m": lax.rem(here + 6, 8),
        "z": here + step_z,
        "o": lax.rem(here + 4, 8),
        "pz": lax.rem(here + 2, 8) + step_z,
        "mz": lax.rem(here + 6, 8) + step_z,
        "oz": lax.rem(here + 4, 8) + step_z,
    }
    devices = {
        side: (2 * chips[side] + h, c) if axis == "row" else (r, chips[side]) for side in "pmz"
    }
    return here, chips, devices


def ring_peers(axis):
    return list(ring_at(axis)[2].values())


def ring(links, axis, slot, own=None, which=(0, 1), ready=None, seen=None, heavy=None, at=None):
    here, chips, to = at or ring_at(axis)
    heavy = axis == "row" if heavy is None else heavy
    seen = seen or (lambda chip, half: None)

    def take(copy, chip, half):
        links.arrive(copy)
        seen(chip, half)

    def forward(chip, half, side):
        return links.go(lambda: slot(chip, half), lambda: slot(chip, half), to[side])

    first = {}
    for k in range(2):
        if ready is not None:
            ready(k)
        target = functools.partial(slot, here, which[k])
        source = functools.partial(own, k) if own is not None else target
        for side in "zpm":
            first[side, k] = links.go(source, target, to[side])
    yield
    for k in range(2):
        take(first["p", k], chips["m"], which[k])
    low = forward(chips["m"], 0, "p")
    for k in range(2):
        take(first["m", k], chips["p"], which[k])
    high = forward(chips["p"], 1, "m")
    yield
    beside = {}
    for k in range(2):
        take(first["z", k], chips["z"], which[k])
        for side in "pm":
            beside[side, k] = forward(chips["z"], which[k], side)
    yield
    if heavy:
        take(low, chips["o"], 0)
        low = forward(chips["o"], 0, "z")
        take(high, chips["o"], 1)
        high = forward(chips["o"], 1, "z")
        yield
        for k in range(2):
            take(beside["p", k], chips["mz"], which[k])
            take(beside["m", k], chips["pz"], which[k])
    else:
        take(low, chips["o"], 0)
        take(high, chips["o"], 1)
        for k in range(2):
            take(beside["p", k], chips["mz"], which[k])
        low = forward(chips["mz"], 0, "p")
        for k in range(2):
            take(beside["m", k], chips["pz"], which[k])
        high = forward(chips["pz"], 1, "m")
        yield
    take(low, chips["oz"], 0)
    take(high, chips["oz"], 1)


def together(*steps):
    active = list(steps)
    while active:
        for step in list(active):
            if next(step, StopIteration) is StopIteration:
                active.remove(step)


def aligned(index, size):
    return pl.ds(pl.multiple_of(index * size, size), size)


def start_kernel(
    square_in,
    mlp_in,
    par,
    hid,
    hx,
    wt,
    w3,
    wk,
    wv,
    wn,
    parg,
    send_sem,
    recv_sem,
    local_sem,
    square_wide,
    mlp_wide,
    square,
    mlp,
):
    r, c, h, q, sibling = place()
    rows = [lax.rem(r + d, N_ROW) for d in range(1, N_ROW)]
    cols = [lax.rem(c + d, N_COL) for d in range(1, N_COL)]

    def time_part(p):
        return square.at[pl.ds(0, 3), :, aligned(p, FEAT)]

    def key_part(p):
        return mlp.at[0, :, aligned(p, MINE)]

    def value_part(p):
        return mlp.at[1, :, aligned(p, MINE)]

    def next_part(p):
        return square.at[pl.ds(4, 3), :, aligned(p, SLICE)]

    mine = hid.at[aligned(h, MINE)]
    square_load = keep(square_in, square_wide, local_sem.at[7])
    mlp_load = keep(mlp_in, mlp_wide, local_sem.at[8])
    local = [
        keep(par, parg.at[r], local_sem.at[1]),
        keep(mine, hx.at[r], local_sem.at[2]),
    ]
    greet([(p, c) for p in rows] + [(r, p) for p in cols])
    links = Links(send_sem, recv_sem)
    times = []
    own_time = []
    other = links.go(hid.at[aligned(1 - h, MINE)], hx.at[r], (sibling, c))

    def hid_own(k):
        return (mine, hx.at[sibling])[k]

    def hid_ready(k):
        if k == 1:
            links.arrive(other)

    def time_ready(k):
        if k == 0:
            for copy in times:
                links.arrive(copy)
            links.go(wt.at[h, :, :, c], wt.at[h, :, :, c], (sibling, c))

    def time_slot(chip, half):
        return wt.at[h, :, pl.ds(8 * half, 8), chip]

    def time_seen(chip, half):
        links.go(time_slot(chip, half), time_slot(chip, half), (sibling, c))

    def out_slot(chip, half):
        return w3.at[chip, :, pl.ds(1024 * half, 1024)]

    def out_own(k):
        return square.at[3, :, pl.ds(1024 * k, 1024)]

    def feed():
        square_load.wait()
        for j in range(3):
            square[j] = square_wide[j].astype(BF16)
        for p in rows:
            times.append(links.go(time_part(p), wt.at[lax.rem(p, 2), :, r, c], (p, c)))
        own_time.append(keep(time_part(r), wt.at[h, :, r, c], local_sem.at[0]))
        yield

    def casts():
        for j in range(3, 7):
            square[j] = square_wide[j].astype(BF16)
        mlp_load.wait()
        mlp[...] = mlp_wide[...].astype(BF16)
        own_time[0].wait()
        yield

    def rest():
        local.extend(
            [
                keep(square.at[3], w3.at[c], local_sem.at[3]),
                keep(key_part(r), wk.at[c, r], local_sem.at[4]),
                keep(value_part(r), wv.at[c, r], local_sem.at[5]),
                keep(next_part(c), wn.at[r, c], local_sem.at[6]),
            ]
        )
        for p in rows:
            links.go(par, parg.at[r], (p, c))
        yield
        for p in rows:
            links.go(key_part(p), wk.at[c, r], (p, c))
        for p in cols:
            links.go(next_part(p), wn.at[r, c], (r, p))
        for p in rows:
            links.go(value_part(p), wv.at[c, r], (p, c))

    together(
        feed(),
        ring(
            links,
            "row",
            lambda chip, side: hx.at[2 * chip + side],
            own=hid_own,
            which=(h, 1 - h),
            ready=hid_ready,
        ),
        casts(),
        ring(links, "col", time_slot, ready=time_ready, seen=time_seen),
        rest(),
        ring(links, "col", out_slot, own=out_own),
    )
    links.finish()
    for copy in local:
        copy.wait()


def dot(a, b, dims=((1,), (0,))):
    return lax.dot_general(a, b, (dims, ((), ())), preferred_element_type=F32)


def split(x):
    high = x.astype(BF16)
    return high, (x - high.astype(F32)).astype(BF16)


def dot3(a, b, dims=((1,), (0,))):
    a_high, a_low = a
    b_high, b_low = b
    return dot(a_high, b_high, dims) + (dot(a_high, b_low, dims) + dot(a_low, b_high, dims))


def norm(source, gain, bias):
    center = jnp.sum(source, axis=-1, keepdims=True) / WIDTH
    second = jnp.sum(source * source, axis=-1, keepdims=True) / WIDTH
    scaled = (source - center) * lax.rsqrt(second - center * center + 1e-05)
    return (scaled * gain + bias).astype(BF16).astype(F32)


def row_of(par, i):
    return jnp.concatenate([par[j, i : i + 1, :] for j in range(N_ROW)], axis=1)


def step_back(z):
    position = lax.rem(lax.broadcasted_iota(jnp.int32, z.shape, 0), LMAX)
    return jnp.where(position == 0, 0.0, pltpu.roll(z, 1, 0)) - z


def one_prompt(prompt, lens, rkv, low, coef, up, att, final):
    r, c, h, q, _ = place()
    length = lens[c * 8 + h * 4 + prompt]
    tokens = aligned(prompt, LMAX)
    wide = SLICE
    channels = aligned(q, SLICE)
    heads = wide // HEAD
    live = (lax.broadcasted_iota(jnp.int32, (LMAX, wide), 0) < length).astype(F32)
    lane = lax.broadcasted_iota(jnp.int32, (LMAX, wide), 1) // HEAD
    t = lax.broadcasted_iota(jnp.int32, (LMAX, LMAX), 0)
    u = lax.broadcasted_iota(jnp.int32, (LMAX, LMAX), 1)
    seg = (
        lax.broadcasted_iota(jnp.int32, (wide, wide), 0) // HEAD
        == lax.broadcasted_iota(jnp.int32, (wide, wide), 1) // HEAD
    ).astype(F32).astype(BF16)
    lower = (t >= u).astype(F32).astype(BF16)

    def head_sum(x):
        high, low_part = split(x)
        return dot(high, seg) + dot(low_part, seg)

    def only(x, k):
        return jnp.where(lane == k, x, jnp.zeros_like(x))

    receptance, key, value = rkv[0], rkv[1], rkv[2]
    decay = (
        -0.606531
        * jax.nn.sigmoid(coef[0:1, channels] + dot(jnp.tanh(low[0]).astype(BF16), up[0, :, channels]))
        * live
    )
    rate = jax.nn.sigmoid(coef[1:2, channels] + dot(low[1].astype(BF16), up[1, :, channels]))
    kappa = key * coef[2:3, channels]
    kappa = kappa * lax.rsqrt(head_sum(kappa * kappa) + 1e-05)
    remove = -kappa * live
    write = kappa * rate * live
    key = key * live
    value = value * live
    d_high, d_rest = split(decay)
    d_mid, d_low = split(decay - d_high.astype(F32))
    total = dot(lower, d_high) + (dot(lower, d_mid) + dot(lower, d_low))
    middle = total[LMAX // 2 - 1 : LMAX // 2, :]
    last = total[LMAX - 1 : LMAX, :]
    back = jnp.exp(middle - total)
    pull = split(remove * jnp.exp(total - decay - middle))
    read = split(receptance * jnp.exp(total - middle))
    write_back = split(write * back)
    key_back = split(key * back)
    value_parts = split(value)

    left = tuple(
        jnp.concatenate([x for k in range(heads) for x in (only(pull[i], k), only(read[i], k))])
        for i in range(2)
    )
    right = tuple(jnp.concatenate([write_back[i], key_back[i]]) for i in range(2))
    pairs = dot3(left, right, ((1,), (1,)))
    strict = t > u
    t2 = lax.broadcasted_iota(jnp.int32, (LMAX, 2 * LMAX), 0)
    u2 = lax.rem(lax.broadcasted_iota(jnp.int32, (LMAX, 2 * LMAX), 1), LMAX)
    upto = t2 >= u2
    solves, pull_key, reads = [], [], []
    for k in range(heads):
        base = k * 2 * LMAX
        system = jnp.where(strict, pairs[base : base + LMAX, :LMAX], 0.0)
        pull_key.append(split(jnp.where(strict, pairs[base : base + LMAX, LMAX:], 0.0)))
        reads.append(split(jnp.where(upto, pairs[base + LMAX : base + 2 * LMAX], 0.0)))
        solves.append(system)
    inverse = []
    for k in range(heads):
        near = (t // 2 == u // 2)
        inverse.append(
            jnp.where(near, solves[k], 0.0) + (t == u).astype(F32)
        )
    size = 2
    while size < LMAX:
        inside = (t // (2 * size) == u // (2 * size)) & (t // size != u // size)
        grown = []
        for k in range(heads):
            known = split(inverse[k])
            cross = split(jnp.where(inside, solves[k], 0.0))
            product = split(dot3(known, cross))
            grown.append(inverse[k] + dot3(product, known))
        inverse = grown
        size *= 2

    def across(mats, parts):
        wide_left = tuple(jnp.concatenate([mat[i] for mat in mats], axis=1) for i in range(2))
        tall = tuple(
            jnp.concatenate([only(part[i], k) for k in range(heads) for part in parts])
            for i in range(2)
        )
        return dot3(wide_left, tall)

    start = across(pull_key, [value_parts])
    pulled = split(across([split(x) for x in inverse], [split(start)]))
    output = across(reads, [pulled, value_parts])
    tail = jnp.exp(last - total)
    write_tail = split(write * tail)
    key_tail = split(key * tail)
    tall = tuple(jnp.concatenate([pulled[i], value_parts[i]]) for i in range(2))
    tails = tuple(jnp.concatenate([write_tail[i], key_tail[i]]) for i in range(2))
    state = dot3(tall, tails, ((0,), (0,)))
    even = lax.broadcasted_iota(jnp.int32, (HEAD, FEAT), 1) < HEAD
    for k in range(heads // 2):
        lanes = slice(k * FEAT, (k + 1) * FEAT)
        final[prompt, k] = jnp.where(
            even,
            state[k * FEAT : k * FEAT + HEAD, lanes],
            state[k * FEAT + HEAD : (k + 1) * FEAT, lanes],
        ).astype(BF16)
    bonus = head_sum(receptance * key * coef[3:4, channels])
    out = (output + bonus * value) * live
    center = head_sum(out) * (1.0 / HEAD)
    out = out - center
    spread = head_sum(out * out) * (1.0 / HEAD)
    out = (out * lax.rsqrt(spread + 0.00064) * coef[4:5, channels] + coef[5:6, channels]).astype(BF16)
    for side in range(2):
        att[side, tokens] = out[:, side * FEAT : (side + 1) * FEAT]


PROMPTS = MINE // LMAX
HOPS = 9


class PromptRing:
    def __init__(self, send_sem, recv_sem, base, axis, own, got):
        self.send_sem = send_sem
        self.recv_sem = recv_sem
        self.base = base
        self.here, self.chips, self.to = ring_at(axis)
        self.own = own
        self.got = got
        self.heavy = axis == "row"

    def hop(self, m, slot, chip, side, half=None):
        def block():
            at = self.chips.get(chip, self.here)
            if half is None:
                return self.got.at[pl.ds(2 * at, 2), aligned(m, LMAX)]
            return self.got.at[2 * at + half, aligned(m, LMAX)]

        def source():
            if chip == "own" and self.own is not None:
                return self.own.at[:, aligned(m, LMAX)]
            return block()

        return Copy(
            source,
            block,
            self.send_sem,
            self.recv_sem,
            self.base + m * HOPS + slot,
            self.to[side],
        )

    def hops(self, m):
        return [
            self.hop(m, 0, "own", "p"),
            self.hop(m, 1, "own", "m"),
            self.hop(m, 2, "own", "z"),
            self.hop(m, 3, "m", "p", 0),
            self.hop(m, 4, "p", "m", 1),
            self.hop(m, 5, "z", "p"),
            self.hop(m, 6, "z", "m"),
            self.hop(m, 7, "o", "z", 0) if self.heavy else self.hop(m, 7, "mz", "p", 0),
            self.hop(m, 8, "o", "z", 1) if self.heavy else self.hop(m, 8, "pz", "m", 1),
        ]

    def begin(self, m):
        copies = self.hops(m)
        for k in (2, 0, 1):
            copies[k].start()

    def forward(self, m):
        copies = self.hops(m)
        copies[0].wait_recv()
        copies[3].start()
        copies[1].wait_recv()
        copies[4].start()
        copies[2].wait_recv()
        copies[5].start()
        copies[6].start()

    def close(self, m):
        copies = self.hops(m)
        for early, late in ((3, 7), (4, 8)) if self.heavy else ((6, 8), (5, 7)):
            copies[early].wait_recv()
            copies[late].start()

    def last(self, m):
        for k in (5, 6, 7, 8) if self.heavy else (3, 4, 7, 8):
            self.hops(m)[k].wait_recv()

    def sent(self, m):
        for copy in self.hops(m):
            copy.wait_send()


N_SUM = PROMPTS * 9
N_TURN = N_SUM + 2 * PROMPTS
N_STATE = N_TURN + 1
N_WEIGHT = N_STATE + 3 * PROMPTS * HOPS
N_ALL = N_WEIGHT + 1 + 2 * (1 + 14 + RING) + 1 + 14 + RING


def body_kernel(
    lens,
    hx,
    par,
    shift,
    wt,
    down,
    coef,
    up,
    w3,
    wk,
    wv,
    wn,
    out,
    next_rkv,
    final,
    send_sem,
    recv_sem,
    local_sem,
    rkv,
    low,
    state,
    att,
    attg,
    w3x,
    mid,
    midg,
    held,
    theirs,
    act_scr,
    part,
    got,
    summed,
    fin,
    nx,
    wng,
):
    r, c, h, q, sibling = place()
    x_here = lax.div(r, 4)
    x_plus, x_over, x_minus = (lax.rem(x_here + d, 4) for d in range(1, 4))
    z_row = 4 * x_here + 2 * (1 - lax.rem(q, 2))

    def local():
        return [
            pltpu.make_async_copy(wk.at[c], held.at[0, :, c], local_sem.at[0]),
            pltpu.make_async_copy(wv.at[c], held.at[1, :, c], local_sem.at[1]),
            pltpu.make_async_copy(wn.at[r], wng.at[r], local_sem.at[2]),
        ]

    for copy in local():
        copy.start()

    def target(i):
        return (2 * c + lax.rem(h + i, 2), q)

    barrier = pltpu.get_barrier_semaphore()
    peers = [(lax.rem(r + 4, N_ROW), c), (lax.rem(r + 12, N_ROW), c)] + ring_peers("col")
    peers += [(sibling, c), (z_row, c), (z_row + 1, c)]

    @pl.when(q != c)
    def _():
        for i in range(2):
            pl.semaphore_signal(barrier, inc=1, device_id=target(i), device_id_type=MESH)

    for device in peers:
        pl.semaphore_signal(barrier, inc=1, device_id=device, device_id_type=MESH)
    pl.semaphore_wait(barrier, len(peers) + 2 * (q != c).astype(jnp.int32))

    links = Links(send_sem, recv_sem, N_WEIGHT)
    links.go(w3, w3x, (sibling, c))

    col_place = ring_at("col")

    def mlp_ring(which, source):
        def slot(chip, half):
            return held.at[which, pl.ds(8 * half, 8), chip]

        def over(chip, half):
            return theirs.at[which, pl.ds(8 * half, 8), chip]

        def seen(chip, half):
            links.go(lambda: slot(chip, half), lambda: over(chip, half), (sibling, c))

        def begin():
            links.go(lambda: source.at[c], lambda: theirs.at[which, :, c], (sibling, c))
            yield from ring(
                links,
                "col",
                slot,
                own=lambda k: source.at[c, pl.ds(8 * k, 8)],
                seen=seen,
                at=col_place,
            )

        return begin()

    def weight_slot(chip, half):
        return wng.at[2 * chip + h, pl.ds(4 * half, 4)]

    far_links = Links(send_sem, recv_sem, N_ALL - 1 - 14 - RING)

    def weight_seen(chip, half):
        far_links.go(
            lambda: weight_slot(chip, half), lambda: weight_slot(chip, half), (sibling, c)
        )

    def weight_ring():
        far_links.go(lambda: wn.at[r], lambda: wng.at[r], (sibling, c))
        yield from ring(
            far_links,
            "row",
            weight_slot,
            own=lambda k: wn.at[r, pl.ds(4 * k, 4)],
            seen=weight_seen,
            heavy=False,
        )

    keys = mlp_ring(0, wk)
    values = mlp_ring(1, wv)
    weights = weight_ring()
    for steps in (weights, keys, values):
        next(steps)

    att_ring = PromptRing(send_sem, recv_sem, N_STATE, "row", att, attg)
    mid_ring = PromptRing(send_sem, recv_sem, N_STATE + PROMPTS * HOPS, "row", mid, midg)
    out_ring = PromptRing(send_sem, recv_sem, N_STATE + 2 * PROMPTS * HOPS, "col", None, nx)
    move_state = Copy(state, final, send_sem, recv_sem, N_TURN, target(0))

    def wide(ref, m):
        return jnp.concatenate([ref[j, aligned(m, LMAX), :] for j in range(N_ROW)], axis=1)

    def normed(ref, m, k):
        return norm(wide(ref, m).astype(F32), row_of(par, k), row_of(par, k + 1))

    def blends(m):
        z = normed(hx, m, 0)
        dz = step_back(z)
        for j in range(5):
            blend = (z + dz * shift[j : j + 1, :]).astype(BF16)
            if j < 3:
                weight = jnp.concatenate(
                    [wt[side, j].reshape(WIDTH, FEAT) for side in range(2)], axis=1
                )
                rkv[j] = dot(blend, weight)
            else:
                low[j - 3] = dot(blend, down[j - 3], ((1,), (1,)))

    def core(m):
        blends(m)
        one_prompt(m, lens, rkv, low, coef, up, att, state)
        att_ring.begin(m)
        for side in range(2):
            attg[2 * q + side, aligned(m, LMAX)] = att[side, aligned(m, LMAX)]

    def project(m):
        att_ring.last(m)
        tokens = aligned(m, LMAX)
        weight = jnp.concatenate([w[...].reshape(FEAT, WIDTH) for w in (w3, w3x)])
        total = dot(wide(attg, m), weight, ((1,), (1,)))
        for k, side in enumerate((h, 1 - h)):
            block = (
                hx[r - h + side, tokens, :].astype(F32) + total[:, k * FEAT : (k + 1) * FEAT]
            ).astype(BF16)
            mid[side, tokens, :] = block
            midg[r - h + side, tokens, :] = block
        mid_ring.begin(m)

    def x_move(m, k):
        tokens = aligned(m, LMAX)
        source, first, target_at, step = (
            (part, 4 * x_over, 0, 4),
            (part, 4 * x_over + 2, 2, 12),
            (part, 4 * x_plus + 2, 6, 4),
            (part, 4 * x_minus, 8, 12),
            (got, 12, 4, 4),
            (got, 14, 10, 12),
        )[k]
        return pltpu.make_async_remote_copy(
            src_ref=source.at[pl.ds(first, 2), tokens],
            dst_ref=got.at[pl.ds(target_at, 2), tokens],
            send_sem=send_sem.at[9 * m + k],
            recv_sem=recv_sem.at[9 * m + k],
            device_id=(lax.rem(r + step, N_ROW), c),
            device_id_type=MESH,
        )

    def plane_move(m, k):
        there = sibling if k == 0 else z_row + k - 1
        own_k = 0 if k == 0 else 1 + h
        return pltpu.make_async_remote_copy(
            src_ref=summed.at[there - 4 * x_here, aligned(m, LMAX)],
            dst_ref=fin.at[(0 if k == 0 else 2) + h, aligned(m, LMAX)],
            send_sem=send_sem.at[9 * m + 6 + k],
            recv_sem=recv_sem.at[9 * m + 6 + own_k],
            device_id=(there, c),
            device_id_type=MESH,
        )

    def channel(m):
        mid_ring.last(m)
        tokens = aligned(m, LMAX)
        z = normed(midg, m, 2)
        blend = (z + step_back(z) * shift[5:6, :]).astype(BF16)
        for side, weight in enumerate((held, theirs)):
            act = jnp.square(jnp.maximum(dot(blend, weight[0].reshape(WIDTH, MINE)), 0.0))
            act_scr[side] = act.astype(BF16)

        @pl.loop(0, N_CHIP)
        def _(n):
            total = None
            for side, weight in enumerate((held, theirs)):
                rows_n = weight[1, pl.ds(2 * n, 2)].reshape(SLICE, MINE)
                term = dot(act_scr[side], rows_n, ((1,), (1,)))
                total = term if total is None else total + term
            for side in range(2):
                added = jnp.where(n == q, mid[side, tokens, :].astype(F32), 0.0)
                part[2 * n + side, tokens, :] = (
                    total[:, side * FEAT : (side + 1) * FEAT] + added
                ).astype(BF16)

        for k in range(4):
            x_move(m, k).start()

    def relay(m):
        tokens = aligned(m, LMAX)
        for k, other in enumerate((x_plus, x_minus)):
            x_move(m, k).wait_recv()
            for j in range(2):
                added = part[4 * other + 2 * k + j, tokens, :].astype(F32)
                got[12 + 2 * k + j, tokens, :] = (
                    got[2 * k + j, tokens, :].astype(F32) + added
                ).astype(BF16)
            x_move(m, 4 + k).start()

    def plane_sum(m):
        tokens = aligned(m, LMAX)
        for k in range(2, 6):
            x_move(m, k).wait_recv()
        for k, places in enumerate(((4, 8), (5, 9), (10, 6), (11, 7))):
            total = part[4 * x_here + k, tokens, :].astype(F32)
            for j in places:
                total += got[j, tokens, :].astype(F32)
            summed[k, tokens, :] = total.astype(BF16)
        for k in (1, 2, 0):
            plane_move(m, k).start()
        fin[h, tokens, :] = summed[r - 4 * x_here, tokens, :]

    def source_rows(m, i):
        return pl.ds(pl.multiple_of(lax.rem(h + i, 2) * MINE + m * LMAX, LMAX), LMAX)

    def turn(m, i):
        return pltpu.make_async_remote_copy(
            src_ref=out.at[source_rows(m, i)],
            dst_ref=nx.at[2 * q + h, aligned(m, LMAX)],
            send_sem=send_sem.at[N_SUM + 2 * m + i],
            recv_sem=recv_sem.at[N_SUM + 2 * m + h],
            device_id=target(i),
            device_id_type=MESH,
        )

    def add_up(m):
        tokens = aligned(m, LMAX)
        for k in range(3):
            block = fin.at[0, tokens]
            pltpu.make_async_copy(block, block, recv_sem.at[9 * m + 6 + k]).wait()
        for side in range(2):
            total = fin[side, tokens, :].astype(F32) + fin[2 + side, tokens, :].astype(F32)
            rows_m = pl.ds(pl.multiple_of(side * MINE + m * LMAX, LMAX), LMAX)
            out[rows_m, :] = total.astype(BF16)

        @pl.when(q == c)
        def _():
            keep(
                out.at[source_rows(m, 0)],
                nx.at[r, aligned(m, LMAX)],
                recv_sem.at[N_SUM + 2 * m + h],
            )

        @pl.when(q != c)
        def _():
            turn(m, 0).start()

        turn(m, 1).start()

    def spread(m):
        for k in range(2):
            block = nx.at[2 * c + k, aligned(m, LMAX)]
            pltpu.make_async_copy(block, block, recv_sem.at[N_SUM + 2 * m + k]).wait()
        out_ring.begin(m)

    def project_next(m):
        out_ring.last(m)
        z = normed(nx, m, 4)
        dz = step_back(z)
        for j in range(3):
            blend = (z + dz * shift[6 + j : 7 + j, :]).astype(BF16)
            next_rkv[j, aligned(m, LMAX), :] = dot(
                blend, wng[:, :, j].reshape(WIDTH, SLICE)
            ).astype(BF16)

    stages = (
        core,
        att_ring.forward,
        att_ring.close,
        project,
        mid_ring.forward,
        mid_ring.close,
        channel,
        relay,
        plane_sum,
        add_up,
        spread,
        out_ring.forward,
        out_ring.close,
        project_next,
    )
    end = object()

    def wait_mlp():
        for copy in local():
            copy.wait()
        for copy in links.open:
            copy.wait_recv()
        links.open = []

    def send_state():
        @pl.when(q == c)
        def _():
            keep(state, final, recv_sem.at[N_TURN])

        @pl.when(q != c)
        def _():
            move_state.start()

    def wait_far():
        for copy in far_links.open:
            copy.wait_recv()
        far_links.open = []

    beside = {
        0: [keys, values],
        1: [keys, values, weights, weights],
        2: [lambda: links.arrive(links.copies[0])],
        3: [keys, values, send_state],
        4: [weights],
        5: [keys, values, wait_mlp],
        6: [weights],
        12: [wait_far],
    }

    @pl.loop(0, PROMPTS + len(stages) - 1)
    def _(t):
        for lag, stage in enumerate(stages):

            @pl.when((t >= lag) & (t < PROMPTS + lag))
            def _():
                stage(t - lag)

        for at, works in beside.items():

            @pl.when(t == at)
            def _():
                for work in works:
                    if callable(work):
                        work()
                    else:
                        next(work, end)

    @pl.loop(0, PROMPTS)
    def _(m):
        for k in range(6):
            x_move(m, k).wait_send()
        for k in range(3):
            plane_move(m, k).wait_send()
        for prompt_ring in (att_ring, mid_ring, out_ring):
            prompt_ring.sent(m)

        @pl.when(q != c)
        def _():
            turn(m, 0).wait_send()

        turn(m, 1).wait_send()

    pltpu.make_async_copy(state, final, recv_sem.at[N_TURN]).wait()

    @pl.when(q != c)
    def _():
        move_state.wait_send()

    for copy in links.copies + far_links.copies:
        copy.wait_send()


def per_device(
    hidden,
    lengths,
    square_matrix_shards,
    channel_mix_shards,
    lowrank_down,
    lowrank_up,
    token_shift_weights,
    attention_coefficients,
    norm_parameters,
):
    hx, wt, w3, wk, wv, wn, parg = exchange(
        start_kernel,
        [
            ((N_ROW, MINE, FEAT), BF16),
            ((2, 3, N_ROW, N_COL, 16, FEAT), BF16),
            ((N_COL, 16, WIDTH), BF16),
            ((N_COL, N_ROW, 16, MINE), BF16),
            ((N_COL, N_ROW, 16, MINE), BF16),
            ((N_ROW, N_COL, 3, 16, SLICE), BF16),
            ((N_ROW, 6, FEAT), F32),
        ],
        15 + 1 + 3 * RING + 1 + 14 + 15 + 15 + 7 + 15,
        9,
        1,
        square_matrix_shards,
        channel_mix_shards,
        norm_parameters,
        hidden,
        scratch=[
            pltpu.VMEM(square_matrix_shards.shape, F32),
            pltpu.VMEM(channel_mix_shards.shape, F32),
            pltpu.VMEM(square_matrix_shards.shape, BF16),
            pltpu.VMEM(channel_mix_shards.shape, BF16),
        ],
    )
    lowrank = lowrank_down.shape[2]
    out_hidden, next_rkv, final = exchange(
        body_kernel,
        [
            ((2 * MINE, FEAT), BF16),
            ((3, MINE, SLICE), BF16),
            ((PROMPTS, 2, HEAD, FEAT), BF16),
        ],
        N_ALL,
        3,
        2,
        lengths,
        hx,
        parg,
        token_shift_weights,
        wt,
        lowrank_down.transpose(0, 2, 1),
        attention_coefficients,
        lowrank_up,
        w3,
        wk,
        wv,
        wn,
        scratch=[
            pltpu.VMEM((3, LMAX, SLICE), F32),
            pltpu.VMEM((2, LMAX, lowrank), F32),
            pltpu.VMEM((PROMPTS, 2, HEAD, FEAT), BF16),
            pltpu.VMEM((2, MINE, FEAT), BF16),
            pltpu.VMEM((N_ROW, MINE, FEAT), BF16),
            pltpu.VMEM((N_COL, 16, WIDTH), BF16),
            pltpu.VMEM((2, MINE, FEAT), BF16),
            pltpu.VMEM((N_ROW, MINE, FEAT), BF16),
            pltpu.VMEM((2, N_ROW, N_COL, 16, MINE), BF16),
            pltpu.VMEM((2, N_ROW, N_COL, 16, MINE), BF16),
            pltpu.VMEM((2, LMAX, MINE), BF16),
            pltpu.VMEM((N_ROW, MINE, FEAT), BF16),
            pltpu.VMEM((N_ROW, MINE, FEAT), BF16),
            pltpu.VMEM((4, MINE, FEAT), BF16),
            pltpu.VMEM((4, MINE, FEAT), BF16),
            pltpu.VMEM((N_ROW, MINE, FEAT), BF16),
            pltpu.VMEM((N_ROW, N_COL, 3, 16, SLICE), BF16),
        ],
        in_specs=[pl.BlockSpec(memory_space=pltpu.SMEM)] + [VMEM] * 8 + [ANY] * 3,
        out_specs=[VMEM, VMEM, ANY],
    )
    final = final.reshape(4, 2, HEAD, 2, HEAD).transpose(0, 1, 3, 2, 4).astype(F32)
    final_state = final.reshape(4, 4, HEAD * HEAD)
    return (out_hidden, next_rkv, final_state)


def solution(mesh):
    return jax.shard_map(
        per_device,
        mesh=mesh,
        in_specs=(
            P("col", "row"),
            P(),
            P(None, ("row", "col"), None),
            P(None, ("row", "col"), None),
            P(),
            P(),
            P(),
            P(),
            P(None, "row"),
        ),
        out_specs=(P("col", "row"), P(None, "row", "col"), P("row", "col", None)),
        check_vma=False,
    )
```
